32 devices in a mesh: seq: 8 (over z, y), fsdp: 4 (over x, core).
Axes of the slice: x: 2, y: 2, z: 4, core: 2. Of those that a mesh axis runs over, the one named last changes fastest.
Arguments:
- tokens: bfloat16 [4, 2560, 1024], P('fsdp', 'seq'), may hold values from -6 to 6
- cotangent: bfloat16 [4, 2560, 1024], P('fsdp', 'seq'), may hold values from -6 to 6
- query_weight: bfloat16 [1024, 1024], P('fsdp'), may hold values from -0.25 to 0.25
- key_weight: bfloat16 [1024, 1024], P('fsdp'), may hold values from -0.1875 to 0.1875
- value_weight: bfloat16 [1024, 1024], P('fsdp'), may hold values from -0.1875 to 0.1875
- output_weight: bfloat16 [1024, 1024], P('fsdp'), may hold values from -3 to 3
- gate_weight: bfloat16 [1024, 2816], P('fsdp'), may hold values from -0.1875 to 0.1875
- up_weight: bfloat16 [1024, 2816], P('fsdp'), may hold values from -0.1875 to 0.1875
- down_weight: bfloat16 [2816, 1024], P('fsdp'), may hold values from -0.109375 to 0.109375
- attention_gain: bfloat16 [1024], P('fsdp'), may hold values from 0.099609375 to 1.8984375
- feedforward_gain: bfloat16 [1024], P('fsdp'), may hold values from 0.099609375 to 1.8984375
- lengths: int32 [4, 2], P('fsdp'), may hold values from 0 to 2560, as said below
- token_order: int32 [4, 2560], P('fsdp'), may hold values from 0 to 2559, each once within a row
- real_token: int32 [4, 2560], P('fsdp'), may hold values 0 or 1
Outputs:
- layer_out: bfloat16 [4, 2560, 1024], P('fsdp', 'seq')
- input_grad: float32 [4, 2560, 1024], P('fsdp', 'seq')
- query_grad: float32 [1024, 1024], P('fsdp')
- key_grad: float32 [1024, 1024], P('fsdp')
- value_grad: float32 [1024, 1024], P('fsdp')
- output_grad: float32 [1024, 1024], P('fsdp')
- gate_grad: float32 [1024, 2816], P('fsdp')
- up_grad: float32 [1024, 2816], P('fsdp')
- down_grad: float32 [2816, 1024], P('fsdp')
- attention_gain_grad: float32 [1024], P('fsdp')
- feedforward_gain_grad: float32 [1024], P('fsdp')
The draws below stay inside these ranges and needn't reach their ends.
Inputs may be any that keep to these rules, and one draw needn't show every extreme that they name: Each row lists its sequences' lengths first, each 1024 or more, then zeros; a row's entries sum to 2560; in every draw some row is one sequence of 2560 tokens. `token_order`: each row is a permutation of the 2560 given positions of its group. `real_token`: 1 marks a real token, 0 padding.
All inputs are finite; a program needn't handle non-finite values. No bound on the sum of `real_token` on one device may be relied on, other than what follows from the above.
Results may differ from the reference program's by a relative error of at most 0.02.
Values may be sent and summed in bfloat16 or wider, within the bound.
No kernel may reach another device: no remote copies, remote signals or barrier semaphores. Data moves between devices by JAX's collectives and lax.ppermute only.
A program may use at most 192 MiB of HBM per device.

```python
import jax
import jax.numpy as jnp
from jax import lax

D = 1024
HEADS = 16
HD = 64
FF = 2816
MINLEN = 1024
GROUPS = 4
GROUP = 2560
SEGS = 2
TOKENS = 10240


def draw_lengths(key, part):
    keys_split = jax.random.split(jax.random.fold_in(key, 11), 3)
    counts = jax.random.randint(keys_split[0], (GROUPS,), 1, SEGS + 1)
    single = jax.random.randint(keys_split[1], (), 0, GROUPS)
    counts = jnp.where(jnp.arange(GROUPS) == single, 1, counts)
    shares_raw = jax.random.randint(keys_split[2], (GROUPS, SEGS), 1, 100)
    slot_ids = jnp.arange(SEGS)[None, :]
    live = slot_ids < counts[:, None]
    shares_raw = jnp.where(live, shares_raw, 0)
    extra = GROUP - counts * MINLEN
    shares = extra[:, None] * shares_raw // jnp.sum(shares_raw, axis=1, keepdims=True)
    remainder = extra - jnp.sum(shares, axis=1)
    last_slot = slot_ids == counts[:, None] - 1
    result = jnp.where(live, MINLEN + shares, 0) + jnp.where(last_slot, remainder[:, None], 0)
    return result.astype(jnp.int32)


def touch_ends(array, rng, smallest, high):
    spot = [jax.random.randint(jax.random.fold_in(rng, axis), (), 0, length) for axis, length in enumerate(array.shape)]
    main_axis = array.shape.index(max(array.shape))
    beside = spot[:main_axis] + [(spot[main_axis] + 1) % array.shape[main_axis]] + spot[main_axis + 1:]
    return array.at[tuple(spot)].set(smallest).at[tuple(beside)].set(high)


def strengthened(values, stream_key, source, target, parts, factor):
    owner, partner = [(jnp.arange(values.shape[axis_at]) // (values.shape[axis_at] // parts)).reshape([-1 if axis == axis_at else 1 for axis in range(values.ndim)]) for axis_at in (source, target)]
    chosen = jax.random.permutation(stream_key, parts)[partner]
    strong = (owner == chosen) | (owner == (partner + parts // 2) % parts)
    return jnp.where(strong, factor * values, values)


def levels(stream_key, dims, shards, least, largest):
    loudness = 1.0
    for position, parts in shards:
        heights = jax.random.uniform(jax.random.fold_in(jax.random.fold_in(stream_key, 6), position), (parts,), jnp.float32, least / len(shards), largest / len(shards))
        loudness = loudness * jnp.repeat(jnp.exp(heights), dims[position] // parts).reshape((-1,) + (1,) * (len(dims) - 1 - position))
    return loudness


def bell_draw(stream_key, shape, width, reach, cuts=(), held_as=jnp.bfloat16):
    loudness = levels(stream_key, shape, cuts, -0.22, 0.18) if cuts else 1.0
    array = jax.random.normal(stream_key, shape, jnp.float32) * width * loudness
    return jnp.minimum(jnp.maximum(array, -reach), reach).astype(held_as)


def noise_with(own_key, extent, width, limit, cuts, heavy, kind=jnp.bfloat16):
    entries = width * jax.random.normal(own_key, extent, jnp.float32)
    if cuts:
        entries = entries * levels(own_key, extent, cuts, -0.22, 0.18)
    return jnp.clip(strengthened(entries, jax.random.fold_in(own_key, 3), *heavy), -limit, limit).astype(kind)


def setup_inputs(seed: int = 0) -> dict:
    seeds = jax.random.split(jax.random.key(seed), 15)
    return {
        "tokens": noise_with(seeds[0], (GROUPS, GROUP, D), 1.0, 6.0, ((0, 4), (1, 8)), (1, 2, 8, 2.0)),
        "cotangent": bell_draw(seeds[1], (GROUPS, GROUP, D), 1.0, 6.0, ((0, 4), (1, 8))),
        "query_weight": bell_draw(seeds[2], (D, D), (D // 2) ** -0.5, 0.25, ((0, 4),)),
        "key_weight": bell_draw(seeds[3], (D, D), D ** -0.5, 0.1875, ((0, 4),)),
        "value_weight": bell_draw(seeds[4], (D, D), D ** -0.5, 0.1875, ((0, 4),)),
        "output_weight": bell_draw(seeds[5], (D, D), (max(D // 256, 1)) ** -0.5, 3.0, ((0, 4),)),
        "gate_weight": bell_draw(seeds[6], (D, FF), D ** -0.5, 0.1875, ((0, 4),)),
        "up_weight": bell_draw(seeds[7], (D, FF), D ** -0.5, 0.1875, ((0, 4),)),
        "down_weight": bell_draw(seeds[8], (FF, D), FF ** -0.5, 0.109375, ((0, 4),)),
        "attention_gain": jnp.clip(1.0 + 0.18 * jax.random.normal(seeds[9], (D,), jnp.float32), 0.099609375, 1.8984375).astype(jnp.bfloat16),
        "feedforward_gain": jnp.clip(1.0 + 0.18 * jax.random.normal(seeds[10], (D,), jnp.float32), 0.099609375, 1.8984375).astype(jnp.bfloat16),
        "lengths": draw_lengths(jax.random.fold_in(seeds[14], 71), 0),
        "token_order": jax.vmap(lambda own: jax.random.permutation(own, GROUP))(jax.random.split(seeds[12], GROUPS)).reshape((GROUPS, GROUP)).astype(jnp.int32),
        "real_token": touch_ends((jax.random.randint(seeds[13], (GROUPS, GROUP), 0, 8) < 7).astype(jnp.int32), jax.random.fold_in(seeds[13], 1), 0, 1),
    }


EPSILON = 1e-06
NEGATIVE_FILL = -1e+30

@jax.custom_vjp
def low(v):
    return lax.optimization_barrier(v.astype(jnp.bfloat16)).astype(jnp.float32)

@jax.custom_vjp
def low_back(v):
    return v

def low_keep(v):
    return (low(v), None)

def low_pass(kept, grad):
    return (grad,)

def back_keep(v):
    return (v, None)

def back_low(kept, grad):
    return (low(grad),)
low.defvjp(low_keep, low_pass)
low_back.defvjp(back_keep, back_low)

def highest(left_side, right_side):
    return jnp.dot(left_side, right_side, precision=lax.Precision.HIGHEST, preferred_element_type=jnp.float32)

def normed(values):
    return values * lax.rsqrt(lax.optimization_barrier(jnp.mean(values * values, axis=-1, keepdims=True)) + EPSILON)

def attend_group(group_args):
    query_rows, key_rows, value_rows, lengths_row, order_row, real_row = group_args
    block_size = min(512, GROUP)
    score_scale = float(HD) ** (-0.5)
    positions = jnp.arange(GROUP, dtype=jnp.int32)
    ends_at = jnp.cumsum(lengths_row)
    segment_ids = lax.optimization_barrier(jnp.sum((positions[:, None] >= ends_at[None, :]).astype(jnp.int32), axis=1))

    def to_heads(given_rows):
        return given_rows[order_row].reshape(GROUP, HEADS, HD).transpose(1, 0, 2)
    packed_q = to_heads(query_rows)
    packed_k = to_heads(key_rows)
    packed_v = to_heads(value_rows)

    def one_block(block_index):
        first_row = block_index * block_size
        query_block = lax.dynamic_slice_in_dim(packed_q, first_row, block_size, axis=1)
        scores = low_back(jnp.einsum('hqd,hkd->hqk', query_block, packed_k, precision=lax.Precision.HIGHEST) * score_scale)
        query_segment = lax.dynamic_slice_in_dim(segment_ids, first_row, block_size)
        query_place = first_row + jnp.arange(block_size, dtype=jnp.int32)
        allowed = (query_segment[:, None] == segment_ids[None, :]) & ((real_row[None, :] > 0) | (query_place[:, None] == positions[None, :]))
        masked = jnp.where(allowed[None], scores, NEGATIVE_FILL)
        top_score = lax.optimization_barrier(jnp.max(masked, axis=-1, keepdims=True))
        log_total = top_score + jnp.log(lax.optimization_barrier(jnp.sum(jnp.exp(masked - top_score), axis=-1, keepdims=True)))
        probabilities = low(jnp.exp(masked - log_total))
        return jnp.einsum('hqk,hkd->hqd', probabilities, packed_v, precision=lax.Precision.HIGHEST)
    blocks = lax.map(jax.checkpoint(one_block), jnp.arange(GROUP // block_size, dtype=jnp.int32))
    packed_out = blocks.transpose(1, 0, 2, 3).reshape(HEADS, GROUP, HD)
    rows_first = packed_out.transpose(1, 0, 2).reshape(GROUP, HEADS * HD)
    return jnp.zeros_like(rows_first).at[order_row].set(rows_first)

def reference(tokens, cotangent, query_weight, key_weight, value_weight, output_weight, gate_weight, up_weight, down_weight, attention_gain, feedforward_gain, lengths, token_order, real_token):

    def forward(inputs, query_w, key_w, value_w, output_w, gate_w, up_w, down_w, first_gain, second_gain):
        flat_rows = inputs.reshape(TOKENS, D)
        first_hidden = low(normed(flat_rows) * first_gain)
        queries = low(low_back(highest(first_hidden, query_w)))
        key_rows = low(low_back(highest(first_hidden, key_w)))
        value_rows = low(low_back(highest(first_hidden, value_w)))
        attended = lax.map(attend_group, (queries.reshape(GROUPS, GROUP, D), key_rows.reshape(GROUPS, GROUP, D), value_rows.reshape(GROUPS, GROUP, D), lengths, token_order, real_token))
        attended = low(low_back(attended.reshape(TOKENS, D)))
        middle = flat_rows + low_back(highest(attended, output_w))
        second_hidden = low(normed(middle) * second_gain)
        gate_values = low_back(highest(second_hidden, gate_w))
        up_values = low_back(highest(second_hidden, up_w))
        activated = low(jax.nn.gelu(gate_values, approximate=True) * up_values)
        result = middle + low_back(highest(activated, down_w))
        return result.reshape(GROUPS, GROUP, D)
    floats = [argument_value.astype(jnp.float32) for argument_value in (tokens, query_weight, key_weight, value_weight, output_weight, gate_weight, up_weight, down_weight, attention_gain, feedforward_gain)]
    result, pullback = jax.vjp(forward, *floats)
    grads = pullback(cotangent.astype(jnp.float32))
    return (result.astype(jnp.bfloat16), grads[0], grads[1], grads[2], grads[3], grads[4], grads[5], grads[6], grads[7], grads[8], grads[9])
```

```python
import functools

import jax
import jax.numpy as jnp
from jax import lax
from jax.experimental import pallas as pl
from jax.experimental.pallas import tpu as pltpu
from jax.sharding import PartitionSpec as P

HD = 64
LANES = 128
EPSILON = 1e-06
BLOCKED = -(2.0**100)
ROOT_2_PI = 0.7978845608028654
CUBIC = 0.044715
VMEM_LIMIT = 60 * 1024 * 1024

bf16 = jnp.bfloat16
f32 = jnp.float32


def mm(a, b):
    return jnp.dot(a, b, preferred_element_type=f32)


def mm_nt(a, b):
    return lax.dot_general(a, b, (((1,), (1,)), ((), ())), preferred_element_type=f32)


def mm_tn(a, b):
    return lax.dot_general(a, b, (((0,), (0,)), ((), ())), preferred_element_type=f32)


def params(**extra):
    return pltpu.CompilerParams(vmem_limit_bytes=VMEM_LIMIT, **extra)


def cost(flops, moved, transcendentals=0):
    return pl.CostEstimate(
        flops=int(flops), bytes_accessed=int(moved), transcendentals=int(transcendentals)
    )


def vmem():
    return pl.BlockSpec(memory_space=pltpu.VMEM)


def anywhere():
    return pl.BlockSpec(memory_space=pl.ANY)


def smem():
    return pl.BlockSpec(memory_space=pltpu.SMEM)


def lane_ids(rows):
    return lax.broadcasted_iota(jnp.int32, (rows, LANES), 1)


def split3(column):
    high = column.astype(bf16)
    rest = column - high.astype(f32)
    middle = rest.astype(bf16)
    low = (rest - middle.astype(f32)).astype(bf16)
    return (high.astype(f32), middle.astype(f32), low.astype(f32))


def project_kernel(heads, fresh, *refs):
    x_ref, gain_ref, w_ref, qt_ref, kt_ref = refs[:5]
    qa_ref, ka_ref, va_ref, h1_ref = refs[5:] if fresh else refs[9:]
    x = x_ref[...].astype(f32)
    scaling = lax.rsqrt(jnp.mean(x * x, axis=-1, keepdims=True) + EPSILON)
    h1 = (x * scaling * gain_ref[...].astype(f32)).astype(bf16)
    h1_ref[...] = h1
    qkv = mm(h1, w_ref[...])
    rows = x.shape[0]
    lane = lane_ids(rows)
    q = qkv[:, :LANES].astype(bf16) * jnp.asarray(HD**-0.5, bf16)
    k = qkv[:, LANES : 2 * LANES].astype(bf16)
    v = qkv[:, 2 * LANES :].astype(bf16)
    ones = jnp.where(lane % HD < 3, 1.0, 0.0).astype(bf16)
    for head in range(heads):
        own = lane // HD == head
        qa_ref[head] = jnp.where(own, q, qt_ref[...])
        ka_ref[head] = jnp.where(own, k, kt_ref[...])
        va_ref[head] = jnp.where(own, v, ones)


def project(slot, slots, heads, x, gain, w, q_table, k_table, previous):
    rows, width = x.shape
    total = rows * slots
    row_spec = pl.BlockSpec((rows, LANES), lambda i: (slot, 0))
    head_spec = pl.BlockSpec((heads, rows, LANES), lambda i: (0, slot, 0))
    shapes = [jax.ShapeDtypeStruct((heads, total, LANES), bf16)] * 3 + [
        jax.ShapeDtypeStruct((total, width), bf16)
    ]
    fresh = previous is None
    extra = () if fresh else tuple(previous)
    return pl.pallas_call(
        functools.partial(project_kernel, heads, fresh),
        grid=(1,),
        in_specs=[
            pl.BlockSpec((rows, width), lambda i: (0, 0)),
            pl.BlockSpec((1, width), lambda i: (0, 0)),
            pl.BlockSpec(w.shape, lambda i: (0, 0)),
            row_spec,
            row_spec,
        ]
        + [anywhere()] * len(extra),
        out_specs=[head_spec] * 3 + [pl.BlockSpec((rows, width), lambda i: (slot, 0))],
        out_shape=shapes,
        input_output_aliases={} if fresh else {5 + i: i for i in range(4)},
        compiler_params=params(),
        cost_estimate=cost(2 * rows * width * 3 * LANES, 4 * rows * width + 2 * w.size),
        name="project",
    )(x, gain, w, q_table, k_table, *extra)


def forward_kernel(heads, slots, rows, q_ref, k_ref, v_ref, *outs):
    lane = lane_ids(rows)
    att_refs, sum_ref, qb_ref = outs[:slots], outs[slots], outs[slots + 1]
    for index in range(slots):
        span = slice(index * rows, (index + 1) * rows)
        merged = None
        for head in range(heads):
            q = q_ref[head, span, :]
            own = lane // HD == head
            other = HD if head == 0 else 0
            scores = mm_nt(q, k_ref[head])
            key = k_ref[head, pl.ds(pl.multiple_of(outs[-1][index] * rows, rows), rows), :]
            value = v_ref[head, pl.ds(pl.multiple_of(outs[-1][index] * rows, rows), rows), :]
            q_wide = q.astype(f32)
            padded = q_wide[:, other + HD - 1 : other + HD] > 0.5
            own_score = jnp.sum(
                jnp.where(own, q_wide * key.astype(f32), 0.0), axis=-1, keepdims=True
            )
            top = jnp.max(scores, axis=-1, keepdims=True)
            top = jnp.where(padded, jnp.maximum(top, own_score), top)
            weights = jnp.exp(scores - top).astype(bf16)
            mixed = mm(weights, v_ref[head])
            own_weight = jnp.where(padded, jnp.exp(own_score - top), 0.0).astype(bf16).astype(f32)
            mixed = mixed + own_weight * value.astype(f32)
            total = mixed[:, other : other + 1]
            log_total = top + jnp.log(total)
            mixed = mixed * (1.0 / total)
            merged = mixed if merged is None else jnp.where(own, mixed, merged)
            parts = split3(-log_total)
            base = other + HD - 4
            filled = q_wide
            for place, part in enumerate(parts):
                filled = jnp.where(lane == base + place, part, filled)
            qb_ref[head, span, :] = filled.astype(bf16)
        att_refs[index][...] = merged.astype(bf16)
        sum_ref[span, :] = merged


def forward_body(heads, slots, rows, where_ref, *refs):
    forward_kernel(heads, slots, rows, *refs, where_ref)


def attend(qa, ka, va, group, slots):
    heads, total, _ = qa.shape
    rows = total // slots
    count = len(group)
    first = group[0]
    assert list(group) == list(range(first, first + count)) and first % count == 0
    span = rows * count
    where = jnp.arange(first, first + count, dtype=jnp.int32)
    return pl.pallas_call(
        functools.partial(forward_body, heads, count, rows),
        grid=(1,),
        in_specs=[
            smem(),
            pl.BlockSpec((heads, span, LANES), lambda i: (0, first // count, 0)),
            pl.BlockSpec(ka.shape, lambda i: (0, 0, 0)),
            pl.BlockSpec(va.shape, lambda i: (0, 0, 0)),
        ],
        out_specs=[pl.BlockSpec((rows, LANES), lambda i: (0, 0))] * count
        + [
            pl.BlockSpec((span, LANES), lambda i: (0, 0)),
            pl.BlockSpec((heads, span, LANES), lambda i: (0, 0, 0)),
        ],
        out_shape=[jax.ShapeDtypeStruct((rows, LANES), bf16)] * count
        + [
            jax.ShapeDtypeStruct((span, LANES), f32),
            jax.ShapeDtypeStruct((heads, span, LANES), bf16),
        ],
        compiler_params=params(),
        cost_estimate=cost(
            16 * heads * span * total * LANES, 4 * heads * total * LANES, heads * span * total
        ),
        name="attend",
    )(where, qa, ka, va)


def backward_kernel(heads, parts, rows, count, tile, first, has_dq, *refs):
    total = parts * rows
    dq_in, refs = (refs[0], refs[1:]) if has_dq else (None, refs)
    qb_refs = refs[:1]
    k_ref, v_ref, sum_ref = refs[1:4]
    grad_refs = refs[4 : 4 + parts]
    outs = refs[4 + parts :]
    dk_refs, dv_refs = outs[:count], outs[count : 2 * count]
    dq_ref = outs[2 * count]
    gb, dq_acc, dk_acc, dv_acc = outs[2 * count + 1 :]
    qb = qb_refs[0]
    lane = lane_ids(rows)
    for part in range(parts):
        span = slice(part * rows, (part + 1) * rows)
        grad = grad_refs[part][...].astype(f32)
        product = grad * sum_ref[span, :]
        for head in range(heads):
            other = HD if head == 0 else 0
            own = lane // HD == head
            delta = jnp.sum(jnp.where(own, product, 0.0), axis=-1, keepdims=True)
            filled = jnp.where(own, grad, 0.0)
            for place, piece in enumerate(split3(-delta)):
                filled = jnp.where(lane == other + place, piece, filled)
            gb[head, span, :] = filled.astype(bf16)
    if has_dq:
        dq_acc[...] = dq_in[...]
    else:
        dq_acc[...] = jnp.zeros_like(dq_acc)
    for index in range(count):
        begin = (first + index) * rows
        dk_acc[...] = jnp.zeros_like(dk_acc)
        dv_acc[...] = jnp.zeros_like(dv_acc)

        def step(number, carry):
            at = pl.ds(pl.multiple_of(number * tile, tile), tile)
            for head in range(heads):
                key = k_ref[head, begin : begin + rows, :]
                value = v_ref[head, begin : begin + rows, :]
                q = qb[head, at, :]
                g = gb[head, at, :]
                weights = jnp.exp(mm_nt(key, q))
                inner = mm_nt(value, g)
                score_grad = (weights * inner).astype(bf16)
                dv_acc[head] += mm(weights.astype(bf16), g)
                dk_acc[head] += mm(score_grad, q)
                dq_acc[head, at, :] += mm_tn(score_grad, key)
            return carry

        lax.fori_loop(0, total // tile, step, 0)
        span = slice(begin, begin + rows)
        dk_all, dv_all = None, None
        for head in range(heads):
            other = HD if head == 0 else 0
            own = lane // HD == head
            counted = own | ((lane >= other + HD - 4) & (lane < other + HD - 1))
            q = qb[head, span, :].astype(f32)
            k = k_ref[head, span, :].astype(f32)
            v = v_ref[head, span, :].astype(f32)
            g = gb[head, span, :].astype(f32)
            padded = q[:, other + HD - 1 : other + HD] > 0.5
            score = jnp.sum(jnp.where(counted, q * k, 0.0), axis=-1, keepdims=True)
            weight = jnp.where(padded, jnp.exp(score), 0.0)
            inner = jnp.sum(v * g, axis=-1, keepdims=True)
            score_grad = (weight * inner).astype(bf16).astype(f32)
            weight = weight.astype(bf16).astype(f32)
            dk = dk_acc[head] + score_grad * q
            dv = dv_acc[head] + weight * g
            dq_acc[head, span, :] += score_grad * k
            dk_all = dk if head == 0 else jnp.where(own, dk, dk_all)
            dv_all = dv if head == 0 else jnp.where(own, dv, dv_all)
        dk_refs[index][...] = dk_all.astype(bf16)
        dv_refs[index][...] = dv_all.astype(bf16)
    dq_ref[...] = dq_acc[...]


def attend_back(qb, ka, va, sums, grads, group, slots, dq_before):
    heads, total, _ = ka.shape
    rows = total // slots
    parts = len(grads)
    count = len(group)
    tile = 512
    part_rows = total // parts
    dq_shape = jax.ShapeDtypeStruct((heads, total, LANES), f32)
    inputs = ([] if dq_before is None else [dq_before]) + [qb, ka, va, sums] + list(grads)
    assert part_rows == rows
    out = pl.pallas_call(
        functools.partial(
            backward_kernel, heads, parts, rows, count, tile, group[0], dq_before is not None
        ),
        in_specs=[vmem()] * len(inputs),
        out_specs=[vmem()] * (2 * count + 1),
        out_shape=[jax.ShapeDtypeStruct((rows, LANES), bf16)] * (2 * count) + [dq_shape],
        scratch_shapes=[
            pltpu.VMEM((heads, total, LANES), bf16),
            pltpu.VMEM((heads, total, LANES), f32),
            pltpu.VMEM((heads, rows, LANES), f32),
            pltpu.VMEM((heads, rows, LANES), f32),
        ],
        compiler_params=params(),
        cost_estimate=cost(
            40 * heads * count * rows * total * LANES,
            12 * heads * total * LANES,
            heads * count * rows * total,
        ),
        name="attend_back",
    )(*inputs)
    return (out[:count], out[count : 2 * count], out[2 * count])


def middle_kernel(blocks, pieces, step_width, *refs):
    att_rows, w_rows = refs[0], refs[1]
    refs = refs[2:]
    att_refs = refs[:blocks]
    x_ref, c_ref, gain_ref = refs[blocks : blocks + 3]
    refs = refs[blocks + 3 :]
    wo_refs, wg_refs, wu_refs, wd_refs = [refs[i * pieces : (i + 1) * pieces] for i in range(4)]
    refs = refs[4 * pieces :]
    out_ref, dmid_ref = refs[:2]
    da_refs = refs[2 : 2 + blocks]
    refs = refs[2 + blocks :]
    og_refs, gg_refs, ug_refs, dg_refs = [refs[i * pieces : (i + 1) * pieces] for i in range(4)]
    refs = refs[4 * pieces :]
    wo, wg, wu, wd, og, gg, ug, dg, att, h2_ref, mid_ref, acc_out, acc_back = refs[:13]
    in_sems, out_sems = refs[13:]

    loads = []
    for number, (sources, target) in enumerate(((wo_refs, wo), (wg_refs, wg), (wu_refs, wu), (wd_refs, wd))):
        step_rows = target.shape[0] // pieces
        for piece in range(pieces):
            at = pl.ds(pl.multiple_of(w_rows[piece] * step_rows, step_rows), step_rows)
            copy = pltpu.make_async_copy(sources[piece], target.at[at, :], in_sems.at[number, piece])
            copy.start()
            loads.append(copy)

    width = x_ref.shape[1]
    block_width = width // blocks
    for block in range(blocks):
        at = pl.ds(pl.multiple_of(att_rows[block] * block_width, block_width), block_width)
        att[:, at] = att_refs[block][...]
    for copy in loads[:pieces]:
        copy.wait()
    gain = gain_ref[...].astype(f32)
    middle = x_ref[...].astype(f32) + mm(att[...], wo[...])
    scaling = lax.rsqrt(jnp.mean(middle * middle, axis=-1, keepdims=True) + EPSILON)
    h2_ref[...] = (middle * scaling * gain).astype(bf16)
    mid_ref[...] = middle
    acc_out[...] = jnp.zeros_like(acc_out)
    acc_back[...] = jnp.zeros_like(acc_back)
    for copy in loads[pieces:]:
        copy.wait()

    def column_step(number, carry):
        at = pl.ds(pl.multiple_of(number * step_width, step_width), step_width)
        h2 = h2_ref[...]
        c = c_ref[...]
        gate = mm(h2, wg[:, at])
        up = mm(h2, wu[:, at])
        act_grad = mm_nt(c, wd[at, :])
        square = gate * gate
        bend = jnp.tanh(gate * (ROOT_2_PI + (ROOT_2_PI * CUBIC) * square))
        half = 0.5 * (1.0 + bend)
        curve = gate * half
        slope = half + (0.5 * gate) * (1.0 - bend * bend) * (
            ROOT_2_PI + (3.0 * ROOT_2_PI * CUBIC) * square
        )
        act = (curve * up).astype(bf16)
        d_up = (act_grad * curve).astype(bf16)
        d_gate = (act_grad * up * slope).astype(bf16)
        acc_out[...] += mm(act, wd[at, :])
        dg[at, :] = mm_tn(act, c).astype(bf16)
        gg[:, at] = mm_tn(h2, d_gate).astype(bf16)
        ug[:, at] = mm_tn(h2, d_up).astype(bf16)
        acc_back[...] += mm_nt(d_gate, wg[:, at]) + mm_nt(d_up, wu[:, at])
        return carry

    lax.fori_loop(0, wg.shape[1] // step_width, column_step, 0)

    stores = []

    def send_out(number, source, targets):
        step_rows = source.shape[0] // pieces
        for piece in range(pieces):
            at = pl.ds(pl.multiple_of(w_rows[piece] * step_rows, step_rows), step_rows)
            copy = pltpu.make_async_copy(source.at[at, :], targets[piece], out_sems.at[number, piece])
            copy.start()
            stores.append(copy)

    send_out(1, gg, gg_refs)
    send_out(2, ug, ug_refs)
    send_out(3, dg, dg_refs)
    middle = mid_ref[...]
    scaling = lax.rsqrt(jnp.mean(middle * middle, axis=-1, keepdims=True) + EPSILON)
    out_ref[...] = (middle + acc_out[...]).astype(bf16)
    incoming = acc_back[...] * gain
    centre = jnp.mean(incoming * middle, axis=-1, keepdims=True)
    d_middle = (
        c_ref[...].astype(f32) + scaling * incoming - middle * (scaling * scaling * scaling * centre)
    )
    dmid_ref[...] = d_middle
    branch = d_middle.astype(bf16)
    og[...] = mm_tn(att[...], branch).astype(bf16)
    send_out(0, og, og_refs)
    att[...] = mm_nt(branch, wo[...]).astype(bf16)
    for block in range(blocks):
        at = pl.ds(pl.multiple_of(att_rows[block] * block_width, block_width), block_width)
        da_refs[block][...] = att[:, at]
    for copy in stores:
        copy.wait()


def middle_stage(att_rows, w_rows, att_blocks, x, c, gain, wo, wg, wu, wd):
    blocks, pieces = len(att_blocks), len(wo)
    rows, width = x.shape
    hidden = wg[0].shape[1]
    step_width = 256
    piece_shapes = [w[0].shape for w in (wo, wg, wu, wd)]
    out_shape = (
        [jax.ShapeDtypeStruct((rows, width), bf16), jax.ShapeDtypeStruct((rows, width), f32)]
        + [jax.ShapeDtypeStruct(att_blocks[0].shape, bf16)] * blocks
        + [jax.ShapeDtypeStruct(s, bf16) for s in piece_shapes for _ in range(pieces)]
    )
    full = [(width, width), (width, hidden), (width, hidden), (hidden, width)]
    weights = list(wo) + list(wg) + list(wu) + list(wd)
    out = pl.pallas_call(
        functools.partial(middle_kernel, blocks, pieces, step_width),
        in_specs=[smem(), smem()]
        + [vmem()] * (blocks + 3)
        + [pl.BlockSpec(memory_space=pltpu.HBM)] * len(weights),
        out_specs=[vmem()] * (2 + blocks) + [pl.BlockSpec(memory_space=pltpu.HBM)] * len(weights),
        out_shape=out_shape,
        scratch_shapes=[pltpu.VMEM(s, bf16) for s in full]
        + [pltpu.VMEM(s, bf16) for s in full]
        + [
            pltpu.VMEM((rows, width), bf16),
            pltpu.VMEM((rows, width), bf16),
            pltpu.VMEM((rows, width), f32),
            pltpu.VMEM((rows, width), f32),
            pltpu.VMEM((rows, width), f32),
            pltpu.SemaphoreType.DMA((4, pieces)),
            pltpu.SemaphoreType.DMA((4, pieces)),
        ],
        compiler_params=params(),
        cost_estimate=cost(
            2 * rows * width * (9 * hidden + 3 * width), 4 * (width * width + 3 * width * hidden)
        ),
        name="middle_stage",
    )(att_rows, w_rows, *att_blocks, x, c, gain, *weights)
    layer_out, d_middle = out[:2]
    d_att = out[2 : 2 + blocks]
    rest = out[2 + blocks :]
    grads = [rest[i * pieces : (i + 1) * pieces] for i in range(4)]
    return (layer_out, d_middle, d_att, grads)


def last_kernel(blocks, pieces, *refs):
    att_rows, w_rows = refs[0], refs[1]
    refs = refs[2:]
    grad_refs = [refs[i * blocks : (i + 1) * blocks] for i in range(3)]
    refs = refs[3 * blocks :]
    x_ref, dmid_ref, gain_ref = refs[:3]
    weight_refs = [refs[3 + i * pieces : 3 + (i + 1) * pieces] for i in range(3)]
    out_ref, grad, total = refs[3 + 3 * pieces :]
    width = x_ref.shape[1]
    block_width = width // blocks
    piece_width = width // pieces
    for kind in range(3):
        for block in range(blocks):
            at = pl.ds(pl.multiple_of(att_rows[block] * block_width, block_width), block_width)
            grad[kind, :, at] = grad_refs[kind][block][...]
    for piece in range(pieces):
        at = pl.ds(pl.multiple_of(w_rows[piece] * piece_width, piece_width), piece_width)
        total[:, at] = (
            mm_nt(grad[0], weight_refs[0][piece][...])
            + mm_nt(grad[1], weight_refs[1][piece][...])
            + mm_nt(grad[2], weight_refs[2][piece][...])
        )
    x = x_ref[...].astype(f32)
    scaling = lax.rsqrt(jnp.mean(x * x, axis=-1, keepdims=True) + EPSILON)
    incoming = total[...] * gain_ref[...].astype(f32)
    centre = jnp.mean(incoming * x, axis=-1, keepdims=True)
    out_ref[...] = dmid_ref[...] + scaling * incoming - x * (scaling * scaling * scaling * centre)


def last_stage(att_rows, w_rows, grads, x, d_middle, gain, weights):
    blocks, pieces = len(grads[0]), len(weights[0])
    rows, width = x.shape
    flat = [g for kind in grads for g in kind]
    flat_weights = [w for kind in weights for w in kind]
    return pl.pallas_call(
        functools.partial(last_kernel, blocks, pieces),
        in_specs=[smem(), smem()] + [vmem()] * (len(flat) + 3 + len(flat_weights)),
        out_specs=vmem(),
        out_shape=jax.ShapeDtypeStruct((rows, width), f32),
        scratch_shapes=[pltpu.VMEM((3, rows, width), bf16), pltpu.VMEM((rows, width), f32)],
        compiler_params=params(),
        cost_estimate=cost(6 * rows * width * width, 6 * width * width),
        name="last_stage",
    )(att_rows, w_rows, *flat, x, d_middle, gain, *flat_weights)


def flip(values, axis, delta):
    count = lax.axis_size(axis)
    return lax.ppermute(values, axis, [(i, i ^ delta) for i in range(count)])


def bits_of(count):
    return [1 << i for i in range(count.bit_length() - 1)]


def gather_pieces(values, axis):
    pieces = {0: values}
    for bit in reversed(bits_of(lax.axis_size(axis))):
        for delta in list(pieces):
            pieces[delta | bit] = flip(pieces[delta], axis, bit)
    return [pieces[delta] for delta in range(len(pieces))]


def add_low(a, b):
    return (a.astype(f32) + b.astype(f32)).astype(bf16)


def scatter_pieces(pieces, axis):
    current = dict(enumerate(pieces))
    for bit in bits_of(lax.axis_size(axis)):
        current = {
            delta: add_low(value, flip(current[delta | bit], axis, bit))
            for delta, value in current.items()
            if not delta & bit
        }
    return current[0]


def sum_over(values, axis):
    place = lax.axis_index(axis)
    bits = bits_of(lax.axis_size(axis))
    for bit in bits:
        half = values.shape[0] // 2
        mine = (place // bit) % 2
        kept = lax.dynamic_slice_in_dim(values, mine * half, half, axis=0)
        given = lax.dynamic_slice_in_dim(values, (1 - mine) * half, half, axis=0)
        values = add_low(kept, flip(given, axis, bit))
    return gather_rows(values, axis, reversed(bits))


def gather_rows(values, axis, bits):
    place = lax.axis_index(axis)
    for bit in bits:
        other = flip(values, axis, bit)
        upper = ((place // bit) % 2) == 1
        values = jnp.concatenate(
            [jnp.where(upper, other, values), jnp.where(upper, values, other)], axis=0
        )
    return values


def gather_blocks_chain(values):
    seq = lax.axis_index("seq")
    place = seq // 2

    def move(array, pairs):
        return lax.ppermute(
            array, "seq", [(a * 2 + low, b * 2 + low) for a, b in pairs for low in range(2)]
        )

    right_1 = move(values, [(1, 0), (2, 1), (3, 2)])
    left_1 = move(values, [(0, 1), (1, 2), (2, 3)])
    right_2 = move(right_1, [(1, 0), (2, 1)])
    left_2 = move(left_1, [(1, 2), (2, 3)])
    near = jnp.where(place % 2 == 0, right_1, left_1)
    far = jnp.where(place < 2, right_2, left_2)
    third = move(far, [(1, 0), (2, 3)])
    cross = jnp.where((place == 0) | (place == 3), third, jnp.where(place == 1, right_1, left_1))
    columns = [values, near, far, cross]
    blocks = []
    for column in columns:
        blocks += [column, flip(column, "seq", 1)]
    return blocks


def exchange_blocks(blocks):
    return [blocks[0]] + [flip(blocks[d], "seq", d) for d in range(1, len(blocks))]


def mask_tables(lengths_row, order_row, real_row, block_order, slots):
    total = order_row.shape[0]
    segments = lengths_row.shape[0]
    ends_at = jnp.cumsum(lengths_row)
    positions = jnp.arange(total, dtype=jnp.int32)
    packed_segment = jnp.sum((positions[:, None] >= ends_at[None, :]).astype(jnp.int32), axis=1)
    packed_code = packed_segment * 2 + (real_row > 0).astype(jnp.int32)
    code = jnp.sum(
        jnp.where(positions[:, None] == order_row[None, :], packed_code[None, :], 0), axis=1
    )
    code = jnp.take(code.reshape(slots, total // slots), block_order, axis=0).reshape(total, 1)
    segment, real = code // 2, code % 2
    lane = jnp.arange(LANES, dtype=jnp.int32)[None, :] % HD
    same = lane == segment
    q_table = jnp.where(same | ((lane == HD - 1) & (real == 0)), 1.0, 0.0).astype(bf16)
    open_to = same & (real == 1)
    k_table = jnp.where(
        lane < segments,
        jnp.where(open_to, 0.0, BLOCKED),
        jnp.where((lane >= HD - 4) & (lane < HD - 1), 1.0, 0.0),
    ).astype(bf16)
    return (q_table, k_table)


def on_device(
    tokens,
    cotangent,
    query_weight,
    key_weight,
    value_weight,
    output_weight,
    gate_weight,
    up_weight,
    down_weight,
    attention_gain,
    feedforward_gain,
    lengths,
    token_order,
    real_token,
):
    x, c = tokens[0], cotangent[0]
    rows, width = x.shape
    slots = lax.axis_size("seq")
    shards = lax.axis_size("fsdp")
    seq, shard = lax.axis_index("seq"), lax.axis_index("fsdp")
    direct = slots == 8 and shards == 4
    heads = width // slots // HD
    own_width = heads * HD
    zero = jnp.zeros((1,), jnp.int32)
    if direct:
        block_order = seq ^ jnp.arange(slots, dtype=jnp.int32)
        att_rows = block_order
        w_rows = shard ^ jnp.arange(shards, dtype=jnp.int32)
    else:
        block_order = jnp.arange(slots, dtype=jnp.int32)
        att_rows, w_rows = zero, zero

    def gather_weight(w):
        if direct:
            return gather_pieces(w, "fsdp")
        return [lax.all_gather(w, "fsdp", axis=0, tiled=True)]

    def reduce_weight(pieces):
        if direct:
            return sum_over(scatter_pieces(pieces, "fsdp"), "seq")
        part = lax.psum_scatter(pieces[0], "fsdp", scatter_dimension=0, tiled=True)
        return lax.psum(part, "seq")

    own_columns = [
        lax.dynamic_slice_in_dim(w, seq * own_width, own_width, axis=1)
        for w in (query_weight, key_weight, value_weight)
    ]
    own_columns = jnp.concatenate(
        [jnp.pad(w, ((0, 0), (0, LANES - own_width))) for w in own_columns], axis=1
    )
    gains = jnp.stack([attention_gain, feedforward_gain])
    if direct:
        column_pieces = jnp.stack(gather_pieces(own_columns, "fsdp"))
        own_columns_full = jnp.take(column_pieces, w_rows, axis=0).reshape(width, 3 * LANES)
        gain_pieces = jnp.stack(gather_pieces(gains, "fsdp"))
        gains_full = jnp.take(gain_pieces, w_rows, axis=0).transpose(1, 0, 2).reshape(2, width)
        x_blocks = gather_blocks_chain(x)
    else:
        own_columns_full = lax.all_gather(own_columns, "fsdp", axis=0, tiled=True)
        gains_full = lax.all_gather(gains, "fsdp", axis=1, tiled=True)
        gathered = lax.all_gather(x, "seq", axis=0)
        x_blocks = [gathered[i] for i in range(slots)]
    gain_1, gain_2 = gains_full[0:1], gains_full[1:2]

    q_table, k_table = mask_tables(lengths[0], token_order[0], real_token[0], block_order, slots)
    state = None
    for slot in range(slots):
        state = project(
            slot, slots, heads, x_blocks[slot], gain_1, own_columns_full, q_table, k_table, state
        )
    qa, ka, va, h1 = state

    att_slots, sums, qbs = [None] * slots, [None] * 4, [None] * 4
    per_call = slots // 4
    for quarter in (3, 2, 1, 0):
        group = list(range(quarter * per_call, (quarter + 1) * per_call))
        out = attend(qa, ka, va, group, slots)
        att_slots[quarter * per_call : (quarter + 1) * per_call] = out[:per_call]
        sums[quarter], qbs[quarter] = out[per_call], out[per_call + 1]
    sums = jnp.concatenate(sums, axis=0)
    qb = jnp.concatenate(qbs, axis=1)

    wo, wg, wu, wd = [
        gather_weight(w) for w in (output_weight, gate_weight, up_weight, down_weight)
    ]
    if direct:
        att_blocks = exchange_blocks(att_slots)
    else:
        stacked = jnp.concatenate(att_slots, axis=0)[:, :own_width]
        att_blocks = [lax.all_to_all(stacked, "seq", split_axis=0, concat_axis=1, tiled=True)]
    layer_out, d_middle, d_att, (og, gg, ug, dg) = middle_stage(
        att_rows, w_rows, att_blocks, x, c, gain_2, wo, wg, wu, wd
    )
    if direct:
        grad_blocks = exchange_blocks(d_att)
    else:
        moved = lax.all_to_all(d_att[0], "seq", split_axis=1, concat_axis=0, tiled=True)
        moved = jnp.pad(moved, ((0, 0), (0, LANES - own_width)))
        grad_blocks = [moved[i * rows : (i + 1) * rows] for i in range(slots)]

    down_grad = reduce_weight(dg)
    gate_grad = reduce_weight(gg)
    up_grad = reduce_weight(ug)
    output_grad = reduce_weight(og)

    qkv_weights = [gather_weight(w) for w in (query_weight, key_weight, value_weight)]
    dk_slots, dv_slots = [None] * slots, [None] * slots
    dq = None
    for quarter in (3, 2, 1, 0):
        group = list(range(quarter * per_call, (quarter + 1) * per_call))
        dk_part, dv_part, dq = attend_back(qb, ka, va, sums, grad_blocks, group, slots, dq)
        dk_slots[quarter * per_call : (quarter + 1) * per_call] = dk_part
        dv_slots[quarter * per_call : (quarter + 1) * per_call] = dv_part
    scale = HD**-0.5
    if heads == 2:
        lane = jnp.arange(LANES, dtype=jnp.int32)[None, :]
        dq = jnp.where(lane < HD, dq[0], dq[1])
    else:
        dq = dq[0]
    dq = (dq * scale).astype(bf16)
    dq_slots = [dq[i * rows : (i + 1) * rows] for i in range(slots)]
    all_grads = jnp.concatenate(
        [dq, jnp.concatenate(dk_slots, axis=0), jnp.concatenate(dv_slots, axis=0)], axis=1
    )
    if direct:
        moved_grads = [exchange_blocks(s) for s in (dq_slots, dk_slots, dv_slots)]
    else:
        moved_grads = [
            [
                lax.all_to_all(
                    all_grads[:, i * LANES : i * LANES + own_width],
                    "seq",
                    split_axis=0,
                    concat_axis=1,
                    tiled=True,
                )
            ]
            for i in range(3)
        ]
    own_term = mm_tn(h1, all_grads).astype(bf16)
    if direct:
        own_pieces = jnp.take(own_term.reshape(shards, width // shards, 3 * LANES), w_rows, axis=0)
        own_share = scatter_pieces([own_pieces[i] for i in range(shards)], "fsdp")
        all_shares = gather_rows(own_share[None], "seq", [4, 2, 1])
        all_shares = all_shares.reshape((2, 2, 2) + own_share.shape).transpose(2, 1, 0, 3, 4)
    else:
        own_share = lax.psum_scatter(own_term, "fsdp", scatter_dimension=0, tiled=True)
        all_shares = lax.all_gather(own_share, "seq", axis=0)
    shard_rows = width // shards
    all_shares = all_shares.reshape(slots, shard_rows, 3, LANES)[..., :own_width].astype(f32)
    query_grad, key_grad, value_grad = [
        all_shares[:, :, i, :].transpose(1, 0, 2).reshape(shard_rows, width) for i in range(3)
    ]
    input_grad = last_stage(att_rows, w_rows, moved_grads, x, d_middle, gain_1, qkv_weights)

    def gain_grad(terms, gain):
        summed = sum(jnp.sum(g * w.astype(f32), axis=1) for g, w in terms)
        return summed / gain.astype(f32)

    output_grad, gate_grad, up_grad, down_grad = [
        g.astype(f32) for g in (output_grad, gate_grad, up_grad, down_grad)
    ]
    attention_gain_grad = gain_grad(
        ((query_grad, query_weight), (key_grad, key_weight), (value_grad, value_weight)),
        attention_gain,
    )
    feedforward_gain_grad = gain_grad(
        ((gate_grad, gate_weight), (up_grad, up_weight)), feedforward_gain
    )
    return (
        layer_out[None],
        input_grad[None],
        query_grad,
        key_grad,
        value_grad,
        output_grad,
        gate_grad,
        up_grad,
        down_grad,
        attention_gain_grad,
        feedforward_gain_grad,
    )


def solution(mesh):
    in_specs = (
        P("fsdp", "seq", None),
        P("fsdp", "seq", None),
        P("fsdp", None),
        P("fsdp", None),
        P("fsdp", None),
        P("fsdp", None),
        P("fsdp", None),
        P("fsdp", None),
        P("fsdp", None),
        P("fsdp"),
        P("fsdp"),
        P("fsdp", None),
        P("fsdp", None),
        P("fsdp", None),
    )
    out_specs = (
        P("fsdp", "seq", None),
        P("fsdp", "seq", None),
        P("fsdp", None),
        P("fsdp", None),
        P("fsdp", None),
        P("fsdp", None),
        P("fsdp", None),
        P("fsdp", None),
        P("fsdp", None),
        P("fsdp"),
        P("fsdp"),
    )
    return jax.shard_map(
        on_device, mesh=mesh, in_specs=in_specs, out_specs=out_specs, check_vma=False
    )
```

```python
import functools

import jax
import jax.numpy as jnp
from jax import lax
from jax.experimental import pallas as pl
from jax.experimental.pallas import tpu as pltpu
from jax.sharding import PartitionSpec as P

HD = 64
LANES = 128
EPSILON = 1e-06
BLOCKED = -(2.0**100)
ROOT_2_PI = 0.7978845608028654
CUBIC = 0.044715
VMEM_LIMIT = 60 * 1024 * 1024

bf16 = jnp.bfloat16
f32 = jnp.float32


def mm(a, b):
    return jnp.dot(a, b, preferred_element_type=f32)


def mm_nt(a, b):
    return lax.dot_general(a, b, (((1,), (1,)), ((), ())), preferred_element_type=f32)


def mm_tn(a, b):
    return lax.dot_general(a, b, (((0,), (0,)), ((), ())), preferred_element_type=f32)


def params(**extra):
    return pltpu.CompilerParams(vmem_limit_bytes=VMEM_LIMIT, **extra)


def cost(flops, moved, transcendentals=0):
    return pl.CostEstimate(
        flops=int(flops), bytes_accessed=int(moved), transcendentals=int(transcendentals)
    )


def vmem():
    return pl.BlockSpec(memory_space=pltpu.VMEM)


def anywhere():
    return pl.BlockSpec(memory_space=pl.ANY)


def smem():
    return pl.BlockSpec(memory_space=pltpu.SMEM)


def lane_ids(rows):
    return lax.broadcasted_iota(jnp.int32, (rows, LANES), 1)


def split3(column):
    high = column.astype(bf16)
    rest = column - high.astype(f32)
    middle = rest.astype(bf16)
    low = (rest - middle.astype(f32)).astype(bf16)
    return (high.astype(f32), middle.astype(f32), low.astype(f32))


def project_kernel(heads, fresh, *refs):
    x_ref, gain_ref, w_ref, qt_ref, kt_ref = refs[1:6]
    qa_ref, ka_ref, va_ref, h1_ref = refs[6:] if fresh else refs[10:]
    x = x_ref[...].astype(f32)
    scaling = lax.rsqrt(jnp.mean(x * x, axis=-1, keepdims=True) + EPSILON)
    h1 = (x * scaling * gain_ref[...].astype(f32)).astype(bf16)
    h1_ref[...] = h1
    qkv = mm(h1, w_ref[...])
    rows = x.shape[0]
    lane = lane_ids(rows)
    q = qkv[:, :LANES].astype(bf16) * jnp.asarray(HD**-0.5, bf16)
    k = qkv[:, LANES : 2 * LANES].astype(bf16)
    v = qkv[:, 2 * LANES :].astype(bf16)
    ones = jnp.where(lane % HD < 3, 1.0, 0.0).astype(bf16)
    for head in range(heads):
        own = lane // HD == head
        qa_ref[head] = jnp.where(own, q, qt_ref[...])
        ka_ref[head] = jnp.where(own, k, kt_ref[...])
        va_ref[head] = jnp.where(own, v, ones)


def project(slot, slots, heads, x, gain, w, q_table, k_table, previous):
    rows, width = x.shape
    total = rows * slots
    row_spec = pl.BlockSpec((rows, LANES), lambda i, s: (s[0], 0))
    head_spec = pl.BlockSpec((heads, rows, LANES), lambda i, s: (0, s[0], 0))
    shapes = [jax.ShapeDtypeStruct((heads, total, LANES), bf16)] * 3 + [
        jax.ShapeDtypeStruct((total, width), bf16)
    ]
    fresh = previous is None
    extra = () if fresh else tuple(previous)
    return pl.pallas_call(
        functools.partial(project_kernel, heads, fresh),
        grid_spec=pltpu.PrefetchScalarGridSpec(
            num_scalar_prefetch=1,
            grid=(1,),
            in_specs=[
                pl.BlockSpec((rows, width), lambda i, s: (0, 0)),
                pl.BlockSpec((1, width), lambda i, s: (0, 0)),
                pl.BlockSpec(w.shape, lambda i, s: (0, 0)),
                row_spec,
                row_spec,
            ]
            + [anywhere()] * len(extra),
            out_specs=[head_spec] * 3 + [pl.BlockSpec((rows, width), lambda i, s: (s[0], 0))],
        ),
        out_shape=shapes,
        input_output_aliases={} if fresh else {6 + i: i for i in range(4)},
        compiler_params=params(),
        cost_estimate=cost(2 * rows * width * 3 * LANES, 4 * rows * width + 2 * w.size),
        name="project",
    )(slot, x, gain, w, q_table, k_table, *extra)


def forward_kernel(heads, q_ref, k_near, v_near, k_ref, v_ref, att_ref, sum_ref, qb_ref):
    pack, rows = q_ref.shape[1], q_ref.shape[3]
    span = pack * rows
    lane = lane_ids(span)
    merged = None
    for head in range(heads):
        q = q_ref[head].reshape(span, LANES)
        key = k_near[head].reshape(span, LANES)
        value = v_near[head].reshape(span, LANES)
        own = lane // HD == head
        other = HD if head == 0 else 0
        scores = mm_nt(q, k_ref[head])
        q_wide = q.astype(f32)
        padded = q_wide[:, other + HD - 1 : other + HD] > 0.5
        own_score = jnp.sum(jnp.where(own, q_wide * key.astype(f32), 0.0), axis=-1, keepdims=True)
        top = jnp.max(scores, axis=-1, keepdims=True)
        top = jnp.where(padded, jnp.maximum(top, own_score), top)
        weights = jnp.exp(scores - top).astype(bf16)
        mixed = mm(weights, v_ref[head])
        own_weight = jnp.where(padded, jnp.exp(own_score - top), 0.0).astype(bf16).astype(f32)
        mixed = mixed + own_weight * value.astype(f32)
        total = mixed[:, other : other + 1]
        log_total = top + jnp.log(total)
        mixed = mixed * (1.0 / total)
        merged = mixed if merged is None else jnp.where(own, mixed, merged)
        filled = q_wide
        for place, part in enumerate(split3(-log_total)):
            filled = jnp.where(lane == other + HD - 4 + place, part, filled)
        qb_ref[head] = filled.astype(bf16).reshape(pack, 1, rows, LANES)
    att_ref[...] = merged.astype(bf16).reshape(pack, rows, LANES)
    sum_ref[...] = merged.reshape(pack, 1, rows, LANES)


def forward_body(heads, aliased, *refs):
    forward_kernel(heads, *(refs[:5] + refs[5 + aliased :]))


def attend(qa, ka, va, part, parts, slots, span, previous):
    heads, total, _ = qa.shape
    rows = total // slots // parts
    pack = max(1, min(slots, 320 // rows))
    shape = (heads, slots, parts, rows, LANES)
    view = [a.reshape(shape) for a in (qa, ka, va)]
    begin = span[0] // pack
    block = pl.BlockSpec((heads, pack, 1, rows, LANES), lambda i: (0, begin + i, part, 0, 0))
    whole = pl.BlockSpec(ka.shape, lambda i: (0, 0, 0))
    extra = tuple(previous)
    return pl.pallas_call(
        functools.partial(forward_body, heads, len(extra)),
        grid=((span[1] - span[0]) // pack,),
        in_specs=[block, block, block, whole, whole] + [anywhere()] * len(extra),
        out_specs=[
            pl.BlockSpec((pack, rows, LANES), lambda i: (begin + i, 0, 0)),
            pl.BlockSpec((pack, 1, rows, LANES), lambda i: (begin + i, part, 0, 0)),
            block,
        ],
        out_shape=[
            jax.ShapeDtypeStruct((slots, rows, LANES), bf16),
            jax.ShapeDtypeStruct(shape[1:], f32),
            jax.ShapeDtypeStruct(shape, bf16),
        ],
        input_output_aliases={5 + i: 3 - len(extra) + i for i in range(len(extra))},
        compiler_params=params(),
        cost_estimate=cost(
            8 * heads * total * total * LANES // parts,
            4 * heads * total * LANES,
            heads * total * total // parts,
        ),
        name="attend",
    )(*view, ka, va, *extra)


def backward_kernel(heads, part, parts, tile, *refs):
    first, last = part == 0, part == parts - 1
    qb_ref, k_ref, v_ref = refs[:3]
    if first:
        sum_ref, grad_ref, kv_ref, dq_ref, gb_ref, dk_acc, dv_acc = refs[3:]
        dq_acc = dq_ref
    elif last:
        gb_ref, dq_in, kv_ref, dq_ref, dq_acc, dk_acc, dv_acc = refs[3:]
    else:
        gb_ref, dq_in, kv_ref, dq_ref, dk_acc, dv_acc = refs[3:]
        dq_acc = dq_ref
    slots, rows = k_ref.shape[1], k_ref.shape[3]
    total = qb_ref.shape[1]
    span = slots * rows
    pack = max(1, min(slots, 320 // rows))
    if first:
        block_rows = grad_ref.shape[1]
        lane = lane_ids(block_rows)

        def prepare(slot, carry):
            at = pl.ds(pl.multiple_of(slot * block_rows, block_rows), block_rows)
            grad = grad_ref[slot].astype(f32)
            product = grad * sum_ref[at, :]
            for head in range(heads):
                other = HD if head == 0 else 0
                own = lane // HD == head
                delta = jnp.sum(jnp.where(own, product, 0.0), axis=-1, keepdims=True)
                filled = jnp.where(own, grad, 0.0)
                for place, piece in enumerate(split3(-delta)):
                    filled = jnp.where(lane == other + place, piece, filled)
                gb_ref[head, at, :] = filled.astype(bf16)
                dq_acc[head, at, :] = jnp.zeros((block_rows, LANES), f32)
            return carry

        lax.fori_loop(0, slots, prepare, 0)
    else:
        dq_acc[...] = dq_in[...]
    width = pack * rows
    lane = lane_ids(width)
    for index in range(slots // pack):
        keys = slice(index * pack, (index + 1) * pack)
        dk_acc[...] = jnp.zeros_like(dk_acc)
        dv_acc[...] = jnp.zeros_like(dv_acc)

        def step(number, carry):
            at = pl.ds(pl.multiple_of(number * tile, tile), tile)
            for head in range(heads):
                key = k_ref[head, keys].reshape(width, LANES)
                value = v_ref[head, keys].reshape(width, LANES)
                q = qb_ref[head, at, :]
                g = gb_ref[head, at, :]
                weights = jnp.exp(mm_nt(key, q))
                inner = mm_nt(value, g)
                score_grad = (weights * inner).astype(bf16)
                dv_acc[head] += mm(weights.astype(bf16), g)
                dk_acc[head] += mm(score_grad, q)
                dq_acc[head, at, :] += mm_tn(score_grad, key)
            return carry

        lax.fori_loop(0, total // tile, step, 0)
        dk_all, dv_all = None, None
        for head in range(heads):
            other = HD if head == 0 else 0
            own = lane // HD == head
            counted = own | ((lane >= other + HD - 4) & (lane < other + HD - 1))
            starts = [
                slot * (total // slots) + part * rows
                for slot in range(index * pack, (index + 1) * pack)
            ]
            q = jnp.concatenate([qb_ref[head, b : b + rows, :] for b in starts], axis=0).astype(f32)
            g = jnp.concatenate([gb_ref[head, b : b + rows, :] for b in starts], axis=0).astype(f32)
            k = k_ref[head, keys].reshape(width, LANES).astype(f32)
            v = v_ref[head, keys].reshape(width, LANES).astype(f32)
            padded = q[:, other + HD - 1 : other + HD] > 0.5
            score = jnp.sum(jnp.where(counted, q * k, 0.0), axis=-1, keepdims=True)
            weight = jnp.where(padded, jnp.exp(score), 0.0)
            inner = jnp.sum(v * g, axis=-1, keepdims=True)
            score_grad = (weight * inner).astype(bf16).astype(f32)
            weight = weight.astype(bf16).astype(f32)
            dk = dk_acc[head] + score_grad * q
            dv = dv_acc[head] + weight * g
            dq = score_grad * k
            for place, b in enumerate(starts):
                dq_acc[head, b : b + rows, :] += dq[place * rows : (place + 1) * rows, :]
            dk_all = dk if head == 0 else jnp.where(own, dk, dk_all)
            dv_all = dv if head == 0 else jnp.where(own, dv, dv_all)
        kv_ref[keys, 0] = dk_all.astype(bf16).reshape(pack, rows, LANES)
        kv_ref[keys, 1] = dv_all.astype(bf16).reshape(pack, rows, LANES)
    if last:
        block_rows = total // slots
        lane = lane_ids(block_rows)
        for slot in range(slots):
            at = slice(slot * block_rows, (slot + 1) * block_rows)
            dq = dq_acc[0, at, :]
            if heads == 2:
                dq = jnp.where(lane < HD, dq, dq_acc[1, at, :])
            dq_ref[slot] = (dq * HD**-0.5).astype(bf16)


def attend_back(qb, ka, va, part, parts, slots, sums, grads, state):
    heads, total, _ = ka.shape
    rows = total // slots // parts
    first, last = part == 0, part == parts - 1
    shape = (heads, slots, parts, rows, LANES)
    near = pl.BlockSpec((heads, slots, 1, rows, LANES), lambda i: (0, 0, part, 0, 0))
    wide = pl.BlockSpec((heads, total, LANES), lambda i: (0, 0, 0))
    pack = max(1, min(slots, 320 // rows))
    accumulator = pltpu.VMEM((heads, pack * rows, LANES), f32)
    if first:
        inputs = [sums, grads]
        in_specs = [
            pl.BlockSpec((total, LANES), lambda i: (0, 0)),
            pl.BlockSpec(grads.shape, lambda i: (0, 0, 0)),
        ]
    else:
        inputs, in_specs = list(state), [wide, wide]
    out_shape = [jax.ShapeDtypeStruct((slots, 2, rows, LANES), bf16)]
    out_specs = [pl.BlockSpec((slots, 2, rows, LANES), lambda i: (0, 0, 0, 0))]
    scratch = [accumulator, accumulator]
    if last:
        out_shape.append(jax.ShapeDtypeStruct((slots, total // slots, LANES), bf16))
        out_specs.append(pl.BlockSpec((slots, total // slots, LANES), lambda i: (0, 0, 0)))
        scratch = [pltpu.VMEM((heads, total, LANES), f32)] + scratch
    else:
        out_shape.append(jax.ShapeDtypeStruct((heads, total, LANES), f32))
        out_specs.append(wide)
    if first:
        out_shape.append(jax.ShapeDtypeStruct((heads, total, LANES), bf16))
        out_specs.append(wide)
    return pl.pallas_call(
        functools.partial(backward_kernel, heads, part, parts, 512),
        grid=(1,),
        in_specs=[wide, near, near] + in_specs,
        out_specs=out_specs,
        out_shape=out_shape,
        scratch_shapes=scratch,
        compiler_params=params(),
        cost_estimate=cost(
            20 * heads * total * total * LANES // parts,
            12 * heads * total * LANES,
            heads * total * total // parts,
        ),
        name="attend_back",
    )(qb, ka.reshape(shape), va.reshape(shape), *inputs)


def own_kernel(halves, *refs):
    w_rows, h_ref, dq_ref = refs[:3]
    parts = len(refs) - 4 - halves
    kv_refs, outs, term = refs[3 : 3 + parts], refs[3 + parts : -1], refs[-1]
    slots, _, rows, width = h_ref.shape
    total = slots * parts * rows
    term[:, :LANES] = mm_tn(
        h_ref[...].reshape(total, width), dq_ref[...].reshape(total, LANES)
    ).astype(bf16)
    for kind in range(2):
        summed = None
        for part in range(parts):
            piece = mm_tn(
                h_ref[:, part].reshape(slots * rows, width),
                kv_refs[part][:, kind].reshape(slots * rows, LANES),
            )
            summed = piece if summed is None else summed + piece
        term[:, (kind + 1) * LANES : (kind + 2) * LANES] = summed.astype(bf16)
    place_rows(halves, w_rows, term, outs)


def place_rows(halves, w_rows, source, outs):
    inner, step_rows = outs[0].shape[0], outs[0].shape[1]
    for half in range(halves):
        for index in range(inner):
            piece = index * halves + half
            at = pl.ds(pl.multiple_of(w_rows[piece] * step_rows, step_rows), step_rows)
            outs[half][index] = source[at, :]


def own_terms(w_rows, h1, dq, kvs, shards, halves):
    slots, rows = kvs[0].shape[0], kvs[0].shape[2]
    width = h1.shape[1]
    pieces = shards if halves == 2 else 1
    shape = jax.ShapeDtypeStruct((pieces // halves, width // pieces, 3 * LANES), bf16)
    return pl.pallas_call(
        functools.partial(own_kernel, halves),
        in_specs=[smem()] + [vmem()] * (2 + len(kvs)),
        out_specs=[vmem()] * halves,
        out_shape=[shape] * halves,
        scratch_shapes=[pltpu.VMEM((width, 3 * LANES), bf16)],
        compiler_params=params(),
        cost_estimate=cost(2 * h1.size * 3 * LANES, 2 * h1.size),
        name="own_terms",
    )(w_rows, h1.reshape(slots, len(kvs), rows, width), dq, *kvs)


def middle_kernel(parts, pieces, halves, step_width, layout, *refs):
    w_rows = refs[0]
    att_refs = refs[1 : 1 + parts]
    x_ref, c_ref, gain_ref = refs[1 + parts : 4 + parts]
    refs = refs[4 + parts :]
    sources, refs = refs[: len(layout)], refs[len(layout) :]
    out_ref, dmid_ref, da_ref = refs[:3]
    refs = refs[3:]
    og_refs, gg_refs, ug_refs, dg_refs = [refs[i * halves : (i + 1) * halves] for i in range(4)]
    refs = refs[4 * halves :]
    wo, wg, wu, wd, og, gg, ug, dg, att, h2_ref, h2t_ref, mid_ref, acc_out, acc_back = refs[:14]
    in_sems, out_sems = refs[14:]

    loads = [[], [], [], []]
    targets = (wo, wg, wu, wd)
    for place, (number, piece, offset) in enumerate(layout):
        target = targets[number]
        step_rows = target.shape[0] // pieces
        begin = pl.multiple_of(w_rows[piece] * step_rows + offset, 16)
        at = pl.ds(begin, sources[place].shape[0])
        copy = pltpu.make_async_copy(sources[place], target.at[at, :], in_sems.at[place])
        copy.start()
        loads[number].append(copy)

    rows, width = x_ref.shape
    blocks = da_ref.shape[0]
    block_width = width // blocks
    part_rows = rows // parts
    for part in range(parts):
        for block in range(blocks):
            att[
                part * part_rows : (part + 1) * part_rows,
                block * block_width : (block + 1) * block_width,
            ] = att_refs[part][block][:, :block_width]
    for copy in loads[0]:
        copy.wait()
    gain = gain_ref[...].astype(f32)
    middle = x_ref[...].astype(f32) + mm(att[...], wo[...])
    scaling = lax.rsqrt(jnp.mean(middle * middle, axis=-1, keepdims=True) + EPSILON)
    h2 = (middle * scaling * gain).astype(bf16)
    h2_ref[...] = h2
    h2t_ref[...] = h2.T
    mid_ref[...] = middle
    acc_out[...] = jnp.zeros_like(acc_out)
    acc_back[...] = jnp.zeros_like(acc_back)
    for copy in loads[1] + loads[2] + loads[3]:
        copy.wait()

    def row_copies(number, source, targets, columns):
        step_rows = source.shape[0] // pieces
        copies = []
        for piece in range(pieces):
            at = pl.ds(pl.multiple_of(w_rows[piece] * step_rows, step_rows), step_rows)
            target = targets[piece % halves].at[piece // halves, :, columns]
            copies.append(
                pltpu.make_async_copy(source.at[at, columns], target, out_sems.at[number, piece])
            )
        return copies

    def column_step(number, carry):
        at = pl.ds(pl.multiple_of(number * step_width, step_width), step_width)
        h2 = h2_ref[...]
        c = c_ref[...]
        gate = mm(h2, wg[:, at])
        up = mm(h2, wu[:, at])
        act_grad = mm_nt(c, wd[at, :])
        square = gate * gate
        bend = jnp.tanh(gate * (ROOT_2_PI + (ROOT_2_PI * CUBIC) * square))
        half = 0.5 * (1.0 + bend)
        curve = gate * half
        slope = half + (0.5 * gate) * (1.0 - bend * bend) * (
            ROOT_2_PI + (3.0 * ROOT_2_PI * CUBIC) * square
        )
        act = (curve * up).astype(bf16)
        d_up = (act_grad * curve).astype(bf16)
        d_gate = (act_grad * up * slope).astype(bf16)
        acc_out[...] += mm(act, wd[at, :])
        dg[at, :] = mm_tn(act, c).astype(bf16)
        gg[:, at] = mm(h2t_ref[...], d_gate).astype(bf16)
        ug[:, at] = mm(h2t_ref[...], d_up).astype(bf16)
        acc_back[...] += mm_nt(d_gate, wg[:, at]) + mm_nt(d_up, wu[:, at])
        for kind, source, targets in ((1, gg, gg_refs), (2, ug, ug_refs)):
            for copy in row_copies(kind, source, targets, at):
                copy.start()
        return carry

    lax.fori_loop(0, wg.shape[1] // step_width, column_step, 0)

    everything = slice(None)
    stores = row_copies(3, dg, dg_refs, everything)
    for copy in stores:
        copy.start()
    middle = mid_ref[...]
    scaling = lax.rsqrt(jnp.mean(middle * middle, axis=-1, keepdims=True) + EPSILON)
    out_ref[...] = (middle + acc_out[...]).astype(bf16)
    incoming = acc_back[...] * gain
    centre = jnp.mean(incoming * middle, axis=-1, keepdims=True)
    d_middle = (
        c_ref[...].astype(f32)
        + scaling * incoming
        - middle * (scaling * scaling * scaling * centre)
    )
    dmid_ref[...] = d_middle
    branch = d_middle.astype(bf16)
    og[...] = mm_tn(att[...], branch).astype(bf16)
    last_stores = row_copies(0, og, og_refs, everything)
    for copy in last_stores:
        copy.start()
    d_att = mm_nt(branch, wo[...]).astype(bf16)
    for block in range(blocks):
        piece = d_att[:, block * block_width : (block + 1) * block_width]
        if block_width < LANES:
            piece = jnp.concatenate([piece] * (LANES // block_width), axis=1)
        da_ref[block] = piece
    stores += row_copies(1, gg, gg_refs, everything) + row_copies(2, ug, ug_refs, everything)
    for copy in stores + last_stores:
        copy.wait()


def middle_stage(w_rows, att_parts, x, c, gain, wo, wg, wu, wd, pieces, halves):
    parts = len(att_parts)
    rows, width = x.shape
    hidden = wg[0][2].shape[1]
    layout = [
        (number, piece, offset)
        for number, entries in enumerate((wo, wg, wu, wd))
        for piece, offset, _ in entries
    ]
    weights = [w for entries in (wo, wg, wu, wd) for _, _, w in entries]
    slots = att_parts[0].shape[0]
    step_width = 256
    full = [(width, width), (width, hidden), (width, hidden), (hidden, width)]
    piece_shapes = [(a // pieces, b) for a, b in full]
    out_shape = [
        jax.ShapeDtypeStruct((rows, width), bf16),
        jax.ShapeDtypeStruct((rows, width), f32),
        jax.ShapeDtypeStruct((slots, rows, LANES), bf16),
    ] + [
        jax.ShapeDtypeStruct((pieces // halves,) + s, bf16)
        for s in piece_shapes
        for _ in range(halves)
    ]
    hbm = pl.BlockSpec(memory_space=pltpu.HBM)
    out = pl.pallas_call(
        functools.partial(middle_kernel, parts, pieces, halves, step_width, layout),
        in_specs=[smem()] + [vmem()] * (parts + 3) + [hbm] * len(weights),
        out_specs=[vmem()] * 3 + [hbm] * (4 * halves),
        out_shape=out_shape,
        scratch_shapes=[pltpu.VMEM(s, bf16) for s in full]
        + [pltpu.VMEM(s, bf16) for s in full]
        + [
            pltpu.VMEM((rows, width), bf16),
            pltpu.VMEM((rows, width), bf16),
            pltpu.VMEM((width, rows), bf16),
            pltpu.VMEM((rows, width), f32),
            pltpu.VMEM((rows, width), f32),
            pltpu.VMEM((rows, width), f32),
            pltpu.SemaphoreType.DMA((len(layout),)),
            pltpu.SemaphoreType.DMA((4, pieces)),
        ],
        compiler_params=params(),
        cost_estimate=cost(
            2 * rows * width * (9 * hidden + 3 * width), 4 * (width * width + 3 * width * hidden)
        ),
        name="middle_stage",
    )(w_rows, *att_parts, x, c, gain, *weights)
    return (out[:3], [out[3 + i * halves : 3 + (i + 1) * halves] for i in range(4)])


def last_kernel(parts, pieces, *refs):
    w_rows, dq_ref = refs[:2]
    kv_refs = refs[2 : 2 + parts]
    x_ref, dmid_ref, gain_ref = refs[2 + parts : 5 + parts]
    weight_refs = refs[5 + parts : 5 + parts + pieces]
    out_ref, grad, total = refs[5 + parts + pieces :]
    rows, width = x_ref.shape
    blocks = dq_ref.shape[0]
    block_width = width // blocks
    piece_width = width // pieces
    done = 0
    for part in range(parts):
        part_rows = kv_refs[part].shape[2]
        for block in range(blocks):
            lanes = slice(block * block_width, (block + 1) * block_width)
            for kind in range(2):
                grad[kind + 1, done : done + part_rows, lanes] = kv_refs[part][block, kind][
                    :, :block_width
                ]
        done += part_rows
    for block in range(blocks):
        lanes = slice(block * block_width, (block + 1) * block_width)
        grad[0, :, lanes] = dq_ref[block][:, :block_width]
    for piece in range(pieces):
        at = pl.ds(pl.multiple_of(w_rows[piece] * piece_width, piece_width), piece_width)
        w = weight_refs[piece]
        total[:, at] = (
            mm_nt(grad[0], w[:, :width])
            + mm_nt(grad[1], w[:, width : 2 * width])
            + mm_nt(grad[2], w[:, 2 * width :])
        )
    x = x_ref[...].astype(f32)
    scaling = lax.rsqrt(jnp.mean(x * x, axis=-1, keepdims=True) + EPSILON)
    incoming = total[...] * gain_ref[...].astype(f32)
    centre = jnp.mean(incoming * x, axis=-1, keepdims=True)
    out_ref[...] = dmid_ref[...] + scaling * incoming - x * (scaling * scaling * scaling * centre)


def last_stage(w_rows, dq, kvs, x, d_middle, gain, weights):
    rows, width = x.shape
    return pl.pallas_call(
        functools.partial(last_kernel, len(kvs), len(weights)),
        in_specs=[smem()] + [vmem()] * (4 + len(kvs) + len(weights)),
        out_specs=vmem(),
        out_shape=jax.ShapeDtypeStruct((rows, width), f32),
        scratch_shapes=[pltpu.VMEM((3, rows, width), bf16), pltpu.VMEM((rows, width), f32)],
        compiler_params=params(),
        cost_estimate=cost(6 * rows * width * width, 6 * width * width),
        name="last_stage",
    )(w_rows, dq, *kvs, x, d_middle, gain, *weights)


def flip(values, axis, delta):
    count = lax.axis_size(axis)
    return lax.ppermute(values, axis, [(i, i ^ delta) for i in range(count)])


def after(values, *others):
    return lax.optimization_barrier((values, *others))[0]


def bits_of(count):
    return [1 << i for i in range(count.bit_length() - 1)]


def add_low(a, b):
    return (a.astype(f32) + b.astype(f32)).astype(bf16)


def cut(values, start, size):
    return lax.dynamic_slice_in_dim(values, start, size, axis=0)


class Line:
    def __init__(self):
        self.last = None

    def hold(self, values):
        if self.last is not None:
            values = after(values, self.last)
        self.last = values
        return values


class Reduction:
    def __init__(self, kept, given, line):
        self.kept, self.given, self.line = kept, given, line

    def core(self):
        arrived = flip(self.given, "fsdp", 1)
        self.own = add_low(self.kept[0], arrived[0])
        self.send = add_low(self.kept[1], arrived[1])

    def across(self):
        self.arrived = flip(self.send, "fsdp", 2)

    def halve(self, bit):
        place = lax.axis_index("seq")
        half = self.own.shape[0] // 2
        mine = (place // bit) % 2
        keep, give = mine * half, (1 - mine) * half
        given = add_low(cut(self.own, give, half), cut(self.arrived, give, half))
        kept = add_low(cut(self.own, keep, half), cut(self.arrived, keep, half))
        self.own, self.arrived = kept, flip(self.line.hold(given), "seq", bit)

    def settle(self):
        self.own = add_low(self.own, self.arrived)
        self.joined = None

    def widen(self, bit):
        self.join()
        self.own = self.line.hold(self.own)
        self.arrived, self.joined = flip(self.own, "seq", bit), bit

    def join(self):
        if self.joined is None:
            return
        upper = ((lax.axis_index("seq") // self.joined) % 2) == 1
        first = jnp.where(upper, self.arrived, self.own)
        second = jnp.where(upper, self.own, self.arrived)
        self.own, self.joined = jnp.concatenate([first, second], axis=0), None


def mask_tables(lengths_row, order_row, real_row):
    total = order_row.shape[0]
    segments = lengths_row.shape[0]
    ends_at = jnp.cumsum(lengths_row)
    positions = jnp.arange(total, dtype=jnp.int32)
    packed_segment = jnp.sum((positions[:, None] >= ends_at[None, :]).astype(jnp.int32), axis=1)
    packed_code = packed_segment * 2 + (real_row > 0).astype(jnp.int32)
    code = jnp.sum(
        jnp.where(positions[:, None] == order_row[None, :], packed_code[None, :], 0), axis=1
    ).reshape(total, 1)
    segment, real = code // 2, code % 2
    lane = jnp.arange(LANES, dtype=jnp.int32)[None, :] % HD
    same = lane == segment
    q_table = jnp.where(same | ((lane == HD - 1) & (real == 0)), 1.0, 0.0).astype(bf16)
    open_to = same & (real == 1)
    k_table = jnp.where(
        lane < segments,
        jnp.where(open_to, 0.0, BLOCKED),
        jnp.where((lane >= HD - 4) & (lane < HD - 1), 1.0, 0.0),
    ).astype(bf16)
    return (q_table, k_table)


def move_chain(array, pairs):
    return lax.ppermute(
        array, "seq", [(a * 2 + low, b * 2 + low) for a, b in pairs for low in range(2)]
    )


def turn(blocks):
    return lax.all_to_all(blocks, "seq", split_axis=0, concat_axis=0, tiled=True)


def on_device(
    tokens,
    cotangent,
    query_weight,
    key_weight,
    value_weight,
    output_weight,
    gate_weight,
    up_weight,
    down_weight,
    attention_gain,
    feedforward_gain,
    lengths,
    token_order,
    real_token,
):
    x, c = tokens[0], cotangent[0]
    rows, width = x.shape
    slots = lax.axis_size("seq")
    shards = lax.axis_size("fsdp")
    seq, shard = lax.axis_index("seq"), lax.axis_index("fsdp")
    direct = slots == 8 and shards == 4
    heads = width // slots // HD
    own_width = heads * HD
    shard_rows = width // shards
    halves = 2 if direct else 1

    own_columns = [
        lax.dynamic_slice_in_dim(w, seq * own_width, own_width, axis=1)
        for w in (query_weight, key_weight, value_weight)
    ]
    gains = jnp.stack([attention_gain, feedforward_gain], axis=1)
    own_columns = jnp.concatenate(
        [jnp.pad(w, ((0, 0), (0, LANES - own_width))) for w in own_columns]
        + [jnp.pad(gains, ((0, 0), (0, LANES - 2)))],
        axis=1,
    )
    qkv_weight = jnp.concatenate([query_weight, key_weight, value_weight], axis=1)
    q_table, k_table = mask_tables(lengths[0], token_order[0], real_token[0])

    if direct:
        w_rows = shard ^ jnp.arange(shards, dtype=jnp.int32)
        place = seq // 2
        half = shard_rows // 2
        columns_x = flip(own_columns, "fsdp", 2)
        beside = flip(x, "seq", 1)
        right_1 = move_chain(x, [(1, 0), (2, 1), (3, 2)])
        left_1 = move_chain(x, [(0, 1), (1, 2), (2, 3)])
        output_x = flip(output_weight, "fsdp", 2)
        both = jnp.stack([own_columns, columns_x])
        both_c = flip(both, "fsdp", 1)
        column_pieces = jnp.stack([both[0], both_c[0], both[1], both_c[1]])
        columns_full = jnp.take(column_pieces, w_rows, axis=0).reshape(width, 4 * LANES)
        near = jnp.where(place % 2 == 0, right_1, left_1)
        right_1, left_1, near, _, _ = lax.optimization_barrier(
            (right_1, left_1, near, beside, output_x)
        )
        right_2 = move_chain(right_1, [(1, 0), (2, 1)])
        left_2 = move_chain(left_1, [(1, 2), (2, 3)])
        near_beside = flip(near, "seq", 1)
        gate_x1 = flip(after(gate_weight[:half], near), "fsdp", 2)
        far = jnp.where(place < 2, right_2, left_2)
        block_slots = [seq ^ d for d in range(slots)]
    else:
        w_rows = jnp.zeros((1,), jnp.int32)
        columns_full = lax.all_gather(own_columns, "fsdp", axis=0, tiled=True)
        gathered = lax.all_gather(x, "seq", axis=0)
        x_blocks = [gathered[i] for i in range(slots)]
        block_slots = [jnp.asarray(i, jnp.int32) for i in range(slots)]

    own_columns_full = columns_full[:, : 3 * LANES]
    gain_1 = columns_full[:, 3 * LANES].reshape(1, width)
    gain_2 = columns_full[:, 3 * LANES + 1].reshape(1, width)
    state = None

    def project_block(number, block, state):
        slot = block_slots[number].reshape(1).astype(jnp.int32)
        return project(
            slot, slots, heads, block, gain_1, own_columns_full, q_table, k_table, state
        )

    if direct:
        state = project_block(0, x, state)
        state = project_block(1, beside, state)
        far, _, _, _ = lax.optimization_barrier((far, near_beside, gate_x1, state[0]))
        third = move_chain(far, [(1, 0), (2, 3)])
        far_beside = flip(far, "seq", 1)
        gate_x2 = flip(after(gate_weight[half:], far), "fsdp", 2)
        gate_c = flip(after(gate_weight, far), "fsdp", 1)
        state = project_block(2, near, state)
        state = project_block(3, near_beside, state)
        state = project_block(4, far, state)
        cross = jnp.where(
            (place == 0) | (place == 3), third, jnp.where(place == 1, right_1, left_1)
        )
        cross, _, _, _, _ = lax.optimization_barrier(
            (cross, far_beside, gate_x2, gate_c, state[0])
        )
        cross_beside = flip(cross, "seq", 1)
        up_x1 = flip(after(up_weight[:half], cross), "fsdp", 2)
        gate_xc1 = flip(after(gate_x1, cross), "fsdp", 1)
        up_c = flip(after(up_weight, cross), "fsdp", 1)
        state = project_block(5, far_beside, state)
        state = project_block(6, cross, state)
        cross_beside, _, _, _ = lax.optimization_barrier((cross_beside, up_x1, gate_xc1, up_c))
        state = project_block(7, cross_beside, state)
    else:
        for number, block in enumerate(x_blocks):
            state = project_block(number, block, state)
    qa, ka, va, h1 = state

    att_first, sums, qb = attend(qa, ka, va, 0, 2, slots, (0, slots), ())
    middle_slot = slots // 2
    if direct:
        up_x2 = flip(after(up_weight[half:], qa), "fsdp", 2)
        down_x = flip(after(down_weight, qa), "fsdp", 2)
        gate_xc2 = flip(after(gate_x2, qa), "fsdp", 1)
        output_c = flip(after(output_weight, qa), "fsdp", 1)
        qb, _, _, _ = lax.optimization_barrier((qb, up_x2, gate_xc2, output_c))
    att_turned = turn(att_first)
    att_second, sums, qb = attend(
        qa, ka, va, 1, 2, slots, (0, middle_slot), (sums, qb)
    )
    if direct:
        output_xc = flip(after(output_x, att_first), "fsdp", 1)
        up_xc1 = flip(after(up_x1, att_first), "fsdp", 1)
        up_xc2 = flip(after(up_x2, att_first), "fsdp", 1)
        qb, _, _, _, _ = lax.optimization_barrier((qb, output_xc, up_xc1, up_xc2, att_turned))
    att_second, sums, qb = attend(
        qa, ka, va, 1, 2, slots, (middle_slot, slots), (att_second, sums, qb)
    )
    if direct:
        down_c = flip(after(down_weight, att_second), "fsdp", 1)
        down_xc = flip(after(down_x, att_second), "fsdp", 1)
        qkv_x = flip(after(qkv_weight, att_second), "fsdp", 2)
        wg = [
            (0, 0, gate_weight), (1, 0, gate_c), (2, 0, gate_x1), (2, half, gate_x2),
            (3, 0, gate_xc1), (3, half, gate_xc2),
        ]
        wu = [
            (0, 0, up_weight), (1, 0, up_c), (2, 0, up_x1), (2, half, up_x2),
            (3, 0, up_xc1), (3, half, up_xc2),
        ]
        wd = [(0, 0, down_weight), (1, 0, down_c), (2, 0, down_x), (3, 0, down_xc)]
        wo = [(0, 0, output_weight), (1, 0, output_c), (2, 0, output_x), (3, 0, output_xc)]
        pieces = shards
    else:
        wo, wg, wu, wd = [
            [(0, 0, lax.all_gather(w, "fsdp", axis=0, tiled=True))]
            for w in (output_weight, gate_weight, up_weight, down_weight)
        ]
        pieces = 1
    att_parts = [att_turned, turn(att_second)]
    total = rows * slots
    sums = sums.reshape(total, LANES)
    qb = qb.reshape(heads, total, LANES)

    (layer_out, d_middle, d_att), (og, gg, ug, dg) = middle_stage(
        w_rows, att_parts, x, c, gain_2, wo, wg, wu, wd, pieces, halves
    )
    grad_blocks = turn(d_att)
    parts = 4
    back = functools.partial(attend_back, qb, ka, va)
    if direct:
        line = Line()
        gate_r, up_r, down_r, output_r = [
            Reduction(kept, given, line) for kept, given in (gg, ug, dg, og)
        ]
        gate_r.given = after(gate_r.given, qkv_x)
        core_line = Line()
        for r in (gate_r, up_r, down_r, output_r):
            r.core()
            r.own, r.send = core_line.hold(r.own), core_line.hold(r.send)
            r.across()
        qkv_c = flip(after(qkv_weight, d_att), "fsdp", 1)
        grad_blocks = lax.optimization_barrier(
            (grad_blocks, gate_r.send, up_r.send, down_r.send, output_r.send)
        )[0]
    else:
        qkv_pieces = [lax.all_gather(qkv_weight, "fsdp", axis=0, tiled=True)]
    kv_0, dq, gb = back(0, parts, slots, sums, grad_blocks, None)
    kv_1, dq = back(1, parts, slots, None, None, (gb, dq))
    if direct:
        gate_r.arrived = after(gate_r.arrived, kv_1)
        gate_r.halve(1)
        gb = lax.optimization_barrier((gb, gate_r.own, qkv_c))[0]
    kv_early = turn(jnp.concatenate([kv_0, kv_1], axis=2))
    kv_2, dq = back(2, parts, slots, None, None, (gb, dq))
    if direct:
        up_r.arrived = after(up_r.arrived, kv_2)
        up_r.halve(2)
        gb = after(gb, up_r.own)
    kv_3, dq = back(3, parts, slots, None, None, (gb, dq))
    kv_late = jnp.concatenate([kv_2, kv_3], axis=2)
    late = turn(jnp.concatenate([kv_late.reshape(slots, rows, LANES), dq], axis=1))
    kv_late = late[:, :rows].reshape(kv_late.shape)
    dq_turned = late[:, rows:]
    if direct:
        gate_r.arrived = after(gate_r.arrived, kv_3)
        gate_r.halve(2)
        qkv_xc = flip(after(qkv_x, kv_2), "fsdp", 1)
        qkv_pieces = [qkv_weight, qkv_c, qkv_x, qkv_xc]
        dq = lax.optimization_barrier((dq, gate_r.own, kv_early))[0]
    own = own_terms(w_rows, h1, dq, [kv_0, kv_1, kv_2, kv_3], shards, halves)
    if direct:
        own_r = Reduction(*own, line)
        up_r.arrived = after(up_r.arrived, own[0])
        down_r.arrived = after(down_r.arrived, own[0])
        output_r.arrived = after(output_r.arrived, own[0])
        own_r.core()
        up_r.halve(1)
        down_r.halve(1)
        own_r.across()
        gate_r.halve(4)
        up_r.halve(4)
        output_r.halve(2)
        gate_r.settle()
        gate_r.widen(4)
        own_r.settle()
        own_r.own = own_r.own[None]
        own_r.widen(4)
        up_r.settle()
        up_r.widen(4)
        output_r.halve(1)
        down_r.halve(2)
        gate_r.own = after(gate_r.own, late)
        gate_r.widen(2)
        own_r.widen(2)
        up_r.widen(1)
        output_r.halve(4)
        down_r.halve(4)
        gate_r.widen(1)
        own_r.widen(1)
        input_grad = last_stage(
            w_rows, dq_turned, [kv_early, kv_late], x, d_middle, gain_1, qkv_pieces
        )
        up_r.widen(2)
        output_r.settle()
        output_r.widen(4)
        down_r.settle()
        down_r.own = after(down_r.own, input_grad)
        down_r.widen(4)
        output_r.widen(1)
        down_r.widen(2)
        output_r.widen(2)
        down_r.widen(1)
        for r in (gate_r, up_r, down_r, output_r, own_r):
            r.join()
        gate_grad, up_grad, down_grad, output_grad = [
            r.own for r in (gate_r, up_r, down_r, output_r)
        ]
        all_shares = own_r.own.reshape(2, 2, 2, shard_rows, 3 * LANES)
        all_shares = all_shares.transpose(2, 1, 0, 3, 4)
    else:
        own_share = lax.psum_scatter(own[0][0], "fsdp", scatter_dimension=0, tiled=True)
        all_shares = lax.all_gather(own_share, "seq", axis=0)
        gate_grad, up_grad, down_grad, output_grad = [
            lax.psum(lax.psum_scatter(g[0][0], "fsdp", scatter_dimension=0, tiled=True), "seq")
            for g in (gg, ug, dg, og)
        ]
    all_shares = all_shares.reshape(slots, shard_rows, 3, LANES)[..., :own_width].astype(f32)
    query_grad, key_grad, value_grad = [
        all_shares[:, :, i, :].transpose(1, 0, 2).reshape(shard_rows, width) for i in range(3)
    ]
    if not direct:
        input_grad = last_stage(
            w_rows, dq_turned, [kv_early, kv_late], x, d_middle, gain_1, qkv_pieces
        )

    def gain_grad(terms, gain):
        summed = sum(jnp.sum(g * w.astype(f32), axis=1) for g, w in terms)
        return summed / gain.astype(f32)

    output_grad, gate_grad, up_grad, down_grad = [
        g.astype(f32) for g in (output_grad, gate_grad, up_grad, down_grad)
    ]
    attention_gain_grad = gain_grad(
        ((query_grad, query_weight), (key_grad, key_weight), (value_grad, value_weight)),
        attention_gain,
    )
    feedforward_gain_grad = gain_grad(
        ((gate_grad, gate_weight), (up_grad, up_weight)), feedforward_gain
    )
    return (
        layer_out[None],
        input_grad[None],
        query_grad,
        key_grad,
        value_grad,
        output_grad,
        gate_grad,
        up_grad,
        down_grad,
        attention_gain_grad,
        feedforward_gain_grad,
    )


def solution(mesh):
    in_specs = (
        P("fsdp", "seq", None),
        P("fsdp", "seq", None),
        P("fsdp", None),
        P("fsdp", None),
        P("fsdp", None),
        P("fsdp", None),
        P("fsdp", None),
        P("fsdp", None),
        P("fsdp", None),
        P("fsdp"),
        P("fsdp"),
        P("fsdp", None),
        P("fsdp", None),
        P("fsdp", None),
    )
    out_specs = (
        P("fsdp", "seq", None),
        P("fsdp", "seq", None),
        P("fsdp", None),
        P("fsdp", None),
        P("fsdp", None),
        P("fsdp", None),
        P("fsdp", None),
        P("fsdp", None),
        P("fsdp", None),
        P("fsdp"),
        P("fsdp"),
    )
    return jax.shard_map(
        on_device, mesh=mesh, in_specs=in_specs, out_specs=out_specs, check_vma=False
    )
```

```python
import functools

import jax
import jax.numpy as jnp
from jax import lax
from jax.experimental import pallas as pl
from jax.experimental.pallas import tpu as pltpu
from jax.sharding import PartitionSpec as P

HD = 64
LANES = 128
EPSILON = 1e-06
BLOCKED = -(2.0**100)
ROOT_2_PI = 0.7978845608028654
CUBIC = 0.044715
VMEM_LIMIT = 60 * 1024 * 1024

bf16 = jnp.bfloat16
f32 = jnp.float32


def mm(a, b):
    return jnp.dot(a, b, preferred_element_type=f32)


def mm_nt(a, b):
    return lax.dot_general(a, b, (((1,), (1,)), ((), ())), preferred_element_type=f32)


def mm_tn(a, b):
    return lax.dot_general(a, b, (((0,), (0,)), ((), ())), preferred_element_type=f32)


def params(**extra):
    return pltpu.CompilerParams(vmem_limit_bytes=VMEM_LIMIT, **extra)


def cost(flops, moved, transcendentals=0):
    return pl.CostEstimate(
        flops=int(flops), bytes_accessed=int(moved), transcendentals=int(transcendentals)
    )


def vmem():
    return pl.BlockSpec(memory_space=pltpu.VMEM)


def anywhere():
    return pl.BlockSpec(memory_space=pl.ANY)


def smem():
    return pl.BlockSpec(memory_space=pltpu.SMEM)


def lane_ids(rows):
    return lax.broadcasted_iota(jnp.int32, (rows, LANES), 1)


def split3(column):
    high = column.astype(bf16)
    rest = column - high.astype(f32)
    middle = rest.astype(bf16)
    low = (rest - middle.astype(f32)).astype(bf16)
    return (high.astype(f32), middle.astype(f32), low.astype(f32))


def project_kernel(heads, segments, layout, aliased, *refs):
    w_rows, x_ref = refs[1:3]
    arrays = 1 + max(array for array, _ in layout)
    w_refs = refs[3 : 3 + arrays]
    code_ref = refs[3 + arrays]
    qa_ref, ka_ref, va_ref, h1_ref, gain_row = refs[4 + arrays + aliased :]
    piece_rows = w_refs[0].shape[1]
    spans = []
    for piece, (array, index) in enumerate(layout):
        at = pl.ds(pl.multiple_of(w_rows[piece] * piece_rows, piece_rows), piece_rows)
        spans.append(at)
        columns = w_refs[array][index, :, 3 * LANES :].astype(f32)
        gain_row[:, at] = columns.T[0:8, :]
    x = x_ref[...].astype(f32)
    scaling = lax.rsqrt(jnp.mean(x * x, axis=-1, keepdims=True) + EPSILON)
    h1_ref[...] = (x * scaling * gain_row[0:1, :]).astype(bf16)
    qkv = None
    for at, (array, index) in zip(spans, layout):
        part = mm(h1_ref[:, at], w_refs[array][index, :, : 3 * LANES])
        qkv = part if qkv is None else qkv + part
    rows = x.shape[0]
    lane = lane_ids(rows)
    q = qkv[:, :LANES].astype(bf16) * jnp.asarray(HD**-0.5, bf16)
    k = qkv[:, LANES : 2 * LANES].astype(bf16)
    v = qkv[:, 2 * LANES :].astype(bf16)
    place = lane % HD
    code = code_ref[...]
    same = place == code // 2
    padded = code % 2 == 0
    q_table = jnp.where(same | ((place == HD - 1) & padded), 1.0, 0.0).astype(bf16)
    k_table = jnp.where(
        place < segments,
        jnp.where(same & ~padded, 0.0, BLOCKED),
        jnp.where((place >= HD - 4) & (place < HD - 1), 1.0, 0.0),
    ).astype(bf16)
    ones = jnp.where(place < 3, 1.0, 0.0).astype(bf16)
    for head in range(heads):
        own = lane // HD == head
        qa_ref[head] = jnp.where(own, q, q_table)
        ka_ref[head] = jnp.where(own, k, k_table)
        va_ref[head] = jnp.where(own, v, ones)


def project(slot, w_rows, slots, heads, segments, x, layout, arrays, codes, previous):
    rows, width = x.shape
    total = rows * slots
    head_spec = pl.BlockSpec((heads, rows, LANES), lambda i, s, w: (0, s[0], 0))
    shapes = [jax.ShapeDtypeStruct((heads, total, LANES), bf16)] * 3 + [
        jax.ShapeDtypeStruct((total, width), bf16)
    ]
    extra = () if previous is None else tuple(previous)
    first = 4 + len(arrays)
    return pl.pallas_call(
        functools.partial(project_kernel, heads, segments, layout, len(extra)),
        grid_spec=pltpu.PrefetchScalarGridSpec(
            num_scalar_prefetch=2,
            grid=(1,),
            in_specs=[pl.BlockSpec((rows, width), lambda i, s, w: (0, 0))]
            + [pl.BlockSpec(a.shape, lambda i, s, w: (0, 0, 0)) for a in arrays]
            + [pl.BlockSpec((rows, 1), lambda i, s, w: (s[0], 0))]
            + [anywhere()] * len(extra),
            out_specs=[head_spec] * 3 + [pl.BlockSpec((rows, width), lambda i, s, w: (s[0], 0))],
            scratch_shapes=[pltpu.VMEM((8, width), f32)],
        ),
        out_shape=shapes,
        input_output_aliases={first + i: i for i in range(len(extra))},
        compiler_params=params(),
        cost_estimate=cost(2 * rows * width * 3 * LANES, 4 * rows * width + 8 * LANES * width),
        name="project",
    )(slot, w_rows, x, *arrays, codes, *extra)


def forward_kernel(heads, q_ref, k_near, v_near, k_ref, v_ref, att_ref, sum_ref, qb_ref):
    pack, rows = q_ref.shape[1], q_ref.shape[3]
    span = pack * rows
    lane = lane_ids(span)
    merged = None
    for head in range(heads):
        q = q_ref[head].reshape(span, LANES)
        key = k_near[head].reshape(span, LANES)
        value = v_near[head].reshape(span, LANES)
        own = lane // HD == head
        other = HD if head == 0 else 0
        scores = mm_nt(q, k_ref[head])
        q_wide = q.astype(f32)
        padded = q_wide[:, other + HD - 1 : other + HD] > 0.5
        own_score = jnp.sum(jnp.where(own, q_wide * key.astype(f32), 0.0), axis=-1, keepdims=True)
        top = jnp.max(scores, axis=-1, keepdims=True)
        top = jnp.where(padded, jnp.maximum(top, own_score), top)
        weights = jnp.exp(scores - top).astype(bf16)
        mixed = mm(weights, v_ref[head])
        own_weight = jnp.where(padded, jnp.exp(own_score - top), 0.0).astype(bf16).astype(f32)
        mixed = mixed + own_weight * value.astype(f32)
        total = mixed[:, other : other + 1]
        log_total = top + jnp.log(total)
        mixed = mixed * (1.0 / total)
        merged = mixed if merged is None else jnp.where(own, mixed, merged)
        filled = q_wide
        for place, part in enumerate(split3(-log_total)):
            filled = jnp.where(lane == other + HD - 4 + place, part, filled)
        qb_ref[head] = filled.astype(bf16).reshape(pack, 1, rows, LANES)
    att_ref[...] = merged.astype(bf16).reshape(pack, rows, LANES)
    sum_ref[...] = merged.reshape(pack, 1, rows, LANES)


def forward_body(heads, aliased, *refs):
    forward_kernel(heads, *(refs[:5] + refs[5 + aliased :]))


def attend(qa, ka, va, part, parts, slots, span, previous):
    heads, total, _ = qa.shape
    rows = total // slots // parts
    pack = max(1, min(slots, 320 // rows))
    shape = (heads, slots, parts, rows, LANES)
    view = [a.reshape(shape) for a in (qa, ka, va)]
    begin = span[0] // pack
    block = pl.BlockSpec((heads, pack, 1, rows, LANES), lambda i: (0, begin + i, part, 0, 0))
    whole = pl.BlockSpec(ka.shape, lambda i: (0, 0, 0))
    extra = tuple(previous)
    return pl.pallas_call(
        functools.partial(forward_body, heads, len(extra)),
        grid=((span[1] - span[0]) // pack,),
        in_specs=[block, block, block, whole, whole] + [anywhere()] * len(extra),
        out_specs=[
            pl.BlockSpec((pack, rows, LANES), lambda i: (begin + i, 0, 0)),
            pl.BlockSpec((pack, 1, rows, LANES), lambda i: (begin + i, part, 0, 0)),
            block,
        ],
        out_shape=[
            jax.ShapeDtypeStruct((slots, rows, LANES), bf16),
            jax.ShapeDtypeStruct(shape[1:], f32),
            jax.ShapeDtypeStruct(shape, bf16),
        ],
        input_output_aliases={5 + i: 3 - len(extra) + i for i in range(len(extra))},
        compiler_params=params(),
        cost_estimate=cost(
            8 * heads * total * total * LANES // parts,
            4 * heads * total * LANES,
            heads * total * total // parts,
        ),
        name="attend",
    )(*view, ka, va, *extra)


def backward_kernel(heads, part, parts, tile, *refs):
    first, last = part == 0, part == parts - 1
    qb_ref, k_ref, v_ref = refs[:3]
    if first:
        sum_ref, grad_ref, kv_ref, dq_ref, gb_ref, dk_acc, dv_acc = refs[3:]
        dq_acc = dq_ref
    elif last:
        gb_ref, dq_in, kv_ref, dq_ref, dq_acc, dk_acc, dv_acc = refs[3:]
    else:
        gb_ref, dq_in, kv_ref, dq_ref, dk_acc, dv_acc = refs[3:]
        dq_acc = dq_ref
    slots, rows = k_ref.shape[1], k_ref.shape[3]
    total = qb_ref.shape[1]
    span = slots * rows
    pack = max(1, min(slots, 320 // rows))
    if first:
        block_rows = grad_ref.shape[1]
        lane = lane_ids(block_rows)

        def prepare(slot, carry):
            at = pl.ds(pl.multiple_of(slot * block_rows, block_rows), block_rows)
            grad = grad_ref[slot].astype(f32)
            product = grad * sum_ref[at, :]
            for head in range(heads):
                other = HD if head == 0 else 0
                own = lane // HD == head
                delta = jnp.sum(jnp.where(own, product, 0.0), axis=-1, keepdims=True)
                filled = jnp.where(own, grad, 0.0)
                for place, piece in enumerate(split3(-delta)):
                    filled = jnp.where(lane == other + place, piece, filled)
                gb_ref[head, at, :] = filled.astype(bf16)
                dq_acc[head, at, :] = jnp.zeros((block_rows, LANES), f32)
            return carry

        lax.fori_loop(0, slots, prepare, 0)
    else:
        dq_acc[...] = dq_in[...]
    width = pack * rows
    lane = lane_ids(width)
    for index in range(slots // pack):
        keys = slice(index * pack, (index + 1) * pack)
        dk_acc[...] = jnp.zeros_like(dk_acc)
        dv_acc[...] = jnp.zeros_like(dv_acc)

        def step(number, carry):
            at = pl.ds(pl.multiple_of(number * tile, tile), tile)
            for head in range(heads):
                key = k_ref[head, keys].reshape(width, LANES)
                value = v_ref[head, keys].reshape(width, LANES)
                q = qb_ref[head, at, :]
                g = gb_ref[head, at, :]
                weights = jnp.exp(mm_nt(key, q))
                inner = mm_nt(value, g)
                score_grad = (weights * inner).astype(bf16)
                dv_acc[head] += mm(weights.astype(bf16), g)
                dk_acc[head] += mm(score_grad, q)
                dq_acc[head, at, :] += mm_tn(score_grad, key)
            return carry

        lax.fori_loop(0, total // tile, step, 0)
        dk_all, dv_all = None, None
        for head in range(heads):
            other = HD if head == 0 else 0
            own = lane // HD == head
            counted = own | ((lane >= other + HD - 4) & (lane < other + HD - 1))
            starts = [
                slot * (total // slots) + part * rows
                for slot in range(index * pack, (index + 1) * pack)
            ]
            q = jnp.concatenate([qb_ref[head, b : b + rows, :] for b in starts], axis=0).astype(f32)
            g = jnp.concatenate([gb_ref[head, b : b + rows, :] for b in starts], axis=0).astype(f32)
            k = k_ref[head, keys].reshape(width, LANES).astype(f32)
            v = v_ref[head, keys].reshape(width, LANES).astype(f32)
            padded = q[:, other + HD - 1 : other + HD] > 0.5
            score = jnp.sum(jnp.where(counted, q * k, 0.0), axis=-1, keepdims=True)
            weight = jnp.where(padded, jnp.exp(score), 0.0)
            inner = jnp.sum(v * g, axis=-1, keepdims=True)
            score_grad = (weight * inner).astype(bf16).astype(f32)
            weight = weight.astype(bf16).astype(f32)
            dk = dk_acc[head] + score_grad * q
            dv = dv_acc[head] + weight * g
            dq = score_grad * k
            for place, b in enumerate(starts):
                dq_acc[head, b : b + rows, :] += dq[place * rows : (place + 1) * rows, :]
            dk_all = dk if head == 0 else jnp.where(own, dk, dk_all)
            dv_all = dv if head == 0 else jnp.where(own, dv, dv_all)
        kv_ref[keys, 0] = dk_all.astype(bf16).reshape(pack, rows, LANES)
        kv_ref[keys, 1] = dv_all.astype(bf16).reshape(pack, rows, LANES)
    if last:
        block_rows = total // slots
        lane = lane_ids(block_rows)
        for slot in range(slots):
            at = slice(slot * block_rows, (slot + 1) * block_rows)
            dq = dq_acc[0, at, :]
            if heads == 2:
                dq = jnp.where(lane < HD, dq, dq_acc[1, at, :])
            dq_ref[slot] = (dq * HD**-0.5).astype(bf16)


def attend_back(qb, ka, va, part, parts, slots, sums, grads, state):
    heads, total, _ = ka.shape
    rows = total // slots // parts
    first, last = part == 0, part == parts - 1
    shape = (heads, slots, parts, rows, LANES)
    near = pl.BlockSpec((heads, slots, 1, rows, LANES), lambda i: (0, 0, part, 0, 0))
    wide = pl.BlockSpec((heads, total, LANES), lambda i: (0, 0, 0))
    pack = max(1, min(slots, 320 // rows))
    accumulator = pltpu.VMEM((heads, pack * rows, LANES), f32)
    if first:
        inputs = [sums, grads]
        in_specs = [
            pl.BlockSpec((total, LANES), lambda i: (0, 0)),
            pl.BlockSpec(grads.shape, lambda i: (0, 0, 0)),
        ]
    else:
        inputs, in_specs = list(state), [wide, wide]
    out_shape = [jax.ShapeDtypeStruct((slots, 2, rows, LANES), bf16)]
    out_specs = [pl.BlockSpec((slots, 2, rows, LANES), lambda i: (0, 0, 0, 0))]
    scratch = [accumulator, accumulator]
    if last:
        out_shape.append(jax.ShapeDtypeStruct((slots, total // slots, LANES), bf16))
        out_specs.append(pl.BlockSpec((slots, total // slots, LANES), lambda i: (0, 0, 0)))
        scratch = [pltpu.VMEM((heads, total, LANES), f32)] + scratch
    else:
        out_shape.append(jax.ShapeDtypeStruct((heads, total, LANES), f32))
        out_specs.append(wide)
    if first:
        out_shape.append(jax.ShapeDtypeStruct((heads, total, LANES), bf16))
        out_specs.append(wide)
    return pl.pallas_call(
        functools.partial(backward_kernel, heads, part, parts, 512),
        grid=(1,),
        in_specs=[wide, near, near] + in_specs,
        out_specs=out_specs,
        out_shape=out_shape,
        scratch_shapes=scratch,
        compiler_params=params(),
        cost_estimate=cost(
            20 * heads * total * total * LANES // parts,
            12 * heads * total * LANES,
            heads * total * total // parts,
        ),
        name="attend_back",
    )(qb, ka.reshape(shape), va.reshape(shape), *inputs)


def own_kernel(halves, *refs):
    w_rows, h_ref, dq_ref = refs[:3]
    parts = len(refs) - 4 - halves
    kv_refs, outs, term = refs[3 : 3 + parts], refs[3 + parts : -1], refs[-1]
    slots, _, rows, width = h_ref.shape
    total = slots * parts * rows
    term[:, :LANES] = mm_tn(
        h_ref[...].reshape(total, width), dq_ref[...].reshape(total, LANES)
    ).astype(bf16)
    for kind in range(2):
        summed = None
        for part in range(parts):
            piece = mm_tn(
                h_ref[:, part].reshape(slots * rows, width),
                kv_refs[part][:, kind].reshape(slots * rows, LANES),
            )
            summed = piece if summed is None else summed + piece
        term[:, (kind + 1) * LANES : (kind + 2) * LANES] = summed.astype(bf16)
    place_rows(halves, w_rows, term, outs)


def place_rows(halves, w_rows, source, outs):
    inner, step_rows = outs[0].shape[0], outs[0].shape[1]
    for half in range(halves):
        for index in range(inner):
            piece = index * halves + half
            at = pl.ds(pl.multiple_of(w_rows[piece] * step_rows, step_rows), step_rows)
            outs[half][index] = source[at, :]


def own_terms(w_rows, h1, dq, kvs, shards, halves):
    slots, rows = kvs[0].shape[0], kvs[0].shape[2]
    width = h1.shape[1]
    pieces = shards if halves == 2 else 1
    shape = jax.ShapeDtypeStruct((pieces // halves, width // pieces, 3 * LANES), bf16)
    return pl.pallas_call(
        functools.partial(own_kernel, halves),
        in_specs=[smem()] + [vmem()] * (2 + len(kvs)),
        out_specs=[vmem()] * halves,
        out_shape=[shape] * halves,
        scratch_shapes=[pltpu.VMEM((width, 3 * LANES), bf16)],
        compiler_params=params(),
        cost_estimate=cost(2 * h1.size * 3 * LANES, 2 * h1.size),
        name="own_terms",
    )(w_rows, h1.reshape(slots, len(kvs), rows, width), dq, *kvs)


def load_rows(entries, sources, targets, sems, rows_of):
    started = [[] for _ in targets]
    for number, (target, source, index, place, step_rows, offset, column) in enumerate(entries):
        begin = pl.multiple_of(rows_of[index][place] * step_rows + offset, 16)
        at = pl.ds(begin, sources[source].shape[0])
        width = targets[target].shape[1]
        copy = pltpu.make_async_copy(
            sources[source].at[:, column : column + width],
            targets[target].at[at, :],
            sems.at[number],
        )
        copy.start()
        started[target].append(copy)
    return started


def store_rows(source, targets, sems, index, columns, shift=0):
    moved = columns if shift == 0 else pl.ds(shift + columns.start, columns.size)
    copies = []
    halves = len(targets)
    for piece in range(halves * targets[0].shape[0]):
        step_rows = targets[0].shape[1]
        at = pl.ds(pl.multiple_of(index[piece] * step_rows, step_rows), step_rows)
        target = targets[piece % halves].at[piece // halves, :, moved]
        copies.append(pltpu.make_async_copy(source.at[at, columns], target, sems.at[piece]))
    return copies


def pre_kernel(parts, entries, *refs):
    w_rows = refs[0]
    att_refs = refs[1 : 1 + parts]
    x_ref, gain_ref = refs[1 + parts : 3 + parts]
    sources = refs[3 + parts : -5]
    mid_ref, h2_ref, att_ref, wo, sems = refs[-5:]
    loads = load_rows(entries, sources, (wo,), sems, (w_rows,))
    rows, width = x_ref.shape
    blocks = att_refs[0].shape[0]
    block_width = width // blocks
    part_rows = rows // parts
    for part in range(parts):
        for block in range(blocks):
            att_ref[
                part * part_rows : (part + 1) * part_rows,
                block * block_width : (block + 1) * block_width,
            ] = att_refs[part][block][:, :block_width]
    for copy in loads[0]:
        copy.wait()
    middle = x_ref[...].astype(f32) + mm(att_ref[...], wo[...])
    scaling = lax.rsqrt(jnp.mean(middle * middle, axis=-1, keepdims=True) + EPSILON)
    h2_ref[...] = (middle * scaling * gain_ref[...].astype(f32)).astype(bf16)
    mid_ref[...] = middle


def pre_stage(w_rows, att_parts, x, gain, entries, sources):
    rows, width = x.shape
    hbm = pl.BlockSpec(memory_space=pltpu.HBM)
    return pl.pallas_call(
        functools.partial(pre_kernel, len(att_parts), entries),
        in_specs=[smem()] + [vmem()] * (len(att_parts) + 2) + [hbm] * len(sources),
        out_specs=[vmem()] * 3,
        out_shape=[
            jax.ShapeDtypeStruct((rows, width), f32),
            jax.ShapeDtypeStruct((rows, width), bf16),
            jax.ShapeDtypeStruct((rows, width), bf16),
        ],
        scratch_shapes=[
            pltpu.VMEM((width, width), bf16),
            pltpu.SemaphoreType.DMA((len(entries),)),
        ],
        compiler_params=params(),
        cost_estimate=cost(2 * rows * width * width, 2 * width * width),
        name="pre_stage",
    )(w_rows, *att_parts, x, gain, *sources)


def main_kernel(groups, halves, entries, count, *refs):
    w_rows, d_rows = refs[:2]
    h2_refs, c_refs = refs[2 : 2 + groups], refs[2 + groups : 2 + 2 * groups]
    refs = refs[2 + 2 * groups :]
    sources, refs = refs[:count], refs[count:]
    out_refs, back_refs = refs[:groups], refs[groups : 2 * groups]
    refs = refs[2 * groups :]
    gu_refs, dg_refs = refs[:halves], refs[halves : 2 * halves]
    refs = refs[2 * halves :]
    wg, wu, wd, gg, ug, dg, h2_all, h2t, c_all, acc_out, acc_back, in_sems, out_sems = refs
    loads = load_rows(entries, sources, (wg, wu, wd), in_sems, (w_rows, d_rows))
    rows = h2_refs[0].shape[0]
    for group in range(groups):
        span = slice(group * rows, (group + 1) * rows)
        h2_all[span, :] = h2_refs[group][...]
        c_all[span, :] = c_refs[group][...]
    h2t[...] = h2_all[...].T
    acc_out[...] = jnp.zeros_like(acc_out)
    acc_back[...] = jnp.zeros_like(acc_back)
    for started in loads:
        for copy in started:
            copy.wait()

    def columns_at(at):
        h2 = h2_all[...]
        c = c_all[...]
        gate = mm(h2, wg[:, at])
        up = mm(h2, wu[:, at])
        act_grad = mm_nt(c, wd[at, :])
        square = gate * gate
        bend = jnp.tanh(gate * (ROOT_2_PI + (ROOT_2_PI * CUBIC) * square))
        half = 0.5 * (1.0 + bend)
        curve = gate * half
        slope = half + (0.5 * gate) * (1.0 - bend * bend) * (
            ROOT_2_PI + (3.0 * ROOT_2_PI * CUBIC) * square
        )
        act = (curve * up).astype(bf16)
        d_up = (act_grad * curve).astype(bf16)
        d_gate = (act_grad * up * slope).astype(bf16)
        acc_back[...] += mm_nt(d_gate, wg[:, at]) + mm_nt(d_up, wu[:, at])
        gg[:, at] = mm(h2t[...], d_gate).astype(bf16)
        ug[:, at] = mm(h2t[...], d_up).astype(bf16)
        dg[at, :] = mm_tn(act, c).astype(bf16)
        acc_out[...] += mm(act, wd[at, :])
        for kind, source in ((0, gg), (1, ug)):
            for copy in store_rows(source, gu_refs, out_sems.at[kind], w_rows, at, kind * width):
                copy.start()

    width = wg.shape[1]
    step_width = 256
    whole = width // step_width

    def column_step(number, carry):
        columns_at(pl.ds(pl.multiple_of(number * step_width, step_width), step_width))
        return carry

    lax.fori_loop(0, whole, column_step, 0)
    if width % step_width:
        columns_at(pl.ds(whole * step_width, width % step_width))
    everything = slice(None)
    stores = store_rows(dg, dg_refs, out_sems.at[2], d_rows, everything)
    for copy in stores:
        copy.start()
    for group in range(groups):
        span = slice(group * rows, (group + 1) * rows)
        kind = out_refs[group].dtype
        out_refs[group][...] = acc_out[span, :].astype(kind)
        back_refs[group][...] = acc_back[span, :].astype(kind)
    whole = pl.ds(0, width)
    stores += store_rows(gg, gu_refs, out_sems.at[0], w_rows, whole)
    stores += store_rows(ug, gu_refs, out_sems.at[1], w_rows, whole, width)
    for copy in stores:
        copy.wait()


def main_stage(w_rows, d_rows, h2s, cs, hidden, entries, sources, halves):
    groups = len(h2s)
    rows, width = h2s[0].shape
    pieces, d_pieces = w_rows.shape[0], d_rows.shape[0]
    hbm = pl.BlockSpec(memory_space=pltpu.HBM)
    partial = [jax.ShapeDtypeStruct((rows, width), f32 if g == 0 else bf16) for g in range(groups)]
    up_shape = jax.ShapeDtypeStruct((pieces // halves, width // pieces, 2 * hidden), bf16)
    down_shape = jax.ShapeDtypeStruct((d_pieces // halves, hidden // d_pieces, width), bf16)
    total = groups * rows
    out = pl.pallas_call(
        functools.partial(main_kernel, groups, halves, entries, len(sources)),
        in_specs=[smem(), smem()] + [vmem()] * (2 * groups) + [hbm] * len(sources),
        out_specs=[vmem()] * (2 * groups) + [hbm] * (2 * halves),
        out_shape=partial * 2 + [up_shape] * halves + [down_shape] * halves,
        scratch_shapes=[
            pltpu.VMEM((width, hidden), bf16),
            pltpu.VMEM((width, hidden), bf16),
            pltpu.VMEM((hidden, width), bf16),
            pltpu.VMEM((width, hidden), bf16),
            pltpu.VMEM((width, hidden), bf16),
            pltpu.VMEM((hidden, width), bf16),
            pltpu.VMEM((total, width), bf16),
            pltpu.VMEM((width, total), bf16),
            pltpu.VMEM((total, width), bf16),
            pltpu.VMEM((total, width), f32),
            pltpu.VMEM((total, width), f32),
            pltpu.SemaphoreType.DMA((len(entries),)),
            pltpu.SemaphoreType.DMA((3, max(pieces, d_pieces))),
        ],
        compiler_params=params(),
        cost_estimate=cost(18 * total * width * hidden, 12 * width * hidden),
        name="main_stage",
    )(w_rows, d_rows, *h2s, *cs, *sources)
    outs, backs, grads = list(out[:groups]), list(out[groups : 2 * groups]), out[2 * groups :]
    return (outs, backs, grads[:halves], grads[halves:])


def post_kernel(groups, entries, count, *refs):
    w_rows, mid_ref = refs[:2]
    backs, refs = refs[2 : 2 + groups], refs[2 + groups :]
    c_ref, gain_ref = refs[:2]
    sources, refs = refs[2 : 2 + count], refs[2 + count :]
    dmid_ref, branch_ref, da_ref, wo, in_sems = refs
    loads = load_rows(entries, sources, (wo,), in_sems, (w_rows,))
    middle = mid_ref[...]
    scaling = lax.rsqrt(jnp.mean(middle * middle, axis=-1, keepdims=True) + EPSILON)
    incoming = sum(ref[...].astype(f32) for ref in backs) * gain_ref[...].astype(f32)
    centre = jnp.mean(incoming * middle, axis=-1, keepdims=True)
    d_middle = (
        c_ref[...].astype(f32)
        + scaling * incoming
        - middle * (scaling * scaling * scaling * centre)
    )
    dmid_ref[...] = d_middle
    branch = d_middle.astype(bf16)
    branch_ref[...] = branch
    for copy in loads[0]:
        copy.wait()
    d_att = mm_nt(branch, wo[...]).astype(bf16)
    blocks = da_ref.shape[0]
    block_width = d_att.shape[1] // blocks
    for block in range(blocks):
        piece = d_att[:, block * block_width : (block + 1) * block_width]
        if block_width < LANES:
            piece = jnp.concatenate([piece] * (LANES // block_width), axis=1)
        da_ref[block] = piece


def post_stage(w_rows, middle, backs, c, gain, slots, entries, sources):
    groups = len(backs)
    rows, width = middle.shape
    hbm = pl.BlockSpec(memory_space=pltpu.HBM)
    return pl.pallas_call(
        functools.partial(post_kernel, groups, entries, len(sources)),
        in_specs=[smem()] + [vmem()] * (3 + groups) + [hbm] * len(sources),
        out_specs=[vmem()] * 3,
        out_shape=[
            jax.ShapeDtypeStruct((rows, width), f32),
            jax.ShapeDtypeStruct((rows, width), bf16),
            jax.ShapeDtypeStruct((slots, rows, LANES), bf16),
        ],
        scratch_shapes=[
            pltpu.VMEM((width, width), bf16),
            pltpu.SemaphoreType.DMA((len(entries),)),
        ],
        compiler_params=params(),
        cost_estimate=cost(2 * rows * width * width, 4 * width * width),
        name="post_stage",
    )(w_rows, middle, *backs, c, gain, *sources)


def out_kernel(halves, w_rows, att_ref, branch_ref, *refs):
    og, sems = refs[halves:]
    og[...] = mm_tn(att_ref[...], branch_ref[...]).astype(bf16)
    stores = store_rows(og, refs[:halves], sems, w_rows, slice(None))
    for copy in stores:
        copy.start()
    for copy in stores:
        copy.wait()


def out_terms(w_rows, att, branch, halves):
    rows, width = att.shape
    pieces = w_rows.shape[0]
    hbm = pl.BlockSpec(memory_space=pltpu.HBM)
    shape = jax.ShapeDtypeStruct((pieces // halves, width // pieces, width), bf16)
    return pl.pallas_call(
        functools.partial(out_kernel, halves),
        in_specs=[smem(), vmem(), vmem()],
        out_specs=[hbm] * halves,
        out_shape=[shape] * halves,
        scratch_shapes=[pltpu.VMEM((width, width), bf16), pltpu.SemaphoreType.DMA((pieces,))],
        compiler_params=params(),
        cost_estimate=cost(2 * rows * width * width, 4 * width * width),
        name="out_terms",
    )(w_rows, att, branch)


def last_kernel(parts, pieces, *refs):
    w_rows, dq_ref = refs[:2]
    kv_refs = refs[2 : 2 + parts]
    x_ref, dmid_ref, gain_ref = refs[2 + parts : 5 + parts]
    weight_refs = refs[5 + parts : 5 + parts + pieces]
    out_ref, grad, total = refs[5 + parts + pieces :]
    rows, width = x_ref.shape
    blocks = dq_ref.shape[0]
    block_width = width // blocks
    piece_width = width // pieces
    done = 0
    for part in range(parts):
        part_rows = kv_refs[part].shape[2]
        for block in range(blocks):
            lanes = slice(block * block_width, (block + 1) * block_width)
            for kind in range(2):
                grad[kind + 1, done : done + part_rows, lanes] = kv_refs[part][block, kind][
                    :, :block_width
                ]
        done += part_rows
    for block in range(blocks):
        lanes = slice(block * block_width, (block + 1) * block_width)
        grad[0, :, lanes] = dq_ref[block][:, :block_width]
    for piece in range(pieces):
        at = pl.ds(pl.multiple_of(w_rows[piece] * piece_width, piece_width), piece_width)
        w = weight_refs[piece]
        total[:, at] = (
            mm_nt(grad[0], w[:, :width])
            + mm_nt(grad[1], w[:, width : 2 * width])
            + mm_nt(grad[2], w[:, 2 * width :])
        )
    x = x_ref[...].astype(f32)
    scaling = lax.rsqrt(jnp.mean(x * x, axis=-1, keepdims=True) + EPSILON)
    incoming = total[...] * gain_ref[...].astype(f32)
    centre = jnp.mean(incoming * x, axis=-1, keepdims=True)
    out_ref[...] = dmid_ref[...] + scaling * incoming - x * (scaling * scaling * scaling * centre)


def last_stage(w_rows, dq, kvs, x, d_middle, gain, weights):
    rows, width = x.shape
    return pl.pallas_call(
        functools.partial(last_kernel, len(kvs), len(weights)),
        in_specs=[smem()] + [vmem()] * (4 + len(kvs) + len(weights)),
        out_specs=vmem(),
        out_shape=jax.ShapeDtypeStruct((rows, width), f32),
        scratch_shapes=[pltpu.VMEM((3, rows, width), bf16), pltpu.VMEM((rows, width), f32)],
        compiler_params=params(),
        cost_estimate=cost(6 * rows * width * width, 6 * width * width),
        name="last_stage",
    )(w_rows, dq, *kvs, x, d_middle, gain, *weights)


def finish_kernel(mine_ref, own_ref, other_ref, w_ref, gain_ref, *outs):
    width = outs[0].shape[1]
    mine = mine_ref[0]
    for source, bit in ((own_ref, mine), (other_ref, 1 - mine)):
        for index in range(4):
            slot = (index % 2) * 4 + bit * 2 + index // 2
            at = pl.ds(pl.multiple_of(slot * LANES, LANES), LANES)
            for kind in range(3):
                outs[kind][:, at] = source[index, :, kind * LANES : (kind + 1) * LANES].astype(f32)
    total = None
    for kind in range(3):
        weight = w_ref[:, kind * width : (kind + 1) * width].astype(f32)
        part = jnp.sum(outs[kind][...] * weight, axis=-1, keepdims=True)
        total = part if total is None else total + part
    outs[3][...] = total / gain_ref[...].astype(f32)


def finish_own(mine, own, other, weights, gain):
    rows, width = own.shape[1], weights.shape[1] // 3
    return pl.pallas_call(
        finish_kernel,
        in_specs=[smem()] + [vmem()] * 4,
        out_specs=[vmem()] * 4,
        out_shape=[jax.ShapeDtypeStruct((rows, width), f32)] * 3
        + [jax.ShapeDtypeStruct((rows, 1), f32)],
        compiler_params=params(),
        cost_estimate=cost(6 * rows * width, 20 * rows * width),
        name="finish_own",
    )(mine, own, other, weights, gain)


def flip(values, axis, delta):
    count = lax.axis_size(axis)
    return lax.ppermute(values, axis, [(i, i ^ delta) for i in range(count)])


def after(values, *others):
    return lax.optimization_barrier((values, *others))[0]


def bits_of(count):
    return [1 << i for i in range(count.bit_length() - 1)]


def add_low(a, b):
    return (a.astype(f32) + b.astype(f32)).astype(bf16)


def cut(values, start, size):
    return lax.dynamic_slice_in_dim(values, start, size, axis=-2)


class Line:
    def __init__(self):
        self.last = None

    def hold(self, values):
        if self.last is not None:
            values = after(values, self.last)
        self.last = values
        return values


class Reduction:
    def __init__(self, kept, given, line):
        self.own, self.given, self.line, self.joined = kept, given, line, None

    def core(self):
        self.arrived = flip(self.line.hold(self.given), "fsdp", 1)

    def hold(self, *others):
        self.arrived = lax.optimization_barrier((self.arrived, *others))[0]

    def across(self):
        given = self.line.hold(add_low(self.own[1], self.arrived[1]))
        self.own = add_low(self.own[0], self.arrived[0])
        self.arrived = flip(given, "fsdp", 2)

    def halve(self, bit):
        place = lax.axis_index("seq")
        half = self.own.shape[-2] // 2
        mine = (place // bit) % 2
        keep, give = mine * half, (1 - mine) * half
        given = add_low(cut(self.own, give, half), cut(self.arrived, give, half))
        kept = add_low(cut(self.own, keep, half), cut(self.arrived, keep, half))
        self.own, self.arrived = kept, flip(self.line.hold(given), "seq", bit)

    def settle(self):
        self.own = add_low(self.own, self.arrived)

    def swap_columns(self):
        self.settle()
        self.arrived = flip(self.line.hold(self.own[1]), "fsdp", 2)

    def join_columns(self):
        upper = (lax.axis_index("fsdp") // 2) == 1
        width = self.arrived.shape[-1] // 2
        parts = []
        for kind in range(2):
            here = self.own[0, :, kind * width : (kind + 1) * width]
            there = self.arrived[:, kind * width : (kind + 1) * width]
            parts += [jnp.where(upper, there, here), jnp.where(upper, here, there)]
        self.own = jnp.concatenate(parts, axis=-1)

    def widen(self, bit):
        self.join()
        self.own = self.line.hold(self.own)
        self.arrived, self.joined = flip(self.own, "seq", bit), bit

    def join(self):
        if self.joined is None:
            return
        upper = ((lax.axis_index("seq") // self.joined) % 2) == 1
        first = jnp.where(upper, self.arrived, self.own)
        second = jnp.where(upper, self.own, self.arrived)
        self.own, self.joined = jnp.concatenate([first, second], axis=0), None


def token_codes(lengths_row, order_row, real_row):
    total = order_row.shape[0]
    ends_at = jnp.cumsum(lengths_row)
    positions = jnp.arange(total, dtype=jnp.int32)
    packed_segment = jnp.sum((positions[:, None] >= ends_at[None, :]).astype(jnp.int32), axis=1)
    packed_code = packed_segment * 2 + (real_row > 0).astype(jnp.int32)
    return jnp.sum(
        jnp.where(positions[:, None] == order_row[None, :], packed_code[None, :], 0), axis=1
    ).reshape(total, 1)


def move_chain(array, pairs):
    return lax.ppermute(
        array, "seq", [(a * 2 + low, b * 2 + low) for a, b in pairs for low in range(2)]
    )


def turn(blocks):
    return lax.all_to_all(blocks, "seq", split_axis=0, concat_axis=0, tiled=True)


def on_device(
    tokens,
    cotangent,
    query_weight,
    key_weight,
    value_weight,
    output_weight,
    gate_weight,
    up_weight,
    down_weight,
    attention_gain,
    feedforward_gain,
    lengths,
    token_order,
    real_token,
):
    x, c = tokens[0], cotangent[0]
    rows, width = x.shape
    slots = lax.axis_size("seq")
    shards = lax.axis_size("fsdp")
    seq, shard = lax.axis_index("seq"), lax.axis_index("fsdp")
    direct = slots == 8 and shards == 4
    heads = width // slots // HD
    own_width = heads * HD
    shard_rows = width // shards
    halves = 2 if direct else 1

    own_columns = [
        lax.dynamic_slice_in_dim(w, seq * own_width, own_width, axis=1)
        for w in (query_weight, key_weight, value_weight)
    ]
    gains = jnp.stack([attention_gain, feedforward_gain], axis=1)
    own_columns = jnp.concatenate(
        [jnp.pad(w, ((0, 0), (0, LANES - own_width))) for w in own_columns]
        + [jnp.pad(gains, ((0, 0), (0, LANES - 2)))],
        axis=1,
    )
    qkv_weight = jnp.concatenate([query_weight, key_weight, value_weight], axis=1)

    if direct:
        w_rows = shard ^ jnp.arange(shards, dtype=jnp.int32)
        place = seq // 2
        half = shard_rows // 2
        hidden = gate_weight.shape[1] // 2
        columns_x = flip(own_columns, "fsdp", 2)
        beside = flip(x, "seq", 1)
        near = move_chain(x, [(0, 1), (1, 0), (2, 3), (3, 2)])
        inner = move_chain(x, [(1, 2), (2, 1)])
        output_x = flip(output_weight, "fsdp", 2)
        both = jnp.stack([own_columns, columns_x])
        both_c = flip(both, "fsdp", 1)
        column_arrays = [both, both_c]
        column_layout = ((0, 0), (1, 0), (0, 1), (1, 1))
        near, inner, _ = lax.optimization_barrier((near, inner, beside))
        far_inner = move_chain(near, [(1, 2), (2, 1)])
        far_outer = move_chain(inner, [(1, 0), (2, 3)])
        near_beside = flip(near, "seq", 1)
        far_half = (1 - shard // 2) * hidden
        near_half = (shard // 2) * hidden
        up_own, up_sent = [
            jnp.concatenate(
                [
                    lax.dynamic_slice_in_dim(after(w, own_columns), start, hidden, axis=1)
                    for w in (gate_weight, up_weight)
                ],
                axis=1,
            )
            for start in (near_half, far_half)
        ]
        up_x1 = flip(after(up_sent[:half], near), "fsdp", 2)
        token_order = after(token_order, near)
        is_inner = (place == 1) | (place == 2)
        block_slots = [seq ^ d for d in range(slots)]
    else:
        w_rows = jnp.zeros((1,), jnp.int32)
        column_arrays = [lax.all_gather(own_columns, "fsdp", axis=0, tiled=True)[None]]
        column_layout = ((0, 0),)
        gathered = lax.all_gather(x, "seq", axis=0)
        x_blocks = [gathered[i] for i in range(slots)]
        block_slots = [jnp.asarray(i, jnp.int32) for i in range(slots)]

    codes = token_codes(lengths[0], token_order[0], real_token[0])
    gain_pieces = jnp.stack(
        [column_arrays[a][i, :, 3 * LANES : 3 * LANES + 2] for a, i in column_layout]
    )
    gain_rows = jnp.take(gain_pieces, w_rows, axis=0).reshape(width, 2)
    gain_1, gain_2 = gain_rows[:, 0].reshape(1, width), gain_rows[:, 1].reshape(1, width)
    state = None

    def project_block(number, block, state):
        slot = block_slots[number].reshape(1).astype(jnp.int32)
        return project(
            slot,
            w_rows,
            slots,
            heads,
            lengths.shape[1],
            block,
            column_layout,
            column_arrays,
            codes,
            state,
        )

    if direct:
        state = project_block(0, x, state)
        state = project_block(1, beside, state)
        far_inner, far_outer, _, _, _, _ = lax.optimization_barrier(
            (far_inner, far_outer, near_beside, up_x1, output_x, state[0])
        )
        third = move_chain(far_inner, [(1, 0), (2, 3)])
        far = jnp.where(is_inner, far_inner, far_outer)
        far_beside = flip(far, "seq", 1)
        up_x2 = flip(after(up_sent[half:], far_inner), "fsdp", 2)
        up_c = flip(after(up_own, far_inner), "fsdp", 1)
        state = project_block(2, near, state)
        state = project_block(3, near_beside, state)
        state = project_block(4, far, state)
        third, _, _, _, _ = lax.optimization_barrier(
            (third, far_beside, up_x2, up_c, state[0])
        )
        cross = jnp.where(is_inner, inner, third)
        cross_beside = flip(cross, "seq", 1)
        c_x = flip(after(c, cross), "fsdp", 2)
        up_xc1 = flip(after(up_x1, cross), "fsdp", 1)
        down_c = flip(after(down_weight, cross), "fsdp", 1)
        state = project_block(5, far_beside, state)
        state = project_block(6, cross, state)
        cross_beside, _, _, _ = lax.optimization_barrier((cross_beside, c_x, up_xc1, down_c))
        state = project_block(7, cross_beside, state)
    else:
        for number, block in enumerate(x_blocks):
            state = project_block(number, block, state)
    qa, ka, va, h1 = state

    att_first, sums, qb = attend(qa, ka, va, 0, 2, slots, (0, slots), ())
    middle_slot = slots // 2
    if direct:
        qkv_x = flip(after(qkv_weight, qa), "fsdp", 2)
        up_xc2 = flip(after(up_x2, qa), "fsdp", 1)
        output_c = flip(after(output_weight, qa), "fsdp", 1)
        output_xc = flip(after(output_x, qa), "fsdp", 1)
        qb, _, _, _ = lax.optimization_barrier((qb, up_xc2, output_c, output_xc))
    att_turned = turn(att_first)
    att_second, sums, qb = attend(
        qa, ka, va, 1, 2, slots, (0, middle_slot), (sums, qb)
    )
    if direct:
        qb, _, _ = lax.optimization_barrier((qb, att_turned, qkv_x))
    att_second, sums, qb = attend(
        qa, ka, va, 1, 2, slots, (middle_slot, slots), (att_second, sums, qb)
    )
    if direct:
        output_pieces = [output_weight, output_c, output_x, output_xc]
        output_entries = [(0, p, 0, p, shard_rows, 0, 0) for p in range(4)]
        d_rows = (shard % 2) ^ jnp.arange(2, dtype=jnp.int32)
        ff_sources = [up_own, up_c, up_x1, up_x2, up_xc1, up_xc2, down_weight, down_c]
        ff_entries = [
            (kind, source, 0, place, shard_rows, offset, kind * hidden)
            for kind in range(2)
            for source, place, offset in (
                (0, 0, 0), (1, 1, 0), (2, 2, 0), (3, 2, half), (4, 3, 0), (5, 3, half),
            )
        ] + [(2, 6, 1, 0, down_weight.shape[0], 0, 0), (2, 7, 1, 1, down_weight.shape[0], 0, 0)]
    else:
        output_pieces = [lax.all_gather(output_weight, "fsdp", axis=0, tiled=True)]
        output_entries = [(0, 0, 0, 0, width, 0, 0)]
        d_rows = w_rows
        ff_sources = [
            lax.all_gather(w, "fsdp", axis=0, tiled=True)
            for w in (gate_weight, up_weight, down_weight)
        ]
        hidden = gate_weight.shape[1]
        ff_entries = [(i, i, 0, 0, width, 0, 0) for i in range(3)]
    att_parts = [att_turned, turn(att_second)]
    total = rows * slots
    sums = sums.reshape(total, LANES)
    qb = qb.reshape(heads, total, LANES)

    middle, h2, att = pre_stage(w_rows, att_parts, x, gain_2, output_entries, output_pieces)
    if direct:
        h2s, cs = [h2, flip(h2, "fsdp", 2)], [c, c_x]
    else:
        h2s, cs = [h2], [c]
    outs, backs, gu, dg = main_stage(
        w_rows, d_rows, h2s, cs, hidden, ff_entries, ff_sources, halves
    )
    if direct:
        line = Line()
        backs[1] = flip(backs[1], "fsdp", 2)
        up_r = Reduction(*gu, line)
        down_r = Reduction(dg[0][0], dg[1][0], line)
        up_r.core()
        down_r.core()
        up_r.halve(1)
        down_r.halve(2)
        backs[1] = lax.optimization_barrier((backs[1], up_r.own, down_r.own))[0]
    d_middle, branch, d_att = post_stage(
        w_rows, middle, backs, c, gain_2, slots, output_entries, output_pieces
    )
    og = out_terms(w_rows, att, branch, halves)
    grad_blocks = turn(d_att)
    parts = 4
    back = functools.partial(attend_back, qb, ka, va)
    if direct:
        qkv_c = flip(after(qkv_weight, d_att), "fsdp", 1)
        output_r = Reduction(*og, line)
        down_r.hold(d_att)
        down_r.halve(1)
        output_r.core()
        up_r.hold(d_att)
        up_r.halve(2)
        grad_blocks = lax.optimization_barrier(
            (grad_blocks, down_r.own, up_r.own, qkv_c)
        )[0]
    else:
        qkv_pieces = [lax.all_gather(qkv_weight, "fsdp", axis=0, tiled=True)]
    kv_0, dq, gb = back(0, parts, slots, sums, grad_blocks, None)
    if direct:
        for r in (down_r, up_r, output_r):
            r.hold(kv_0)
        down_r.halve(4)
        up_r.halve(4)
        output_r.across()
        outs[1] = flip(after(outs[1], kv_0), "fsdp", 2)
        qkv_xc = flip(after(qkv_x, kv_0), "fsdp", 1)
        qkv_pieces = [qkv_weight, qkv_c, qkv_x, qkv_xc]
        gb = lax.optimization_barrier((gb, down_r.own, up_r.own, output_r.own))[0]
    kv_1, dq = back(1, parts, slots, None, None, (gb, dq))
    kv_early = turn(jnp.concatenate([kv_0, kv_1], axis=2))
    if direct:
        for r in (down_r, up_r, output_r):
            r.hold(kv_1)
        up_r.swap_columns()
        down_r.settle()
        down_r.widen(4)
        output_r.halve(2)
        gb = lax.optimization_barrier((gb, down_r.own, up_r.own, output_r.own, qkv_xc, outs[1]))[0]
    kv_2, dq = back(2, parts, slots, None, None, (gb, dq))
    if direct:
        for r in (down_r, up_r, output_r):
            r.hold(kv_2)
        up_r.join_columns()
        up_r.widen(4)
        down_r.widen(1)
        output_r.halve(1)
        gb = lax.optimization_barrier((gb, down_r.own, up_r.own, output_r.own))[0]
    kv_3, dq = back(3, parts, slots, None, None, (gb, dq))
    kv_late = jnp.concatenate([kv_2, kv_3], axis=2)
    late = turn(jnp.concatenate([kv_late.reshape(slots, rows, LANES), dq], axis=1))
    kv_late = late[:, :rows].reshape(kv_late.shape)
    dq_turned = late[:, rows:]
    if direct:
        for r in (down_r, up_r, output_r):
            r.hold(kv_3)
        up_r.widen(2)
        down_r.widen(2)
        output_r.halve(4)
        dq = lax.optimization_barrier((dq, down_r.own, up_r.own, output_r.own, kv_early))[0]
    layer_out = (middle + sum(part.astype(f32) for part in outs)).astype(bf16)
    own = own_terms(w_rows, h1, dq, [kv_0, kv_1, kv_2, kv_3], shards, halves)
    if direct:
        own_r = Reduction(*own, line)
        own_r.core()
        for r in (up_r, output_r):
            r.hold(own[0])
        up_r.widen(1)
        output_r.settle()
        output_r.widen(4)
        own_r.across()
        output_r.widen(1)
        own_r.settle()
        own_r.own = after(own_r.own[None], down_r.arrived)
        own_r.widen(4)
        output_r.widen(2)
        own_r.widen(1)
        own_r.arrived = after(own_r.arrived, late)
        own_r.widen(2)
        input_grad = last_stage(
            w_rows, dq_turned, [kv_early, kv_late], x, d_middle, gain_1, qkv_pieces
        )
        for r in (up_r, down_r, output_r):
            r.join()
        gate_grad, up_grad = up_r.own[:, : 2 * hidden], up_r.own[:, 2 * hidden :]
        down_grad, output_grad = down_r.own, output_r.own
        query_grad, key_grad, value_grad, attention_gain_grad = finish_own(
            ((seq // 2) % 2).reshape(1).astype(jnp.int32),
            own_r.own,
            own_r.arrived,
            qkv_weight,
            attention_gain.reshape(shard_rows, 1),
        )
        attention_gain_grad = attention_gain_grad.reshape(shard_rows)
    else:
        own_share = lax.psum_scatter(own[0][0], "fsdp", scatter_dimension=0, tiled=True)
        all_shares = lax.all_gather(own_share, "seq", axis=0)
        gate_grad, up_grad, down_grad, output_grad = [
            lax.psum(lax.psum_scatter(g, "fsdp", scatter_dimension=0, tiled=True), "seq")
            for g in (gu[0][0, :, :hidden], gu[0][0, :, hidden:], dg[0][0], og[0][0])
        ]
    def gain_grad(terms, gain):
        summed = sum(jnp.sum(g * w.astype(f32), axis=1) for g, w in terms)
        return summed / gain.astype(f32)

    if not direct:
        all_shares = all_shares.reshape(slots, shard_rows, 3, LANES)[..., :own_width].astype(f32)
        query_grad, key_grad, value_grad = [
            all_shares[:, :, i, :].transpose(1, 0, 2).reshape(shard_rows, width) for i in range(3)
        ]
        input_grad = last_stage(
            w_rows, dq_turned, [kv_early, kv_late], x, d_middle, gain_1, qkv_pieces
        )
        attention_gain_grad = gain_grad(
            ((query_grad, query_weight), (key_grad, key_weight), (value_grad, value_weight)),
            attention_gain,
        )
    output_grad, gate_grad, up_grad, down_grad = [
        g.astype(f32) for g in (output_grad, gate_grad, up_grad, down_grad)
    ]
    feedforward_gain_grad = gain_grad(
        ((gate_grad, gate_weight), (up_grad, up_weight)), feedforward_gain
    )
    return (
        layer_out[None],
        input_grad[None],
        query_grad,
        key_grad,
        value_grad,
        output_grad,
        gate_grad,
        up_grad,
        down_grad,
        attention_gain_grad,
        feedforward_gain_grad,
    )


def solution(mesh):
    in_specs = (
        P("fsdp", "seq", None),
        P("fsdp", "seq", None),
        P("fsdp", None),
        P("fsdp", None),
        P("fsdp", None),
        P("fsdp", None),
        P("fsdp", None),
        P("fsdp", None),
        P("fsdp", None),
        P("fsdp"),
        P("fsdp"),
        P("fsdp", None),
        P("fsdp", None),
        P("fsdp", None),
    )
    out_specs = (
        P("fsdp", "seq", None),
        P("fsdp", "seq", None),
        P("fsdp", None),
        P("fsdp", None),
        P("fsdp", None),
        P("fsdp", None),
        P("fsdp", None),
        P("fsdp", None),
        P("fsdp", None),
        P("fsdp"),
        P("fsdp"),
    )
    return jax.shard_map(
        on_device, mesh=mesh, in_specs=in_specs, out_specs=out_specs, check_vma=False
    )
```

```python
import functools

import jax
import jax.numpy as jnp
from jax import lax
from jax.experimental import pallas as pl
from jax.experimental.pallas import tpu as pltpu
from jax.sharding import PartitionSpec as P

HD = 64
LANES = 128
EPSILON = 1e-06
BLOCKED = -(2.0**100)
ROOT_2_PI = 0.7978845608028654
CUBIC = 0.044715
VMEM_LIMIT = 60 * 1024 * 1024

bf16 = jnp.bfloat16
f32 = jnp.float32


def mm(a, b):
    return jnp.dot(a, b, preferred_element_type=f32)


def mm_nt(a, b):
    return lax.dot_general(a, b, (((1,), (1,)), ((), ())), preferred_element_type=f32)


def mm_tn(a, b):
    return lax.dot_general(a, b, (((0,), (0,)), ((), ())), preferred_element_type=f32)


def params(**extra):
    return pltpu.CompilerParams(vmem_limit_bytes=VMEM_LIMIT, **extra)


def cost(flops, moved, transcendentals=0):
    return pl.CostEstimate(
        flops=int(flops), bytes_accessed=int(moved), transcendentals=int(transcendentals)
    )


def vmem():
    return pl.BlockSpec(memory_space=pltpu.VMEM)


def anywhere():
    return pl.BlockSpec(memory_space=pl.ANY)


def smem():
    return pl.BlockSpec(memory_space=pltpu.SMEM)


def lane_ids(rows):
    return lax.broadcasted_iota(jnp.int32, (rows, LANES), 1)


def split3(column):
    high = column.astype(bf16)
    rest = column - high.astype(f32)
    middle = rest.astype(bf16)
    low = (rest - middle.astype(f32)).astype(bf16)
    return (high.astype(f32), middle.astype(f32), low.astype(f32))


def project_kernel(heads, segments, layout, aliased, *refs):
    w_rows, x_ref = refs[1:3]
    arrays = 1 + max(array for array, _ in layout)
    w_refs = refs[3 : 3 + arrays]
    code_ref = refs[3 + arrays]
    qa_ref, ka_ref, va_ref, h1_ref, own_ref, gain_row = refs[4 + arrays + aliased :]
    piece_rows = w_refs[0].shape[1]
    spans = []
    for piece, (array, index) in enumerate(layout):
        at = pl.ds(pl.multiple_of(w_rows[piece] * piece_rows, piece_rows), piece_rows)
        spans.append(at)
        columns = w_refs[array][index, :, 3 * LANES :].astype(f32)
        gain_row[:, at] = columns.T[0:8, :]
    x = x_ref[...].astype(f32)
    scaling = lax.rsqrt(jnp.mean(x * x, axis=-1, keepdims=True) + EPSILON)
    h1_ref[...] = (x * scaling * gain_row[0:1, :]).astype(bf16)
    qkv = None
    for at, (array, index) in zip(spans, layout):
        part = mm(h1_ref[:, at], w_refs[array][index, :, : 3 * LANES])
        qkv = part if qkv is None else qkv + part
    rows = x.shape[0]
    lane = lane_ids(rows)
    q = qkv[:, :LANES].astype(bf16) * jnp.asarray(HD**-0.5, bf16)
    k = qkv[:, LANES : 2 * LANES].astype(bf16)
    v = qkv[:, 2 * LANES :].astype(bf16)
    place = lane % HD
    code = code_ref[...]
    same = place == code // 2
    padded = code % 2 == 0
    q_table = jnp.where(same | ((place == HD - 1) & padded), 1.0, 0.0).astype(bf16)
    k_table = jnp.where(
        place < segments,
        jnp.where(same & ~padded, 0.0, BLOCKED),
        jnp.where((place >= HD - 4) & (place < HD - 1), 1.0, 0.0),
    ).astype(bf16)
    ones = jnp.ones((rows, LANES), bf16)
    product = q.astype(f32) * k.astype(f32)
    for head in range(heads):
        own = lane // HD == head
        qa_ref[head] = jnp.where(own, q, q_table)
        ka_ref[head] = jnp.where(own, k, k_table)
        va_ref[head] = jnp.where(own, v, ones)
        score = jnp.sum(jnp.where(own, product, 0.0), axis=-1, keepdims=True)
        score = jnp.where(padded, score, 4.0 * BLOCKED)
        own_ref[head] = jnp.broadcast_to(score, (rows, LANES))


def project(slot, w_rows, slots, heads, segments, x, layout, arrays, codes, previous):
    rows, width = x.shape
    total = rows * slots
    head_spec = pl.BlockSpec((heads, rows, LANES), lambda i, s, w: (0, s[0], 0))
    shapes = [jax.ShapeDtypeStruct((heads, total, LANES), bf16)] * 3 + [
        jax.ShapeDtypeStruct((total, width), bf16),
        jax.ShapeDtypeStruct((heads, total, LANES), f32),
    ]
    extra = () if previous is None else tuple(previous)
    first = 4 + len(arrays)
    return pl.pallas_call(
        functools.partial(project_kernel, heads, segments, layout, len(extra)),
        grid_spec=pltpu.PrefetchScalarGridSpec(
            num_scalar_prefetch=2,
            grid=(1,),
            in_specs=[pl.BlockSpec((rows, width), lambda i, s, w: (0, 0))]
            + [pl.BlockSpec(a.shape, lambda i, s, w: (0, 0, 0)) for a in arrays]
            + [pl.BlockSpec((rows, 1), lambda i, s, w: (s[0], 0))]
            + [anywhere()] * len(extra),
            out_specs=[head_spec] * 3
            + [pl.BlockSpec((rows, width), lambda i, s, w: (s[0], 0)), head_spec],
            scratch_shapes=[pltpu.VMEM((8, width), f32)],
        ),
        out_shape=shapes,
        input_output_aliases={first + i: i for i in range(len(extra))},
        compiler_params=params(),
        cost_estimate=cost(2 * rows * width * 3 * LANES, 4 * rows * width + 8 * LANES * width),
        name="project",
    )(slot, w_rows, x, *arrays, codes, *extra)


def forward_kernel(
    heads, step, q_ref, own_ref, v_near, k_ref, v_ref,
    att_ref, sum_ref, qb_ref, weight_ref, scores, tops, acc,
):
    pack, rows = q_ref.shape[1], q_ref.shape[3]
    span = pack * rows
    total = k_ref.shape[1]
    lane = lane_ids(span)
    folds = step // LANES

    def queries(head):
        return q_ref[head].reshape(span, LANES)

    def find(head, at):
        found = mm_nt(queries(head), k_ref[head, at, :])
        scores[head, :, at] = found
        top = tops[head]
        for fold in range(folds):
            top = jnp.maximum(top, found[:, fold * LANES : (fold + 1) * LANES])
        tops[head] = top

    def mix(head, at):
        top = tops[head]
        shifted = scores[head, :, at] - jnp.concatenate([top] * folds, axis=1)
        acc[head] += mm(jnp.exp(shifted).astype(bf16), v_ref[head, at, :])

    def settle(head):
        top = jnp.max(tops[head], axis=-1, keepdims=True)
        tops[head] = jnp.maximum(
            jnp.broadcast_to(top, (span, LANES)), own_ref[head].reshape(span, LANES)
        )

    def sweep(first, second):
        def run(number, carry):
            at = pl.ds(pl.multiple_of(number * step, step), step)
            if second is not None:
                mix(second, at)
            if first is not None:
                find(first, at)
            return carry

        lax.fori_loop(0, total // step, run, 0)
        if first is not None:
            settle(first)

    tops[...] = jnp.full_like(tops, 4.0 * BLOCKED)
    acc[...] = jnp.zeros_like(acc)
    for head in range(heads + 1):
        sweep(head if head < heads else None, head - 1 if head > 0 else None)
    merged = None
    for head in range(heads):
        own = lane // HD == head
        other = HD if head == 0 else 0
        top = tops[head]
        value = v_near[head].reshape(span, LANES).astype(f32)
        own_weight = jnp.exp(own_ref[head].reshape(span, LANES) - top).astype(bf16).astype(f32)
        mixed = acc[head] + own_weight * value
        swapped = pltpu.roll(mixed, HD, axis=1)
        weight_sum = jnp.where(own, swapped, mixed)
        inverse = 1.0 / weight_sum
        weight_ref[head] = (own_weight * inverse).astype(bf16).reshape(pack, 1, rows, LANES)
        log_total = top + jnp.log(weight_sum)
        mixed = mixed * inverse
        merged = mixed if merged is None else jnp.where(own, mixed, merged)
        filled = queries(head).astype(f32)
        for place, part in enumerate(split3(-log_total)):
            filled = jnp.where(lane == other + HD - 4 + place, part, filled)
        qb_ref[head] = filled.astype(bf16).reshape(pack, 1, rows, LANES)
    att_ref[...] = merged.astype(bf16).reshape(pack, 1, rows, LANES)
    sum_ref[...] = merged.reshape(pack, 1, rows, LANES)


def attend(qa, ka, va, own, parts, slots):
    heads, total, _ = qa.shape
    rows = total // slots // parts
    shape = (heads, slots, parts, rows, LANES)
    view = [a.reshape(shape) for a in (qa, own, va)]
    block = pl.BlockSpec((heads, slots, 1, rows, LANES), lambda i: (0, 0, i, 0, 0))
    whole = pl.BlockSpec(ka.shape, lambda i: (0, 0, 0))
    flat = pl.BlockSpec((slots, 1, rows, LANES), lambda i: (0, i, 0, 0))
    span = slots * rows
    return pl.pallas_call(
        functools.partial(forward_kernel, heads, 512),
        grid=(parts,),
        in_specs=[block, block, block, whole, whole],
        out_specs=[flat, flat, block, block],
        out_shape=[
            jax.ShapeDtypeStruct(shape[1:], bf16),
            jax.ShapeDtypeStruct(shape[1:], f32),
            jax.ShapeDtypeStruct(shape, bf16),
            jax.ShapeDtypeStruct(shape, bf16),
        ],
        scratch_shapes=[
            pltpu.VMEM((heads, span, total), f32),
            pltpu.VMEM((heads, span, LANES), f32),
            pltpu.VMEM((heads, span, LANES), f32),
        ],
        compiler_params=params(),
        cost_estimate=cost(
            8 * heads * total * total * LANES, 4 * heads * total * LANES, heads * total * total
        ),
        name="attend",
    )(*view, ka, va)


def backward_kernel(heads, part, parts, tile, *refs):
    first, last = part == 0, part == parts - 1
    qb_ref, k_ref, v_ref, weight_ref = refs[:4]
    if first:
        sum_ref, grad_ref, kv_ref, dq_ref, gb_ref, dk_acc, dv_acc = refs[4:]
        dq_acc = dq_ref
    elif last:
        gb_ref, dq_in, kv_ref, dq_ref, dq_acc, dk_acc, dv_acc = refs[4:]
    else:
        gb_ref, dq_in, kv_ref, dq_ref, dk_acc, dv_acc = refs[4:]
        dq_acc = dq_ref
    slots, rows = k_ref.shape[1], k_ref.shape[3]
    total = qb_ref.shape[1]
    span = slots * rows
    pack = slots
    if first:
        block_rows = grad_ref.shape[1]
        lane = lane_ids(block_rows)

        def prepare(slot, carry):
            at = pl.ds(pl.multiple_of(slot * block_rows, block_rows), block_rows)
            grad = grad_ref[slot].astype(f32)
            product = grad * sum_ref[at, :]
            for head in range(heads):
                other = HD if head == 0 else 0
                own = lane // HD == head
                delta = jnp.sum(jnp.where(own, product, 0.0), axis=-1, keepdims=True)
                filled = jnp.where(own, grad, 0.0)
                for place, piece in enumerate(split3(-delta)):
                    filled = jnp.where(lane == other + place, piece, filled)
                gb_ref[head, at, :] = filled.astype(bf16)
                dq_acc[head, at, :] = jnp.zeros((block_rows, LANES), f32)
            return carry

        lax.fori_loop(0, slots, prepare, 0)
    else:
        dq_acc[...] = dq_in[...]
    width = pack * rows
    lane = lane_ids(width)
    for index in range(slots // pack):
        keys = slice(index * pack, (index + 1) * pack)
        dk_acc[...] = jnp.zeros_like(dk_acc)
        dv_acc[...] = jnp.zeros_like(dv_acc)

        def step(number, carry):
            at = pl.ds(pl.multiple_of(number * tile, tile), tile)
            for head in range(heads):
                key = k_ref[head, keys].reshape(width, LANES)
                value = v_ref[head, keys].reshape(width, LANES)
                q = qb_ref[head, at, :]
                g = gb_ref[head, at, :]
                weights = jnp.exp(mm_nt(key, q))
                inner = mm_nt(value, g)
                score_grad = (weights * inner).astype(bf16)
                dv_acc[head] += mm(weights.astype(bf16), g)
                dk_acc[head] += mm(score_grad, q)
                dq_acc[head, at, :] += mm_tn(score_grad, key)
            return carry

        lax.fori_loop(0, total // tile, step, 0)
        dk_all, dv_all = None, None
        for head in range(heads):
            own = lane // HD == head
            starts = [
                slot * (total // slots) + part * rows
                for slot in range(index * pack, (index + 1) * pack)
            ]
            q = jnp.concatenate([qb_ref[head, b : b + rows, :] for b in starts], axis=0).astype(f32)
            g = jnp.concatenate([gb_ref[head, b : b + rows, :] for b in starts], axis=0).astype(f32)
            k = k_ref[head, keys].reshape(width, LANES).astype(f32)
            v = v_ref[head, keys].reshape(width, LANES).astype(f32)
            weight = weight_ref[head, keys].reshape(width, LANES).astype(f32)
            inner = jnp.sum(v * g, axis=-1, keepdims=True)
            score_grad = (weight * inner).astype(bf16).astype(f32)
            dk = dk_acc[head] + score_grad * q
            dv = dv_acc[head] + weight * g
            dq = score_grad * k
            for place, b in enumerate(starts):
                dq_acc[head, b : b + rows, :] += dq[place * rows : (place + 1) * rows, :]
            dk_all = dk if head == 0 else jnp.where(own, dk, dk_all)
            dv_all = dv if head == 0 else jnp.where(own, dv, dv_all)
        kv_ref[keys, 0] = dk_all.astype(bf16).reshape(pack, rows, LANES)
        kv_ref[keys, 1] = dv_all.astype(bf16).reshape(pack, rows, LANES)
    if last:
        block_rows = total // slots
        lane = lane_ids(block_rows)
        for slot in range(slots):
            at = slice(slot * block_rows, (slot + 1) * block_rows)
            dq = dq_acc[0, at, :]
            if heads == 2:
                dq = jnp.where(lane < HD, dq, dq_acc[1, at, :])
            dq_ref[slot] = (dq * HD**-0.5).astype(bf16)


def attend_back(qb, ka, va, weights, part, parts, slots, sums, grads, state):
    heads, total, _ = ka.shape
    rows = total // slots // parts
    first, last = part == 0, part == parts - 1
    shape = (heads, slots, parts, rows, LANES)
    near = pl.BlockSpec((heads, slots, 1, rows, LANES), lambda i: (0, 0, part, 0, 0))
    wide = pl.BlockSpec((heads, total, LANES), lambda i: (0, 0, 0))
    pack = slots
    accumulator = pltpu.VMEM((heads, pack * rows, LANES), f32)
    if first:
        inputs = [sums, grads]
        in_specs = [
            pl.BlockSpec((total, LANES), lambda i: (0, 0)),
            pl.BlockSpec(grads.shape, lambda i: (0, 0, 0)),
        ]
    else:
        inputs, in_specs = list(state), [wide, wide]
    out_shape = [jax.ShapeDtypeStruct((slots, 2, rows, LANES), bf16)]
    out_specs = [pl.BlockSpec((slots, 2, rows, LANES), lambda i: (0, 0, 0, 0))]
    scratch = [accumulator, accumulator]
    if last:
        out_shape.append(jax.ShapeDtypeStruct((slots, total // slots, LANES), bf16))
        out_specs.append(pl.BlockSpec((slots, total // slots, LANES), lambda i: (0, 0, 0)))
        scratch = [pltpu.VMEM((heads, total, LANES), f32)] + scratch
    else:
        out_shape.append(jax.ShapeDtypeStruct((heads, total, LANES), f32))
        out_specs.append(wide)
    if first:
        out_shape.append(jax.ShapeDtypeStruct((heads, total, LANES), bf16))
        out_specs.append(wide)
    return pl.pallas_call(
        functools.partial(backward_kernel, heads, part, parts, 512),
        grid=(1,),
        in_specs=[wide, near, near, near] + in_specs,
        out_specs=out_specs,
        out_shape=out_shape,
        scratch_shapes=scratch,
        compiler_params=params(),
        cost_estimate=cost(
            20 * heads * total * total * LANES // parts,
            12 * heads * total * LANES,
            heads * total * total // parts,
        ),
        name="attend_back",
    )(qb, ka.reshape(shape), va.reshape(shape), weights.reshape(shape), *inputs)


def own_kernel(halves, *refs):
    w_rows, h_ref, dq_ref = refs[:3]
    parts = len(refs) - 4 - halves
    kv_refs, outs, term = refs[3 : 3 + parts], refs[3 + parts : -1], refs[-1]
    slots, _, rows, width = h_ref.shape
    total = slots * parts * rows
    term[:, :LANES] = mm_tn(
        h_ref[...].reshape(total, width), dq_ref[...].reshape(total, LANES)
    ).astype(bf16)
    for kind in range(2):
        summed = None
        for part in range(parts):
            piece = mm_tn(
                h_ref[:, part].reshape(slots * rows, width),
                kv_refs[part][:, kind].reshape(slots * rows, LANES),
            )
            summed = piece if summed is None else summed + piece
        term[:, (kind + 1) * LANES : (kind + 2) * LANES] = summed.astype(bf16)
    place_rows(halves, w_rows, term, outs)


def place_rows(halves, w_rows, source, outs):
    inner, step_rows = outs[0].shape[0], outs[0].shape[1]
    for half in range(halves):
        for index in range(inner):
            piece = index * halves + half
            at = pl.ds(pl.multiple_of(w_rows[piece] * step_rows, step_rows), step_rows)
            outs[half][index] = source[at, :]


def own_terms(w_rows, h1, dq, kvs, shards, halves):
    slots, rows = kvs[0].shape[0], kvs[0].shape[2]
    width = h1.shape[1]
    pieces = shards if halves == 2 else 1
    shape = jax.ShapeDtypeStruct((pieces // halves, width // pieces, 3 * LANES), bf16)
    return pl.pallas_call(
        functools.partial(own_kernel, halves),
        in_specs=[smem()] + [vmem()] * (2 + len(kvs)),
        out_specs=[vmem()] * halves,
        out_shape=[shape] * halves,
        scratch_shapes=[pltpu.VMEM((width, 3 * LANES), bf16)],
        compiler_params=params(),
        cost_estimate=cost(2 * h1.size * 3 * LANES, 2 * h1.size),
        name="own_terms",
    )(w_rows, h1.reshape(slots, len(kvs), rows, width), dq, *kvs)


def load_rows(entries, sources, targets, sems, rows_of):
    started = [[] for _ in targets]
    for number, (target, source, index, place, step_rows, offset, column) in enumerate(entries):
        begin = pl.multiple_of(rows_of[index][place] * step_rows + offset, 16)
        at = pl.ds(begin, sources[source].shape[0])
        width = targets[target].shape[1]
        copy = pltpu.make_async_copy(
            sources[source].at[:, column : column + width],
            targets[target].at[at, :],
            sems.at[number],
        )
        copy.start()
        started[target].append(copy)
    return started


def store_rows(source, targets, sems, index, columns, shift=0):
    moved = columns if shift == 0 else pl.ds(shift + columns.start, columns.size)
    copies = []
    halves = len(targets)
    for piece in range(halves * targets[0].shape[0]):
        step_rows = targets[0].shape[1]
        at = pl.ds(pl.multiple_of(index[piece] * step_rows, step_rows), step_rows)
        target = targets[piece % halves].at[piece // halves, :, moved]
        copies.append(pltpu.make_async_copy(source.at[at, columns], target, sems.at[piece]))
    return copies


def pre_kernel(parts, entries, *refs):
    w_rows = refs[0]
    att_refs = refs[1 : 1 + parts]
    x_ref, gain_ref = refs[1 + parts : 3 + parts]
    sources = refs[3 + parts : -5]
    mid_ref, h2_ref, att_ref, wo, sems = refs[-5:]
    loads = load_rows(entries, sources, (wo,), sems, (w_rows,))
    rows, width = x_ref.shape
    blocks = att_refs[0].shape[0]
    block_width = width // blocks
    part_rows = rows // parts
    for part in range(parts):
        for block in range(blocks):
            att_ref[
                part * part_rows : (part + 1) * part_rows,
                block * block_width : (block + 1) * block_width,
            ] = att_refs[part][block][:, :block_width]
    for copy in loads[0]:
        copy.wait()
    middle = x_ref[...].astype(f32) + mm(att_ref[...], wo[...])
    scaling = lax.rsqrt(jnp.mean(middle * middle, axis=-1, keepdims=True) + EPSILON)
    h2_ref[...] = (middle * scaling * gain_ref[...].astype(f32)).astype(bf16)
    mid_ref[...] = middle


def pre_stage(w_rows, att_parts, x, gain, entries, sources):
    rows, width = x.shape
    hbm = pl.BlockSpec(memory_space=pltpu.HBM)
    return pl.pallas_call(
        functools.partial(pre_kernel, len(att_parts), entries),
        in_specs=[smem()] + [vmem()] * (len(att_parts) + 2) + [hbm] * len(sources),
        out_specs=[vmem()] * 3,
        out_shape=[
            jax.ShapeDtypeStruct((rows, width), f32),
            jax.ShapeDtypeStruct((rows, width), bf16),
            jax.ShapeDtypeStruct((rows, width), bf16),
        ],
        scratch_shapes=[
            pltpu.VMEM((width, width), bf16),
            pltpu.SemaphoreType.DMA((len(entries),)),
        ],
        compiler_params=params(),
        cost_estimate=cost(2 * rows * width * width, 2 * width * width),
        name="pre_stage",
    )(w_rows, *att_parts, x, gain, *sources)


def main_kernel(groups, halves, entries, count, *refs):
    w_rows, d_rows = refs[:2]
    h2_refs, c_refs = refs[2 : 2 + groups], refs[2 + groups : 2 + 2 * groups]
    refs = refs[2 + 2 * groups :]
    sources, refs = refs[:count], refs[count:]
    out_refs, back_refs = refs[:groups], refs[groups : 2 * groups]
    refs = refs[2 * groups :]
    gu_refs, dg_refs = refs[:halves], refs[halves : 2 * halves]
    refs = refs[2 * halves :]
    wg, wu, wd, gg, ug, dg, h2_all, h2t, c_all, acc_out, acc_back, in_sems, out_sems = refs
    loads = load_rows(entries, sources, (wg, wu, wd), in_sems, (w_rows, d_rows))
    rows = h2_refs[0].shape[0]
    for group in range(groups):
        span = slice(group * rows, (group + 1) * rows)
        h2_all[span, :] = h2_refs[group][...]
        c_all[span, :] = c_refs[group][...]
    h2t[...] = h2_all[...].T
    acc_out[...] = jnp.zeros_like(acc_out)
    acc_back[...] = jnp.zeros_like(acc_back)
    for started in loads:
        for copy in started:
            copy.wait()

    def columns_at(at):
        h2 = h2_all[...]
        c = c_all[...]
        gate = mm(h2, wg[:, at])
        up = mm(h2, wu[:, at])
        act_grad = mm_nt(c, wd[at, :])
        square = gate * gate
        bend = jnp.tanh(gate * (ROOT_2_PI + (ROOT_2_PI * CUBIC) * square))
        half = 0.5 * (1.0 + bend)
        curve = gate * half
        slope = half + (0.5 * gate) * (1.0 - bend * bend) * (
            ROOT_2_PI + (3.0 * ROOT_2_PI * CUBIC) * square
        )
        act = (curve * up).astype(bf16)
        d_up = (act_grad * curve).astype(bf16)
        d_gate = (act_grad * up * slope).astype(bf16)
        acc_back[...] += mm_nt(d_gate, wg[:, at]) + mm_nt(d_up, wu[:, at])
        gg[:, at] = mm(h2t[...], d_gate).astype(bf16)
        ug[:, at] = mm(h2t[...], d_up).astype(bf16)
        dg[at, :] = mm_tn(act, c).astype(bf16)
        acc_out[...] += mm(act, wd[at, :])
        for kind, source in ((0, gg), (1, ug)):
            for copy in store_rows(source, gu_refs, out_sems.at[kind], w_rows, at, kind * width):
                copy.start()

    width = wg.shape[1]
    step_width = 256
    whole = width // step_width

    def column_step(number, carry):
        columns_at(pl.ds(pl.multiple_of(number * step_width, step_width), step_width))
        return carry

    lax.fori_loop(0, whole, column_step, 0)
    if width % step_width:
        columns_at(pl.ds(whole * step_width, width % step_width))
    everything = slice(None)
    stores = store_rows(dg, dg_refs, out_sems.at[2], d_rows, everything)
    for copy in stores:
        copy.start()
    for group in range(groups):
        span = slice(group * rows, (group + 1) * rows)
        kind = out_refs[group].dtype
        out_refs[group][...] = acc_out[span, :].astype(kind)
        back_refs[group][...] = acc_back[span, :].astype(kind)
    whole = pl.ds(0, width)
    stores += store_rows(gg, gu_refs, out_sems.at[0], w_rows, whole)
    stores += store_rows(ug, gu_refs, out_sems.at[1], w_rows, whole, width)
    for copy in stores:
        copy.wait()


def main_stage(w_rows, d_rows, h2s, cs, hidden, entries, sources, halves):
    groups = len(h2s)
    rows, width = h2s[0].shape
    pieces, d_pieces = w_rows.shape[0], d_rows.shape[0]
    hbm = pl.BlockSpec(memory_space=pltpu.HBM)
    partial = [jax.ShapeDtypeStruct((rows, width), f32 if g == 0 else bf16) for g in range(groups)]
    up_shape = jax.ShapeDtypeStruct((pieces // halves, width // pieces, 2 * hidden), bf16)
    down_shape = jax.ShapeDtypeStruct((d_pieces // halves, hidden // d_pieces, width), bf16)
    total = groups * rows
    out = pl.pallas_call(
        functools.partial(main_kernel, groups, halves, entries, len(sources)),
        in_specs=[smem(), smem()] + [vmem()] * (2 * groups) + [hbm] * len(sources),
        out_specs=[vmem()] * (2 * groups) + [hbm] * (2 * halves),
        out_shape=partial * 2 + [up_shape] * halves + [down_shape] * halves,
        scratch_shapes=[
            pltpu.VMEM((width, hidden), bf16),
            pltpu.VMEM((width, hidden), bf16),
            pltpu.VMEM((hidden, width), bf16),
            pltpu.VMEM((width, hidden), bf16),
            pltpu.VMEM((width, hidden), bf16),
            pltpu.VMEM((hidden, width), bf16),
            pltpu.VMEM((total, width), bf16),
            pltpu.VMEM((width, total), bf16),
            pltpu.VMEM((total, width), bf16),
            pltpu.VMEM((total, width), f32),
            pltpu.VMEM((total, width), f32),
            pltpu.SemaphoreType.DMA((len(entries),)),
            pltpu.SemaphoreType.DMA((3, max(pieces, d_pieces))),
        ],
        compiler_params=params(),
        cost_estimate=cost(18 * total * width * hidden, 12 * width * hidden),
        name="main_stage",
    )(w_rows, d_rows, *h2s, *cs, *sources)
    outs, backs, grads = list(out[:groups]), list(out[groups : 2 * groups]), out[2 * groups :]
    return (outs, backs, grads[:halves], grads[halves:])


def post_kernel(groups, entries, count, *refs):
    w_rows, mid_ref = refs[:2]
    backs, refs = refs[2 : 2 + groups], refs[2 + groups :]
    c_ref, gain_ref = refs[:2]
    sources, refs = refs[2 : 2 + count], refs[2 + count :]
    dmid_ref, branch_ref, da_ref, wo, in_sems = refs
    loads = load_rows(entries, sources, (wo,), in_sems, (w_rows,))
    middle = mid_ref[...]
    scaling = lax.rsqrt(jnp.mean(middle * middle, axis=-1, keepdims=True) + EPSILON)
    incoming = sum(ref[...].astype(f32) for ref in backs) * gain_ref[...].astype(f32)
    centre = jnp.mean(incoming * middle, axis=-1, keepdims=True)
    d_middle = (
        c_ref[...].astype(f32)
        + scaling * incoming
        - middle * (scaling * scaling * scaling * centre)
    )
    dmid_ref[...] = d_middle
    branch = d_middle.astype(bf16)
    branch_ref[...] = branch
    for copy in loads[0]:
        copy.wait()
    d_att = mm_nt(branch, wo[...]).astype(bf16)
    blocks = da_ref.shape[0]
    block_width = d_att.shape[1] // blocks
    for block in range(blocks):
        piece = d_att[:, block * block_width : (block + 1) * block_width]
        if block_width < LANES:
            piece = jnp.concatenate([piece] * (LANES // block_width), axis=1)
        da_ref[block] = piece


def post_stage(w_rows, middle, backs, c, gain, slots, entries, sources):
    groups = len(backs)
    rows, width = middle.shape
    hbm = pl.BlockSpec(memory_space=pltpu.HBM)
    return pl.pallas_call(
        functools.partial(post_kernel, groups, entries, len(sources)),
        in_specs=[smem()] + [vmem()] * (3 + groups) + [hbm] * len(sources),
        out_specs=[vmem()] * 3,
        out_shape=[
            jax.ShapeDtypeStruct((rows, width), f32),
            jax.ShapeDtypeStruct((rows, width), bf16),
            jax.ShapeDtypeStruct((slots, rows, LANES), bf16),
        ],
        scratch_shapes=[
            pltpu.VMEM((width, width), bf16),
            pltpu.SemaphoreType.DMA((len(entries),)),
        ],
        compiler_params=params(),
        cost_estimate=cost(2 * rows * width * width, 4 * width * width),
        name="post_stage",
    )(w_rows, middle, *backs, c, gain, *sources)


def out_kernel(halves, w_rows, att_ref, branch_ref, *refs):
    og, sems = refs[halves:]
    og[...] = mm_tn(att_ref[...], branch_ref[...]).astype(bf16)
    stores = store_rows(og, refs[:halves], sems, w_rows, slice(None))
    for copy in stores:
        copy.start()
    for copy in stores:
        copy.wait()


def out_terms(w_rows, att, branch, halves):
    rows, width = att.shape
    pieces = w_rows.shape[0]
    hbm = pl.BlockSpec(memory_space=pltpu.HBM)
    shape = jax.ShapeDtypeStruct((pieces // halves, width // pieces, width), bf16)
    return pl.pallas_call(
        functools.partial(out_kernel, halves),
        in_specs=[smem(), vmem(), vmem()],
        out_specs=[hbm] * halves,
        out_shape=[shape] * halves,
        scratch_shapes=[pltpu.VMEM((width, width), bf16), pltpu.SemaphoreType.DMA((pieces,))],
        compiler_params=params(),
        cost_estimate=cost(2 * rows * width * width, 4 * width * width),
        name="out_terms",
    )(w_rows, att, branch)


def last_kernel(parts, pieces, *refs):
    w_rows, dq_ref = refs[:2]
    kv_refs = refs[2 : 2 + parts]
    x_ref, dmid_ref, gain_ref = refs[2 + parts : 5 + parts]
    weight_refs = refs[5 + parts : 5 + parts + pieces]
    out_ref, grad, total = refs[5 + parts + pieces :]
    rows, width = x_ref.shape
    blocks = dq_ref.shape[0]
    block_width = width // blocks
    piece_width = width // pieces
    done = 0
    for part in range(parts):
        part_rows = kv_refs[part].shape[2]
        for block in range(blocks):
            lanes = slice(block * block_width, (block + 1) * block_width)
            for kind in range(2):
                grad[kind + 1, done : done + part_rows, lanes] = kv_refs[part][block, kind][
                    :, :block_width
                ]
        done += part_rows
    for block in range(blocks):
        lanes = slice(block * block_width, (block + 1) * block_width)
        grad[0, :, lanes] = dq_ref[block][:, :block_width]
    for piece in range(pieces):
        at = pl.ds(pl.multiple_of(w_rows[piece] * piece_width, piece_width), piece_width)
        w = weight_refs[piece]
        total[:, at] = (
            mm_nt(grad[0], w[:, :width])
            + mm_nt(grad[1], w[:, width : 2 * width])
            + mm_nt(grad[2], w[:, 2 * width :])
        )
    x = x_ref[...].astype(f32)
    scaling = lax.rsqrt(jnp.mean(x * x, axis=-1, keepdims=True) + EPSILON)
    incoming = total[...] * gain_ref[...].astype(f32)
    centre = jnp.mean(incoming * x, axis=-1, keepdims=True)
    out_ref[...] = dmid_ref[...] + scaling * incoming - x * (scaling * scaling * scaling * centre)


def last_stage(w_rows, dq, kvs, x, d_middle, gain, weights):
    rows, width = x.shape
    return pl.pallas_call(
        functools.partial(last_kernel, len(kvs), len(weights)),
        in_specs=[smem()] + [vmem()] * (4 + len(kvs) + len(weights)),
        out_specs=vmem(),
        out_shape=jax.ShapeDtypeStruct((rows, width), f32),
        scratch_shapes=[pltpu.VMEM((3, rows, width), bf16), pltpu.VMEM((rows, width), f32)],
        compiler_params=params(),
        cost_estimate=cost(6 * rows * width * width, 6 * width * width),
        name="last_stage",
    )(w_rows, dq, *kvs, x, d_middle, gain, *weights)


def finish_kernel(mine_ref, own_ref, other_ref, w_ref, gain_ref, *outs):
    width = outs[0].shape[1]
    mine = mine_ref[0]
    for source, bit in ((own_ref, mine), (other_ref, 1 - mine)):
        for index in range(4):
            slot = (index % 2) * 4 + bit * 2 + index // 2
            at = pl.ds(pl.multiple_of(slot * LANES, LANES), LANES)
            for kind in range(3):
                outs[kind][:, at] = source[index, :, kind * LANES : (kind + 1) * LANES].astype(f32)
    total = None
    for kind in range(3):
        weight = w_ref[:, kind * width : (kind + 1) * width].astype(f32)
        part = jnp.sum(outs[kind][...] * weight, axis=-1, keepdims=True)
        total = part if total is None else total + part
    outs[3][...] = total / gain_ref[...].astype(f32)


def finish_own(mine, own, other, weights, gain):
    rows, width = own.shape[1], weights.shape[1] // 3
    return pl.pallas_call(
        finish_kernel,
        in_specs=[smem()] + [vmem()] * 4,
        out_specs=[vmem()] * 4,
        out_shape=[jax.ShapeDtypeStruct((rows, width), f32)] * 3
        + [jax.ShapeDtypeStruct((rows, 1), f32)],
        compiler_params=params(),
        cost_estimate=cost(6 * rows * width, 20 * rows * width),
        name="finish_own",
    )(mine, own, other, weights, gain)


def flip(values, axis, delta):
    count = lax.axis_size(axis)
    return lax.ppermute(values, axis, [(i, i ^ delta) for i in range(count)])


def after(values, *others):
    return lax.optimization_barrier((values, *others))[0]


def bits_of(count):
    return [1 << i for i in range(count.bit_length() - 1)]


def add_low(a, b):
    return (a.astype(f32) + b.astype(f32)).astype(bf16)


def cut(values, start, size):
    return lax.dynamic_slice_in_dim(values, start, size, axis=-2)


class Line:
    def __init__(self):
        self.last = None

    def hold(self, values):
        if self.last is not None:
            values = after(values, self.last)
        self.last = values
        return values


class Reduction:
    def __init__(self, kept, given, line):
        self.own, self.given, self.line, self.joined = kept, given, line, None

    def core(self):
        self.arrived = flip(self.line.hold(self.given), "fsdp", 1)

    def hold(self, *others):
        self.arrived = lax.optimization_barrier((self.arrived, *others))[0]

    def across(self):
        given = self.line.hold(add_low(self.own[1], self.arrived[1]))
        self.own = add_low(self.own[0], self.arrived[0])
        self.arrived = flip(given, "fsdp", 2)

    def halve(self, bit):
        place = lax.axis_index("seq")
        half = self.own.shape[-2] // 2
        mine = (place // bit) % 2
        keep, give = mine * half, (1 - mine) * half
        given = add_low(cut(self.own, give, half), cut(self.arrived, give, half))
        kept = add_low(cut(self.own, keep, half), cut(self.arrived, keep, half))
        self.own, self.arrived = kept, flip(self.line.hold(given), "seq", bit)

    def settle(self):
        self.own = add_low(self.own, self.arrived)

    def swap_columns(self):
        self.settle()
        self.arrived = flip(self.line.hold(self.own[1]), "fsdp", 2)

    def join_columns(self):
        upper = (lax.axis_index("fsdp") // 2) == 1
        width = self.arrived.shape[-1] // 2
        parts = []
        for kind in range(2):
            here = self.own[0, :, kind * width : (kind + 1) * width]
            there = self.arrived[:, kind * width : (kind + 1) * width]
            parts += [jnp.where(upper, there, here), jnp.where(upper, here, there)]
        self.own = jnp.concatenate(parts, axis=-1)

    def widen(self, bit):
        self.join()
        self.own = self.line.hold(self.own)
        self.arrived, self.joined = flip(self.own, "seq", bit), bit

    def join(self):
        if self.joined is None:
            return
        upper = ((lax.axis_index("seq") // self.joined) % 2) == 1
        first = jnp.where(upper, self.arrived, self.own)
        second = jnp.where(upper, self.own, self.arrived)
        self.own, self.joined = jnp.concatenate([first, second], axis=0), None


def token_codes(lengths_row, order_row, real_row):
    total = order_row.shape[0]
    ends_at = jnp.cumsum(lengths_row)
    positions = jnp.arange(total, dtype=jnp.int32)
    packed_segment = jnp.sum((positions[:, None] >= ends_at[None, :]).astype(jnp.int32), axis=1)
    packed_code = packed_segment * 2 + (real_row > 0).astype(jnp.int32)
    return jnp.sum(
        jnp.where(positions[:, None] == order_row[None, :], packed_code[None, :], 0), axis=1
    ).reshape(total, 1)


def parts_of(total):
    return max(2, total // 1280)


def move_chain(array, pairs):
    return lax.ppermute(
        array, "seq", [(a * 2 + low, b * 2 + low) for a, b in pairs for low in range(2)]
    )


def turn(blocks):
    return lax.all_to_all(blocks, "seq", split_axis=0, concat_axis=0, tiled=True)


def on_device(
    tokens,
    cotangent,
    query_weight,
    key_weight,
    value_weight,
    output_weight,
    gate_weight,
    up_weight,
    down_weight,
    attention_gain,
    feedforward_gain,
    lengths,
    token_order,
    real_token,
):
    x, c = tokens[0], cotangent[0]
    rows, width = x.shape
    slots = lax.axis_size("seq")
    shards = lax.axis_size("fsdp")
    seq, shard = lax.axis_index("seq"), lax.axis_index("fsdp")
    direct = slots == 8 and shards == 4
    heads = width // slots // HD
    own_width = heads * HD
    shard_rows = width // shards
    halves = 2 if direct else 1

    own_columns = [
        lax.dynamic_slice_in_dim(w, seq * own_width, own_width, axis=1)
        for w in (query_weight, key_weight, value_weight)
    ]
    gains = jnp.stack([attention_gain, feedforward_gain], axis=1)
    own_columns = jnp.concatenate(
        [jnp.pad(w, ((0, 0), (0, LANES - own_width))) for w in own_columns]
        + [jnp.pad(gains, ((0, 0), (0, LANES - 2)))],
        axis=1,
    )
    qkv_weight = jnp.concatenate([query_weight, key_weight, value_weight], axis=1)

    if direct:
        w_rows = shard ^ jnp.arange(shards, dtype=jnp.int32)
        place = seq // 2
        half = shard_rows // 2
        hidden = gate_weight.shape[1] // 2
        columns_x = flip(own_columns, "fsdp", 2)
        beside = flip(x, "seq", 1)
        near = move_chain(x, [(0, 1), (1, 0), (2, 3), (3, 2)])
        inner = move_chain(x, [(1, 2), (2, 1)])
        output_x = flip(output_weight, "fsdp", 2)
        both = jnp.stack([own_columns, columns_x])
        both_c = flip(both, "fsdp", 1)
        column_arrays = [both, both_c]
        column_layout = ((0, 0), (1, 0), (0, 1), (1, 1))
        near, inner, _ = lax.optimization_barrier((near, inner, beside))
        far_inner = move_chain(near, [(1, 2), (2, 1)])
        far_outer = move_chain(inner, [(1, 0), (2, 3)])
        near_beside = flip(near, "seq", 1)
        far_half = (1 - shard // 2) * hidden
        near_half = (shard // 2) * hidden
        up_own, up_sent = [
            jnp.concatenate(
                [
                    lax.dynamic_slice_in_dim(after(w, own_columns), start, hidden, axis=1)
                    for w in (gate_weight, up_weight)
                ],
                axis=1,
            )
            for start in (near_half, far_half)
        ]
        up_x1 = flip(after(up_sent[:half], near), "fsdp", 2)
        token_order = after(token_order, near)
        is_inner = (place == 1) | (place == 2)
        block_slots = [seq ^ d for d in range(slots)]
    else:
        w_rows = jnp.zeros((1,), jnp.int32)
        column_arrays = [lax.all_gather(own_columns, "fsdp", axis=0, tiled=True)[None]]
        column_layout = ((0, 0),)
        gathered = lax.all_gather(x, "seq", axis=0)
        x_blocks = [gathered[i] for i in range(slots)]
        block_slots = [jnp.asarray(i, jnp.int32) for i in range(slots)]

    codes = token_codes(lengths[0], token_order[0], real_token[0])
    gain_pieces = jnp.stack(
        [column_arrays[a][i, :, 3 * LANES : 3 * LANES + 2] for a, i in column_layout]
    )
    gain_rows = jnp.take(gain_pieces, w_rows, axis=0).reshape(width, 2)
    gain_1, gain_2 = gain_rows[:, 0].reshape(1, width), gain_rows[:, 1].reshape(1, width)
    state = None

    def project_block(number, block, state):
        slot = block_slots[number].reshape(1).astype(jnp.int32)
        return project(
            slot,
            w_rows,
            slots,
            heads,
            lengths.shape[1],
            block,
            column_layout,
            column_arrays,
            codes,
            state,
        )

    if direct:
        state = project_block(0, x, state)
        state = project_block(1, beside, state)
        far_inner, far_outer, _, _, _, _ = lax.optimization_barrier(
            (far_inner, far_outer, near_beside, up_x1, output_x, state[0])
        )
        third = move_chain(far_inner, [(1, 0), (2, 3)])
        far = jnp.where(is_inner, far_inner, far_outer)
        far_beside = flip(far, "seq", 1)
        up_x2 = flip(after(up_sent[half:], far_inner), "fsdp", 2)
        up_c = flip(after(up_own, far_inner), "fsdp", 1)
        state = project_block(2, near, state)
        state = project_block(3, near_beside, state)
        state = project_block(4, far, state)
        third, _, _, _, _ = lax.optimization_barrier(
            (third, far_beside, up_x2, up_c, state[0])
        )
        cross = jnp.where(is_inner, inner, third)
        cross_beside = flip(cross, "seq", 1)
        c_x = flip(after(c, cross), "fsdp", 2)
        up_xc1 = flip(after(up_x1, cross), "fsdp", 1)
        down_c = flip(after(down_weight, cross), "fsdp", 1)
        state = project_block(5, far_beside, state)
        state = project_block(6, cross, state)
        cross_beside, _, _, _ = lax.optimization_barrier((cross_beside, c_x, up_xc1, down_c))
        state = project_block(7, cross_beside, state)
    else:
        for number, block in enumerate(x_blocks):
            state = project_block(number, block, state)
    qa, ka, va, h1, own_scores = state

    att, sums, qb, own_weights = attend(qa, ka, va, own_scores, parts_of(slots * rows), slots)
    if direct:
        qkv_x = flip(after(qkv_weight, qa), "fsdp", 2)
        up_xc2 = flip(after(up_x2, qa), "fsdp", 1)
        output_c = flip(after(output_weight, qa), "fsdp", 1)
        output_xc = flip(after(output_x, qa), "fsdp", 1)
        att = lax.optimization_barrier((att, up_xc2, output_c, output_xc))[0]
    if direct:
        output_pieces = [output_weight, output_c, output_x, output_xc]
        output_entries = [(0, p, 0, p, shard_rows, 0, 0) for p in range(4)]
        d_rows = (shard % 2) ^ jnp.arange(2, dtype=jnp.int32)
        ff_sources = [up_own, up_c, up_x1, up_x2, up_xc1, up_xc2, down_weight, down_c]
        ff_entries = [
            (kind, source, 0, place, shard_rows, offset, kind * hidden)
            for kind in range(2)
            for source, place, offset in (
                (0, 0, 0), (1, 1, 0), (2, 2, 0), (3, 2, half), (4, 3, 0), (5, 3, half),
            )
        ] + [(2, 6, 1, 0, down_weight.shape[0], 0, 0), (2, 7, 1, 1, down_weight.shape[0], 0, 0)]
    else:
        output_pieces = [lax.all_gather(output_weight, "fsdp", axis=0, tiled=True)]
        output_entries = [(0, 0, 0, 0, width, 0, 0)]
        d_rows = w_rows
        ff_sources = [
            lax.all_gather(w, "fsdp", axis=0, tiled=True)
            for w in (gate_weight, up_weight, down_weight)
        ]
        hidden = gate_weight.shape[1]
        ff_entries = [(i, i, 0, 0, width, 0, 0) for i in range(3)]
    att_parts = [turn(att.reshape(slots, rows, LANES))]
    if direct:
        x, _ = lax.optimization_barrier((x, qkv_x))
    total = rows * slots
    sums = sums.reshape(total, LANES)
    qb = qb.reshape(heads, total, LANES)

    middle, h2, att = pre_stage(w_rows, att_parts, x, gain_2, output_entries, output_pieces)
    if direct:
        h2s, cs = [h2, flip(h2, "fsdp", 2)], [c, c_x]
    else:
        h2s, cs = [h2], [c]
    outs, backs, gu, dg = main_stage(
        w_rows, d_rows, h2s, cs, hidden, ff_entries, ff_sources, halves
    )
    if direct:
        line = Line()
        backs[1] = flip(backs[1], "fsdp", 2)
        up_r = Reduction(*gu, line)
        down_r = Reduction(dg[0][0], dg[1][0], line)
        up_r.core()
        down_r.core()
        up_r.halve(1)
        down_r.halve(2)
        backs[1] = lax.optimization_barrier((backs[1], up_r.own, down_r.own))[0]
    d_middle, branch, d_att = post_stage(
        w_rows, middle, backs, c, gain_2, slots, output_entries, output_pieces
    )
    og = out_terms(w_rows, att, branch, halves)
    grad_blocks = turn(d_att)
    parts = 4
    back = functools.partial(attend_back, qb, ka, va, own_weights)
    if direct:
        qkv_c = flip(after(qkv_weight, d_att), "fsdp", 1)
        output_r = Reduction(*og, line)
        down_r.hold(d_att)
        down_r.halve(1)
        output_r.core()
        up_r.hold(d_att)
        up_r.halve(2)
        grad_blocks = lax.optimization_barrier(
            (grad_blocks, down_r.own, up_r.own, qkv_c)
        )[0]
    else:
        qkv_pieces = [lax.all_gather(qkv_weight, "fsdp", axis=0, tiled=True)]
    kv_0, dq, gb = back(0, parts, slots, sums, grad_blocks, None)
    if direct:
        for r in (down_r, up_r, output_r):
            r.hold(kv_0)
        down_r.halve(4)
        up_r.halve(4)
        output_r.across()
        outs[1] = flip(after(outs[1], kv_0), "fsdp", 2)
        qkv_xc = flip(after(qkv_x, kv_0), "fsdp", 1)
        qkv_pieces = [qkv_weight, qkv_c, qkv_x, qkv_xc]
        gb = lax.optimization_barrier((gb, down_r.own, up_r.own, output_r.own))[0]
    kv_1, dq = back(1, parts, slots, None, None, (gb, dq))
    kv_early = turn(jnp.concatenate([kv_0, kv_1], axis=2))
    if direct:
        for r in (down_r, up_r, output_r):
            r.hold(kv_1)
        up_r.swap_columns()
        down_r.settle()
        down_r.widen(4)
        output_r.halve(2)
        gb = lax.optimization_barrier((gb, down_r.own, up_r.own, output_r.own, qkv_xc, outs[1]))[0]
    kv_2, dq = back(2, parts, slots, None, None, (gb, dq))
    if direct:
        for r in (down_r, up_r, output_r):
            r.hold(kv_2)
        up_r.join_columns()
        up_r.widen(4)
        down_r.widen(1)
        output_r.halve(1)
        gb = lax.optimization_barrier((gb, down_r.own, up_r.own, output_r.own))[0]
    kv_3, dq = back(3, parts, slots, None, None, (gb, dq))
    kv_late = jnp.concatenate([kv_2, kv_3], axis=2)
    late = turn(jnp.concatenate([kv_late.reshape(slots, rows, LANES), dq], axis=1))
    kv_late = late[:, :rows].reshape(kv_late.shape)
    dq_turned = late[:, rows:]
    if direct:
        for r in (down_r, up_r, output_r):
            r.hold(kv_3)
        up_r.widen(2)
        down_r.widen(2)
        output_r.halve(4)
        dq = lax.optimization_barrier((dq, down_r.own, up_r.own, output_r.own, kv_early))[0]
    layer_out = (middle + sum(part.astype(f32) for part in outs)).astype(bf16)
    own = own_terms(w_rows, h1, dq, [kv_0, kv_1, kv_2, kv_3], shards, halves)
    if direct:
        own_r = Reduction(*own, line)
        own_r.core()
        for r in (up_r, output_r):
            r.hold(own[0])
        up_r.widen(1)
        output_r.settle()
        output_r.widen(4)
        own_r.across()
        output_r.widen(1)
        own_r.settle()
        own_r.own = after(own_r.own[None], down_r.arrived)
        own_r.widen(4)
        output_r.widen(2)
        own_r.widen(1)
        own_r.arrived = after(own_r.arrived, late)
        own_r.widen(2)
        input_grad = last_stage(
            w_rows, dq_turned, [kv_early, kv_late], x, d_middle, gain_1, qkv_pieces
        )
        for r in (up_r, down_r, output_r):
            r.join()
        gate_grad, up_grad = up_r.own[:, : 2 * hidden], up_r.own[:, 2 * hidden :]
        down_grad, output_grad = down_r.own, output_r.own
        query_grad, key_grad, value_grad, attention_gain_grad = finish_own(
            ((seq // 2) % 2).reshape(1).astype(jnp.int32),
            own_r.own,
            own_r.arrived,
            qkv_weight,
            attention_gain.reshape(shard_rows, 1),
        )
        attention_gain_grad = attention_gain_grad.reshape(shard_rows)
    else:
        own_share = lax.psum_scatter(own[0][0], "fsdp", scatter_dimension=0, tiled=True)
        all_shares = lax.all_gather(own_share, "seq", axis=0)
        gate_grad, up_grad, down_grad, output_grad = [
            lax.psum(lax.psum_scatter(g, "fsdp", scatter_dimension=0, tiled=True), "seq")
            for g in (gu[0][0, :, :hidden], gu[0][0, :, hidden:], dg[0][0], og[0][0])
        ]
    def gain_grad(terms, gain):
        summed = sum(jnp.sum(g * w.astype(f32), axis=1) for g, w in terms)
        return summed / gain.astype(f32)

    if not direct:
        all_shares = all_shares.reshape(slots, shard_rows, 3, LANES)[..., :own_width].astype(f32)
        query_grad, key_grad, value_grad = [
            all_shares[:, :, i, :].transpose(1, 0, 2).reshape(shard_rows, width) for i in range(3)
        ]
        input_grad = last_stage(
            w_rows, dq_turned, [kv_early, kv_late], x, d_middle, gain_1, qkv_pieces
        )
        attention_gain_grad = gain_grad(
            ((query_grad, query_weight), (key_grad, key_weight), (value_grad, value_weight)),
            attention_gain,
        )
    output_grad, gate_grad, up_grad, down_grad = [
        g.astype(f32) for g in (output_grad, gate_grad, up_grad, down_grad)
    ]
    feedforward_gain_grad = gain_grad(
        ((gate_grad, gate_weight), (up_grad, up_weight)), feedforward_gain
    )
    return (
        layer_out[None],
        input_grad[None],
        query_grad,
        key_grad,
        value_grad,
        output_grad,
        gate_grad,
        up_grad,
        down_grad,
        attention_gain_grad,
        feedforward_gain_grad,
    )


def solution(mesh):
    in_specs = (
        P("fsdp", "seq", None),
        P("fsdp", "seq", None),
        P("fsdp", None),
        P("fsdp", None),
        P("fsdp", None),
        P("fsdp", None),
        P("fsdp", None),
        P("fsdp", None),
        P("fsdp", None),
        P("fsdp"),
        P("fsdp"),
        P("fsdp", None),
        P("fsdp", None),
        P("fsdp", None),
    )
    out_specs = (
        P("fsdp", "seq", None),
        P("fsdp", "seq", None),
        P("fsdp", None),
        P("fsdp", None),
        P("fsdp", None),
        P("fsdp", None),
        P("fsdp", None),
        P("fsdp", None),
        P("fsdp", None),
        P("fsdp"),
        P("fsdp"),
    )
    return jax.shard_map(
        on_device, mesh=mesh, in_specs=in_specs, out_specs=out_specs, check_vma=False
    )
```

```python
import functools

import jax
import jax.numpy as jnp
from jax import lax
from jax.experimental import pallas as pl
from jax.experimental.pallas import tpu as pltpu
from jax.sharding import PartitionSpec as P

HD = 64
LANES = 128
EPSILON = 1e-06
BLOCKED = -(2.0**100)
ROOT_2_PI = 0.7978845608028654
CUBIC = 0.044715
VMEM_LIMIT = 60 * 1024 * 1024

bf16 = jnp.bfloat16
f32 = jnp.float32


def mm(a, b):
    return jnp.dot(a, b, preferred_element_type=f32)


def mm_nt(a, b):
    return lax.dot_general(a, b, (((1,), (1,)), ((), ())), preferred_element_type=f32)


def mm_tn(a, b):
    return lax.dot_general(a, b, (((0,), (0,)), ((), ())), preferred_element_type=f32)


def params(**extra):
    return pltpu.CompilerParams(vmem_limit_bytes=VMEM_LIMIT, **extra)


def cost(flops, moved, transcendentals=0):
    return pl.CostEstimate(
        flops=int(flops), bytes_accessed=int(moved), transcendentals=int(transcendentals)
    )


def vmem():
    return pl.BlockSpec(memory_space=pltpu.VMEM)


def anywhere():
    return pl.BlockSpec(memory_space=pl.ANY)


def smem():
    return pl.BlockSpec(memory_space=pltpu.SMEM)


def lane_ids(rows):
    return lax.broadcasted_iota(jnp.int32, (rows, LANES), 1)


def split3(column):
    high = column.astype(bf16)
    rest = column - high.astype(f32)
    middle = rest.astype(bf16)
    low = (rest - middle.astype(f32)).astype(bf16)
    return (high.astype(f32), middle.astype(f32), low.astype(f32))


def project_kernel(heads, segments, layout, aliased, *refs):
    w_rows, x_ref = refs[1:3]
    arrays = 1 + max(array for array, _ in layout)
    w_refs = refs[3 : 3 + arrays]
    code_ref = refs[3 + arrays]
    qa_ref, ka_ref, va_ref, h1_ref, own_ref, gain_row = refs[4 + arrays + aliased :]
    piece_rows = w_refs[0].shape[1]
    spans = []
    for piece, (array, index) in enumerate(layout):
        at = pl.ds(pl.multiple_of(w_rows[piece] * piece_rows, piece_rows), piece_rows)
        spans.append(at)
        columns = w_refs[array][index, :, 3 * LANES :].astype(f32)
        gain_row[:, at] = columns.T[0:8, :]
    x = x_ref[...].astype(f32)
    scaling = lax.rsqrt(jnp.mean(x * x, axis=-1, keepdims=True) + EPSILON)
    h1_ref[...] = (x * scaling * gain_row[0:1, :]).astype(bf16)
    qkv = None
    for at, (array, index) in zip(spans, layout):
        part = mm(h1_ref[:, at], w_refs[array][index, :, : 3 * LANES])
        qkv = part if qkv is None else qkv + part
    rows = x.shape[0]
    lane = lane_ids(rows)
    q = qkv[:, :LANES].astype(bf16) * jnp.asarray(HD**-0.5, bf16)
    k = qkv[:, LANES : 2 * LANES].astype(bf16)
    v = qkv[:, 2 * LANES :].astype(bf16)
    place = lane % HD
    code = code_ref[...]
    same = place == code // 2
    padded = code % 2 == 0
    q_table = jnp.where(same | ((place == HD - 1) & padded), 1.0, 0.0).astype(bf16)
    k_table = jnp.where(
        place < segments,
        jnp.where(same & ~padded, 0.0, BLOCKED),
        jnp.where((place >= HD - 4) & (place < HD - 1), 1.0, 0.0),
    ).astype(bf16)
    ones = jnp.ones((rows, LANES), bf16)
    product = q.astype(f32) * k.astype(f32)
    for head in range(heads):
        own = lane // HD == head
        qa_ref[head] = jnp.where(own, q, q_table)
        ka_ref[head] = jnp.where(own, k, k_table)
        va_ref[head] = jnp.where(own, v, ones)
        score = jnp.sum(jnp.where(own, product, 0.0), axis=-1, keepdims=True)
        score = jnp.where(padded, score, 4.0 * BLOCKED)
        own_ref[head] = jnp.broadcast_to(score, (rows, LANES))


def project(slot, w_rows, slots, heads, segments, x, layout, arrays, codes, previous):
    rows, width = x.shape
    total = rows * slots
    head_spec = pl.BlockSpec((heads, rows, LANES), lambda i, s, w: (0, s[0], 0))
    shapes = [jax.ShapeDtypeStruct((heads, total, LANES), bf16)] * 3 + [
        jax.ShapeDtypeStruct((total, width), bf16),
        jax.ShapeDtypeStruct((heads, total, LANES), f32),
    ]
    extra = () if previous is None else tuple(previous)
    first = 4 + len(arrays)
    return pl.pallas_call(
        functools.partial(project_kernel, heads, segments, layout, len(extra)),
        grid_spec=pltpu.PrefetchScalarGridSpec(
            num_scalar_prefetch=2,
            grid=(1,),
            in_specs=[pl.BlockSpec((rows, width), lambda i, s, w: (0, 0))]
            + [pl.BlockSpec(a.shape, lambda i, s, w: (0, 0, 0)) for a in arrays]
            + [pl.BlockSpec((rows, 1), lambda i, s, w: (s[0], 0))]
            + [anywhere()] * len(extra),
            out_specs=[head_spec] * 3
            + [pl.BlockSpec((rows, width), lambda i, s, w: (s[0], 0)), head_spec],
            scratch_shapes=[pltpu.VMEM((8, width), f32)],
        ),
        out_shape=shapes,
        input_output_aliases={first + i: i for i in range(len(extra))},
        compiler_params=params(),
        cost_estimate=cost(2 * rows * width * 3 * LANES, 4 * rows * width + 8 * LANES * width),
        name="project",
    )(slot, w_rows, x, *arrays, codes, *extra)


def tile_of(total):
    return total if total <= 2560 else 512


def forward_kernel(
    heads, step, q_ref, own_ref, v_near, k_ref, v_ref,
    att_ref, sum_ref, qb_ref, weight_ref, scores, tops, acc,
):
    pack, rows = q_ref.shape[1], q_ref.shape[3]
    span = pack * rows
    total = k_ref.shape[1]
    lane = lane_ids(span)
    folds = step // LANES

    def queries(head):
        return q_ref[head].reshape(span, LANES)

    def find(head, at):
        found = mm_nt(queries(head), k_ref[head, at, :])
        scores[head, :, at] = found
        top = tops[head]
        for fold in range(folds):
            top = jnp.maximum(top, found[:, fold * LANES : (fold + 1) * LANES])
        tops[head] = top

    def mix(head, at):
        top = tops[head]
        shifted = scores[head, :, at] - jnp.concatenate([top] * folds, axis=1)
        acc[head] += mm(jnp.exp(shifted).astype(bf16), v_ref[head, at, :])

    def settle(head):
        top = jnp.max(tops[head], axis=-1, keepdims=True)
        tops[head] = jnp.maximum(
            jnp.broadcast_to(top, (span, LANES)), own_ref[head].reshape(span, LANES)
        )

    def sweep(first, second):
        def run(number, carry):
            at = pl.ds(pl.multiple_of(number * step, step), step)
            if second is not None:
                mix(second, at)
            if first is not None:
                find(first, at)
            return carry

        lax.fori_loop(0, total // step, run, 0)
        if first is not None:
            settle(first)

    tops[...] = jnp.full_like(tops, 4.0 * BLOCKED)
    acc[...] = jnp.zeros_like(acc)
    for head in range(heads + 1):
        sweep(head if head < heads else None, head - 1 if head > 0 else None)
    merged = None
    for head in range(heads):
        own = lane // HD == head
        other = HD if head == 0 else 0
        top = tops[head]
        value = v_near[head].reshape(span, LANES).astype(f32)
        own_weight = jnp.exp(own_ref[head].reshape(span, LANES) - top).astype(bf16).astype(f32)
        mixed = acc[head] + own_weight * value
        swapped = pltpu.roll(mixed, HD, axis=1)
        weight_sum = jnp.where(own, swapped, mixed)
        inverse = 1.0 / weight_sum
        weight_ref[head] = (own_weight * inverse).astype(bf16).reshape(pack, 1, rows, LANES)
        log_total = top + jnp.log(weight_sum)
        mixed = mixed * inverse
        merged = mixed if merged is None else jnp.where(own, mixed, merged)
        filled = queries(head).astype(f32)
        for place, part in enumerate(split3(-log_total)):
            filled = jnp.where(lane == other + HD - 4 + place, part, filled)
        qb_ref[head] = filled.astype(bf16).reshape(pack, 1, rows, LANES)
    att_ref[...] = merged.astype(bf16).reshape(pack, 1, rows, LANES)
    sum_ref[...] = merged.reshape(pack, 1, rows, LANES)


def attend(qa, ka, va, own, parts, slots):
    heads, total, _ = qa.shape
    rows = total // slots // parts
    shape = (heads, slots, parts, rows, LANES)
    view = [a.reshape(shape) for a in (qa, own, va)]
    block = pl.BlockSpec((heads, slots, 1, rows, LANES), lambda i: (0, 0, i, 0, 0))
    whole = pl.BlockSpec(ka.shape, lambda i: (0, 0, 0))
    flat = pl.BlockSpec((slots, 1, rows, LANES), lambda i: (0, i, 0, 0))
    span = slots * rows
    return pl.pallas_call(
        functools.partial(forward_kernel, heads, tile_of(total)),
        grid=(parts,),
        in_specs=[block, block, block, whole, whole],
        out_specs=[flat, flat, block, block],
        out_shape=[
            jax.ShapeDtypeStruct(shape[1:], bf16),
            jax.ShapeDtypeStruct(shape[1:], f32),
            jax.ShapeDtypeStruct(shape, bf16),
            jax.ShapeDtypeStruct(shape, bf16),
        ],
        scratch_shapes=[
            pltpu.VMEM((heads, span, total), f32),
            pltpu.VMEM((heads, span, LANES), f32),
            pltpu.VMEM((heads, span, LANES), f32),
        ],
        compiler_params=params(),
        cost_estimate=cost(
            8 * heads * total * total * LANES, 4 * heads * total * LANES, heads * total * total
        ),
        name="attend",
    )(*view, ka, va)


def backward_kernel(heads, part, parts, tile, *refs):
    first, last = part == 0, part == parts - 1
    qb_ref, k_ref, v_ref, weight_ref = refs[:4]
    if first:
        sum_ref, grad_ref, kv_ref, dq_ref, gb_ref, dk_acc, dv_acc = refs[4:]
        dq_acc = dq_ref
    elif last:
        gb_ref, dq_in, kv_ref, dq_ref, dq_acc, dk_acc, dv_acc = refs[4:]
    else:
        gb_ref, dq_in, kv_ref, dq_ref, dk_acc, dv_acc = refs[4:]
        dq_acc = dq_ref
    slots, rows = k_ref.shape[1], k_ref.shape[3]
    total = qb_ref.shape[1]
    span = slots * rows
    pack = slots
    if first:
        block_rows = grad_ref.shape[1]
        lane = lane_ids(block_rows)

        def prepare(slot, carry):
            at = pl.ds(pl.multiple_of(slot * block_rows, block_rows), block_rows)
            grad = grad_ref[slot].astype(f32)
            product = grad * sum_ref[at, :]
            for head in range(heads):
                other = HD if head == 0 else 0
                own = lane // HD == head
                delta = jnp.sum(jnp.where(own, product, 0.0), axis=-1, keepdims=True)
                filled = jnp.where(own, grad, 0.0)
                for place, piece in enumerate(split3(-delta)):
                    filled = jnp.where(lane == other + place, piece, filled)
                gb_ref[head, at, :] = filled.astype(bf16)
                dq_acc[head, at, :] = jnp.zeros((block_rows, LANES), f32)
            return carry

        lax.fori_loop(0, slots, prepare, 0)
    else:
        dq_acc[...] = dq_in[...]
    width = pack * rows
    lane = lane_ids(width)
    for index in range(slots // pack):
        keys = slice(index * pack, (index + 1) * pack)
        dk_acc[...] = jnp.zeros_like(dk_acc)
        dv_acc[...] = jnp.zeros_like(dv_acc)

        def step(number, carry):
            at = pl.ds(pl.multiple_of(number * tile, tile), tile)
            for head in range(heads):
                key = k_ref[head, keys].reshape(width, LANES)
                value = v_ref[head, keys].reshape(width, LANES)
                q = qb_ref[head, at, :]
                g = gb_ref[head, at, :]
                weights = jnp.exp(mm_nt(key, q))
                inner = mm_nt(value, g)
                score_grad = (weights * inner).astype(bf16)
                dv_acc[head] += mm(weights.astype(bf16), g)
                dk_acc[head] += mm(score_grad, q)
                dq_acc[head, at, :] += mm_tn(score_grad, key)
            return carry

        lax.fori_loop(0, total // tile, step, 0)
        dk_all, dv_all = None, None
        for head in range(heads):
            own = lane // HD == head
            starts = [
                slot * (total // slots) + part * rows
                for slot in range(index * pack, (index + 1) * pack)
            ]
            q = jnp.concatenate([qb_ref[head, b : b + rows, :] for b in starts], axis=0).astype(f32)
            g = jnp.concatenate([gb_ref[head, b : b + rows, :] for b in starts], axis=0).astype(f32)
            k = k_ref[head, keys].reshape(width, LANES).astype(f32)
            v = v_ref[head, keys].reshape(width, LANES).astype(f32)
            weight = weight_ref[head, keys].reshape(width, LANES).astype(f32)
            inner = jnp.sum(v * g, axis=-1, keepdims=True)
            score_grad = (weight * inner).astype(bf16).astype(f32)
            dk = dk_acc[head] + score_grad * q
            dv = dv_acc[head] + weight * g
            dq = score_grad * k
            for place, b in enumerate(starts):
                dq_acc[head, b : b + rows, :] += dq[place * rows : (place + 1) * rows, :]
            dk_all = dk if head == 0 else jnp.where(own, dk, dk_all)
            dv_all = dv if head == 0 else jnp.where(own, dv, dv_all)
        kv_ref[keys, 0] = dk_all.astype(bf16).reshape(pack, rows, LANES)
        kv_ref[keys, 1] = dv_all.astype(bf16).reshape(pack, rows, LANES)
    if last:
        block_rows = total // slots
        lane = lane_ids(block_rows)
        for slot in range(slots):
            at = slice(slot * block_rows, (slot + 1) * block_rows)
            dq = dq_acc[0, at, :]
            if heads == 2:
                dq = jnp.where(lane < HD, dq, dq_acc[1, at, :])
            dq_ref[slot] = (dq * HD**-0.5).astype(bf16)


def attend_back(qb, ka, va, weights, part, parts, slots, sums, grads, state):
    heads, total, _ = ka.shape
    rows = total // slots // parts
    first, last = part == 0, part == parts - 1
    shape = (heads, slots, parts, rows, LANES)
    near = pl.BlockSpec((heads, slots, 1, rows, LANES), lambda i: (0, 0, part, 0, 0))
    wide = pl.BlockSpec((heads, total, LANES), lambda i: (0, 0, 0))
    pack = slots
    accumulator = pltpu.VMEM((heads, pack * rows, LANES), f32)
    if first:
        inputs = [sums, grads]
        in_specs = [
            pl.BlockSpec((total, LANES), lambda i: (0, 0)),
            pl.BlockSpec(grads.shape, lambda i: (0, 0, 0)),
        ]
    else:
        inputs, in_specs = list(state), [wide, wide]
    out_shape = [jax.ShapeDtypeStruct((slots, 2, rows, LANES), bf16)]
    out_specs = [pl.BlockSpec((slots, 2, rows, LANES), lambda i: (0, 0, 0, 0))]
    scratch = [accumulator, accumulator]
    if last:
        out_shape.append(jax.ShapeDtypeStruct((slots, total // slots, LANES), bf16))
        out_specs.append(pl.BlockSpec((slots, total // slots, LANES), lambda i: (0, 0, 0)))
        scratch = [pltpu.VMEM((heads, total, LANES), f32)] + scratch
    else:
        out_shape.append(jax.ShapeDtypeStruct((heads, total, LANES), f32))
        out_specs.append(wide)
    if first:
        out_shape.append(jax.ShapeDtypeStruct((heads, total, LANES), bf16))
        out_specs.append(wide)
    return pl.pallas_call(
        functools.partial(backward_kernel, heads, part, parts, tile_of(total)),
        grid=(1,),
        in_specs=[wide, near, near, near] + in_specs,
        out_specs=out_specs,
        out_shape=out_shape,
        scratch_shapes=scratch,
        compiler_params=params(),
        cost_estimate=cost(
            20 * heads * total * total * LANES // parts,
            12 * heads * total * LANES,
            heads * total * total // parts,
        ),
        name="attend_back",
    )(qb, ka.reshape(shape), va.reshape(shape), weights.reshape(shape), *inputs)


def own_kernel(halves, *refs):
    w_rows, h_ref, dq_ref = refs[:3]
    parts = len(refs) - 4 - halves
    kv_refs, outs, term = refs[3 : 3 + parts], refs[3 + parts : -1], refs[-1]
    slots, _, rows, width = h_ref.shape
    summed = None
    for part in range(parts):
        span = slots * rows
        grads = [dq_ref[:, part * rows : (part + 1) * rows]] + [
            kv_refs[part][:, kind] for kind in range(2)
        ]
        grads = jnp.concatenate([g.reshape(span, LANES) for g in grads], axis=1)
        piece = mm_tn(h_ref[:, part].reshape(span, width), grads)
        summed = piece if summed is None else summed + piece
    term[...] = summed.astype(bf16)
    place_rows(halves, w_rows, term, outs)


def place_rows(halves, w_rows, source, outs):
    inner, step_rows = outs[0].shape[0], outs[0].shape[1]
    for half in range(halves):
        for index in range(inner):
            piece = index * halves + half
            at = pl.ds(pl.multiple_of(w_rows[piece] * step_rows, step_rows), step_rows)
            outs[half][index] = source[at, :]


def own_terms(w_rows, h1, dq, kvs, shards, halves):
    slots, rows = kvs[0].shape[0], kvs[0].shape[2]
    width = h1.shape[1]
    pieces = shards if halves == 2 else 1
    shape = jax.ShapeDtypeStruct((pieces // halves, width // pieces, 3 * LANES), bf16)
    return pl.pallas_call(
        functools.partial(own_kernel, halves),
        in_specs=[smem()] + [vmem()] * (2 + len(kvs)),
        out_specs=[vmem()] * halves,
        out_shape=[shape] * halves,
        scratch_shapes=[pltpu.VMEM((width, 3 * LANES), bf16)],
        compiler_params=params(),
        cost_estimate=cost(2 * h1.size * 3 * LANES, 2 * h1.size),
        name="own_terms",
    )(w_rows, h1.reshape(slots, len(kvs), rows, width), dq, *kvs)


def load_rows(entries, sources, targets, sems, rows_of):
    started = [[] for _ in targets]
    for number, (target, source, index, place, step_rows, offset, column) in enumerate(entries):
        begin = pl.multiple_of(rows_of[index][place] * step_rows + offset, 16)
        at = pl.ds(begin, sources[source].shape[0])
        width = targets[target].shape[1]
        copy = pltpu.make_async_copy(
            sources[source].at[:, column : column + width],
            targets[target].at[at, :],
            sems.at[number],
        )
        copy.start()
        started[target].append(copy)
    return started


def store_rows(source, targets, sems, index, columns, shift=0):
    moved = columns if shift == 0 else pl.ds(shift + columns.start, columns.size)
    copies = []
    halves = len(targets)
    for piece in range(halves * targets[0].shape[0]):
        step_rows = targets[0].shape[1]
        at = pl.ds(pl.multiple_of(index[piece] * step_rows, step_rows), step_rows)
        target = targets[piece % halves].at[piece // halves, :, moved]
        copies.append(pltpu.make_async_copy(source.at[at, columns], target, sems.at[piece]))
    return copies


def pre_kernel(parts, entries, *refs):
    w_rows = refs[0]
    att_refs = refs[1 : 1 + parts]
    x_ref, gain_ref = refs[1 + parts : 3 + parts]
    sources = refs[3 + parts : -5]
    mid_ref, h2_ref, att_ref, wo, sems = refs[-5:]
    loads = load_rows(entries, sources, (wo,), sems, (w_rows,))
    rows, width = x_ref.shape
    blocks = att_refs[0].shape[0]
    block_width = width // blocks
    part_rows = rows // parts
    for part in range(parts):
        for block in range(blocks):
            att_ref[
                part * part_rows : (part + 1) * part_rows,
                block * block_width : (block + 1) * block_width,
            ] = att_refs[part][block][:, :block_width]
    for copy in loads[0]:
        copy.wait()
    middle = x_ref[...].astype(f32) + mm(att_ref[...], wo[...])
    scaling = lax.rsqrt(jnp.mean(middle * middle, axis=-1, keepdims=True) + EPSILON)
    h2_ref[...] = (middle * scaling * gain_ref[...].astype(f32)).astype(bf16)
    mid_ref[...] = middle


def pre_stage(w_rows, att_parts, x, gain, entries, sources):
    rows, width = x.shape
    hbm = pl.BlockSpec(memory_space=pltpu.HBM)
    return pl.pallas_call(
        functools.partial(pre_kernel, len(att_parts), entries),
        in_specs=[smem()] + [vmem()] * (len(att_parts) + 2) + [hbm] * len(sources),
        out_specs=[vmem()] * 3,
        out_shape=[
            jax.ShapeDtypeStruct((rows, width), f32),
            jax.ShapeDtypeStruct((rows, width), bf16),
            jax.ShapeDtypeStruct((rows, width), bf16),
        ],
        scratch_shapes=[
            pltpu.VMEM((width, width), bf16),
            pltpu.SemaphoreType.DMA((len(entries),)),
        ],
        compiler_params=params(),
        cost_estimate=cost(2 * rows * width * width, 2 * width * width),
        name="pre_stage",
    )(w_rows, *att_parts, x, gain, *sources)


def main_kernel(groups, halves, entries, count, *refs):
    w_rows, d_rows = refs[:2]
    h2_refs, c_refs = refs[2 : 2 + groups], refs[2 + groups : 2 + 2 * groups]
    refs = refs[2 + 2 * groups :]
    sources, refs = refs[:count], refs[count:]
    out_refs, back_refs = refs[:groups], refs[groups : 2 * groups]
    refs = refs[2 * groups :]
    gu_refs, dg_refs = refs[:halves], refs[halves : 2 * halves]
    refs = refs[2 * halves :]
    wg, wu, wd, gg, ug, dg, h2_all, h2t, c_all, acc_out, acc_back, in_sems, out_sems = refs
    loads = load_rows(entries, sources, (wg, wu, wd), in_sems, (w_rows, d_rows))
    rows = h2_refs[0].shape[0]
    for group in range(groups):
        span = slice(group * rows, (group + 1) * rows)
        h2_all[span, :] = h2_refs[group][...]
        c_all[span, :] = c_refs[group][...]
    h2t[...] = h2_all[...].T
    acc_out[...] = jnp.zeros_like(acc_out)
    acc_back[...] = jnp.zeros_like(acc_back)
    for started in loads:
        for copy in started:
            copy.wait()

    def columns_at(at):
        h2 = h2_all[...]
        c = c_all[...]
        gate = mm(h2, wg[:, at])
        up = mm(h2, wu[:, at])
        act_grad = mm_nt(c, wd[at, :])
        square = gate * gate
        bend = jnp.tanh(gate * (ROOT_2_PI + (ROOT_2_PI * CUBIC) * square))
        half = 0.5 * (1.0 + bend)
        curve = gate * half
        slope = half + (0.5 * gate) * (1.0 - bend * bend) * (
            ROOT_2_PI + (3.0 * ROOT_2_PI * CUBIC) * square
        )
        act = (curve * up).astype(bf16)
        d_up = (act_grad * curve).astype(bf16)
        d_gate = (act_grad * up * slope).astype(bf16)
        acc_back[...] += mm_nt(d_gate, wg[:, at]) + mm_nt(d_up, wu[:, at])
        gg[:, at] = mm(h2t[...], d_gate).astype(bf16)
        ug[:, at] = mm(h2t[...], d_up).astype(bf16)
        dg[at, :] = mm_tn(act, c).astype(bf16)
        acc_out[...] += mm(act, wd[at, :])
        for kind, source in ((0, gg), (1, ug)):
            for copy in store_rows(source, gu_refs, out_sems.at[kind], w_rows, at, kind * width):
                copy.start()

    width = wg.shape[1]
    step_width = 256
    whole = width // step_width

    def column_step(number, carry):
        columns_at(pl.ds(pl.multiple_of(number * step_width, step_width), step_width))
        return carry

    lax.fori_loop(0, whole, column_step, 0)
    if width % step_width:
        columns_at(pl.ds(whole * step_width, width % step_width))
    everything = slice(None)
    stores = store_rows(dg, dg_refs, out_sems.at[2], d_rows, everything)
    for copy in stores:
        copy.start()
    for group in range(groups):
        span = slice(group * rows, (group + 1) * rows)
        kind = out_refs[group].dtype
        out_refs[group][...] = acc_out[span, :].astype(kind)
        back_refs[group][...] = acc_back[span, :].astype(kind)
    whole = pl.ds(0, width)
    stores += store_rows(gg, gu_refs, out_sems.at[0], w_rows, whole)
    stores += store_rows(ug, gu_refs, out_sems.at[1], w_rows, whole, width)
    for copy in stores:
        copy.wait()


def main_stage(w_rows, d_rows, h2s, cs, hidden, entries, sources, halves):
    groups = len(h2s)
    rows, width = h2s[0].shape
    pieces, d_pieces = w_rows.shape[0], d_rows.shape[0]
    hbm = pl.BlockSpec(memory_space=pltpu.HBM)
    partial = [jax.ShapeDtypeStruct((rows, width), f32 if g == 0 else bf16) for g in range(groups)]
    up_shape = jax.ShapeDtypeStruct((pieces // halves, width // pieces, 2 * hidden), bf16)
    down_shape = jax.ShapeDtypeStruct((d_pieces // halves, hidden // d_pieces, width), bf16)
    total = groups * rows
    out = pl.pallas_call(
        functools.partial(main_kernel, groups, halves, entries, len(sources)),
        in_specs=[smem(), smem()] + [vmem()] * (2 * groups) + [hbm] * len(sources),
        out_specs=[vmem()] * (2 * groups) + [hbm] * (2 * halves),
        out_shape=partial * 2 + [up_shape] * halves + [down_shape] * halves,
        scratch_shapes=[
            pltpu.VMEM((width, hidden), bf16),
            pltpu.VMEM((width, hidden), bf16),
            pltpu.VMEM((hidden, width), bf16),
            pltpu.VMEM((width, hidden), bf16),
            pltpu.VMEM((width, hidden), bf16),
            pltpu.VMEM((hidden, width), bf16),
            pltpu.VMEM((total, width), bf16),
            pltpu.VMEM((width, total), bf16),
            pltpu.VMEM((total, width), bf16),
            pltpu.VMEM((total, width), f32),
            pltpu.VMEM((total, width), f32),
            pltpu.SemaphoreType.DMA((len(entries),)),
            pltpu.SemaphoreType.DMA((3, max(pieces, d_pieces))),
        ],
        compiler_params=params(),
        cost_estimate=cost(18 * total * width * hidden, 12 * width * hidden),
        name="main_stage",
    )(w_rows, d_rows, *h2s, *cs, *sources)
    outs, backs, grads = list(out[:groups]), list(out[groups : 2 * groups]), out[2 * groups :]
    return (outs, backs, grads[:halves], grads[halves:])


def post_kernel(groups, entries, count, *refs):
    w_rows, mid_ref = refs[:2]
    backs, refs = refs[2 : 2 + groups], refs[2 + groups :]
    c_ref, gain_ref = refs[:2]
    sources, refs = refs[2 : 2 + count], refs[2 + count :]
    dmid_ref, branch_ref, da_ref, wo, in_sems = refs
    loads = load_rows(entries, sources, (wo,), in_sems, (w_rows,))
    middle = mid_ref[...]
    scaling = lax.rsqrt(jnp.mean(middle * middle, axis=-1, keepdims=True) + EPSILON)
    incoming = sum(ref[...].astype(f32) for ref in backs) * gain_ref[...].astype(f32)
    centre = jnp.mean(incoming * middle, axis=-1, keepdims=True)
    d_middle = (
        c_ref[...].astype(f32)
        + scaling * incoming
        - middle * (scaling * scaling * scaling * centre)
    )
    dmid_ref[...] = d_middle
    branch = d_middle.astype(bf16)
    branch_ref[...] = branch
    for copy in loads[0]:
        copy.wait()
    d_att = mm_nt(branch, wo[...]).astype(bf16)
    blocks = da_ref.shape[0]
    block_width = d_att.shape[1] // blocks
    for block in range(blocks):
        piece = d_att[:, block * block_width : (block + 1) * block_width]
        if block_width < LANES:
            piece = jnp.concatenate([piece] * (LANES // block_width), axis=1)
        da_ref[block] = piece


def post_stage(w_rows, middle, backs, c, gain, slots, entries, sources):
    groups = len(backs)
    rows, width = middle.shape
    hbm = pl.BlockSpec(memory_space=pltpu.HBM)
    return pl.pallas_call(
        functools.partial(post_kernel, groups, entries, len(sources)),
        in_specs=[smem()] + [vmem()] * (3 + groups) + [hbm] * len(sources),
        out_specs=[vmem()] * 3,
        out_shape=[
            jax.ShapeDtypeStruct((rows, width), f32),
            jax.ShapeDtypeStruct((rows, width), bf16),
            jax.ShapeDtypeStruct((slots, rows, LANES), bf16),
        ],
        scratch_shapes=[
            pltpu.VMEM((width, width), bf16),
            pltpu.SemaphoreType.DMA((len(entries),)),
        ],
        compiler_params=params(),
        cost_estimate=cost(2 * rows * width * width, 4 * width * width),
        name="post_stage",
    )(w_rows, middle, *backs, c, gain, *sources)


def out_kernel(halves, w_rows, att_ref, branch_ref, *refs):
    og, sems = refs[halves:]
    og[...] = mm_tn(att_ref[...], branch_ref[...]).astype(bf16)
    stores = store_rows(og, refs[:halves], sems, w_rows, slice(None))
    for copy in stores:
        copy.start()
    for copy in stores:
        copy.wait()


def out_terms(w_rows, att, branch, halves):
    rows, width = att.shape
    pieces = w_rows.shape[0]
    hbm = pl.BlockSpec(memory_space=pltpu.HBM)
    shape = jax.ShapeDtypeStruct((pieces // halves, width // pieces, width), bf16)
    return pl.pallas_call(
        functools.partial(out_kernel, halves),
        in_specs=[smem(), vmem(), vmem()],
        out_specs=[hbm] * halves,
        out_shape=[shape] * halves,
        scratch_shapes=[pltpu.VMEM((width, width), bf16), pltpu.SemaphoreType.DMA((pieces,))],
        compiler_params=params(),
        cost_estimate=cost(2 * rows * width * width, 4 * width * width),
        name="out_terms",
    )(w_rows, att, branch)


def last_kernel(parts, pieces, *refs):
    w_rows, dq_ref = refs[:2]
    kv_refs = refs[2 : 2 + parts]
    x_ref, dmid_ref, gain_ref = refs[2 + parts : 5 + parts]
    weight_refs = refs[5 + parts : 5 + parts + pieces]
    out_ref, grad, total = refs[5 + parts + pieces :]
    rows, width = x_ref.shape
    blocks = dq_ref.shape[0]
    block_width = width // blocks
    piece_width = width // pieces
    done = 0
    for part in range(parts):
        part_rows = kv_refs[part].shape[2]
        for block in range(blocks):
            lanes = slice(block * block_width, (block + 1) * block_width)
            for kind in range(2):
                grad[kind + 1, done : done + part_rows, lanes] = kv_refs[part][block, kind][
                    :, :block_width
                ]
        done += part_rows
    for block in range(blocks):
        lanes = slice(block * block_width, (block + 1) * block_width)
        grad[0, :, lanes] = dq_ref[block][:, :block_width]
    for piece in range(pieces):
        at = pl.ds(pl.multiple_of(w_rows[piece] * piece_width, piece_width), piece_width)
        w = weight_refs[piece]
        total[:, at] = (
            mm_nt(grad[0], w[:, :width])
            + mm_nt(grad[1], w[:, width : 2 * width])
            + mm_nt(grad[2], w[:, 2 * width :])
        )
    x = x_ref[...].astype(f32)
    scaling = lax.rsqrt(jnp.mean(x * x, axis=-1, keepdims=True) + EPSILON)
    incoming = total[...] * gain_ref[...].astype(f32)
    centre = jnp.mean(incoming * x, axis=-1, keepdims=True)
    out_ref[...] = dmid_ref[...] + scaling * incoming - x * (scaling * scaling * scaling * centre)


def last_stage(w_rows, dq, kvs, x, d_middle, gain, weights):
    rows, width = x.shape
    return pl.pallas_call(
        functools.partial(last_kernel, len(kvs), len(weights)),
        in_specs=[smem()] + [vmem()] * (4 + len(kvs) + len(weights)),
        out_specs=vmem(),
        out_shape=jax.ShapeDtypeStruct((rows, width), f32),
        scratch_shapes=[pltpu.VMEM((3, rows, width), bf16), pltpu.VMEM((rows, width), f32)],
        compiler_params=params(),
        cost_estimate=cost(6 * rows * width * width, 6 * width * width),
        name="last_stage",
    )(w_rows, dq, *kvs, x, d_middle, gain, *weights)


def finish_kernel(mine_ref, own_ref, other_ref, w_ref, gain_ref, *outs):
    width = outs[0].shape[1]
    mine = mine_ref[0]
    for source, bit in ((own_ref, mine), (other_ref, 1 - mine)):
        for index in range(4):
            slot = (index % 2) * 4 + bit * 2 + index // 2
            at = pl.ds(pl.multiple_of(slot * LANES, LANES), LANES)
            for kind in range(3):
                outs[kind][:, at] = source[index, :, kind * LANES : (kind + 1) * LANES].astype(f32)
    total = None
    for kind in range(3):
        weight = w_ref[:, kind * width : (kind + 1) * width].astype(f32)
        part = jnp.sum(outs[kind][...] * weight, axis=-1, keepdims=True)
        total = part if total is None else total + part
    outs[3][...] = total / gain_ref[...].astype(f32)


def finish_own(mine, own, other, weights, gain):
    rows, width = own.shape[1], weights.shape[1] // 3
    return pl.pallas_call(
        finish_kernel,
        in_specs=[smem()] + [vmem()] * 4,
        out_specs=[vmem()] * 4,
        out_shape=[jax.ShapeDtypeStruct((rows, width), f32)] * 3
        + [jax.ShapeDtypeStruct((rows, 1), f32)],
        compiler_params=params(),
        cost_estimate=cost(6 * rows * width, 20 * rows * width),
        name="finish_own",
    )(mine, own, other, weights, gain)


def flip(values, axis, delta):
    count = lax.axis_size(axis)
    return lax.ppermute(values, axis, [(i, i ^ delta) for i in range(count)])


def after(values, *others):
    return lax.optimization_barrier((values, *others))[0]


def bits_of(count):
    return [1 << i for i in range(count.bit_length() - 1)]


def add_low(a, b):
    return (a.astype(f32) + b.astype(f32)).astype(bf16)


def cut(values, start, size):
    return lax.dynamic_slice_in_dim(values, start, size, axis=-2)


class Line:
    def __init__(self):
        self.last = None

    def hold(self, values):
        if self.last is not None:
            values = after(values, self.last)
        self.last = values
        return values


class Reduction:
    def __init__(self, kept, given, line):
        self.own, self.given, self.line, self.joined = kept, given, line, None

    def core(self):
        self.arrived = flip(self.line.hold(self.given), "fsdp", 1)

    def hold(self, *others):
        self.arrived = lax.optimization_barrier((self.arrived, *others))[0]

    def across(self):
        given = self.line.hold(add_low(self.own[1], self.arrived[1]))
        self.own = add_low(self.own[0], self.arrived[0])
        self.arrived = flip(given, "fsdp", 2)

    def halve(self, bit):
        place = lax.axis_index("seq")
        half = self.own.shape[-2] // 2
        mine = (place // bit) % 2
        keep, give = mine * half, (1 - mine) * half
        given = add_low(cut(self.own, give, half), cut(self.arrived, give, half))
        kept = add_low(cut(self.own, keep, half), cut(self.arrived, keep, half))
        self.own, self.arrived = kept, flip(self.line.hold(given), "seq", bit)

    def settle(self):
        self.own = add_low(self.own, self.arrived)

    def swap_columns(self):
        self.settle()
        self.arrived = flip(self.line.hold(self.own[1]), "fsdp", 2)

    def join_columns(self):
        upper = (lax.axis_index("fsdp") // 2) == 1
        width = self.arrived.shape[-1] // 2
        parts = []
        for kind in range(2):
            here = self.own[0, :, kind * width : (kind + 1) * width]
            there = self.arrived[:, kind * width : (kind + 1) * width]
            parts += [jnp.where(upper, there, here), jnp.where(upper, here, there)]
        self.own = jnp.concatenate(parts, axis=-1)

    def widen(self, bit):
        self.join()
        self.own = self.line.hold(self.own)
        self.arrived, self.joined = flip(self.own, "seq", bit), bit

    def join(self):
        if self.joined is None:
            return
        upper = ((lax.axis_index("seq") // self.joined) % 2) == 1
        first = jnp.where(upper, self.arrived, self.own)
        second = jnp.where(upper, self.own, self.arrived)
        self.own, self.joined = jnp.concatenate([first, second], axis=0), None


def token_codes(lengths_row, order_row, real_row):
    total = order_row.shape[0]
    ends_at = jnp.cumsum(lengths_row)
    positions = jnp.arange(total, dtype=jnp.int32)
    packed_segment = jnp.sum((positions[:, None] >= ends_at[None, :]).astype(jnp.int32), axis=1)
    packed_code = packed_segment * 2 + (real_row > 0).astype(jnp.int32)
    return jnp.sum(
        jnp.where(positions[:, None] == order_row[None, :], packed_code[None, :], 0), axis=1
    ).reshape(total, 1)


def parts_of(total):
    return max(2, total // 1280)


def move_chain(array, pairs):
    return lax.ppermute(
        array, "seq", [(a * 2 + low, b * 2 + low) for a, b in pairs for low in range(2)]
    )


def turn(blocks):
    return lax.all_to_all(blocks, "seq", split_axis=0, concat_axis=0, tiled=True)


def on_device(
    tokens,
    cotangent,
    query_weight,
    key_weight,
    value_weight,
    output_weight,
    gate_weight,
    up_weight,
    down_weight,
    attention_gain,
    feedforward_gain,
    lengths,
    token_order,
    real_token,
):
    x, c = tokens[0], cotangent[0]
    rows, width = x.shape
    slots = lax.axis_size("seq")
    shards = lax.axis_size("fsdp")
    seq, shard = lax.axis_index("seq"), lax.axis_index("fsdp")
    direct = slots == 8 and shards == 4
    heads = width // slots // HD
    own_width = heads * HD
    shard_rows = width // shards
    halves = 2 if direct else 1

    own_columns = [
        lax.dynamic_slice_in_dim(w, seq * own_width, own_width, axis=1)
        for w in (query_weight, key_weight, value_weight)
    ]
    gains = jnp.stack([attention_gain, feedforward_gain], axis=1)
    own_columns = jnp.concatenate(
        [jnp.pad(w, ((0, 0), (0, LANES - own_width))) for w in own_columns]
        + [jnp.pad(gains, ((0, 0), (0, LANES - 2)))],
        axis=1,
    )
    qkv_weight = jnp.concatenate([query_weight, key_weight, value_weight], axis=1)

    if direct:
        w_rows = shard ^ jnp.arange(shards, dtype=jnp.int32)
        place = seq // 2
        half = shard_rows // 2
        hidden = gate_weight.shape[1] // 2
        columns_x = flip(own_columns, "fsdp", 2)
        beside = flip(x, "seq", 1)
        near = move_chain(x, [(0, 1), (1, 0), (2, 3), (3, 2)])
        inner = move_chain(x, [(1, 2), (2, 1)])
        output_x = flip(output_weight, "fsdp", 2)
        both = jnp.stack([own_columns, columns_x])
        both_c = flip(both, "fsdp", 1)
        column_arrays = [both, both_c]
        column_layout = ((0, 0), (1, 0), (0, 1), (1, 1))
        near, inner, _ = lax.optimization_barrier((near, inner, beside))
        far_inner = move_chain(near, [(1, 2), (2, 1)])
        far_outer = move_chain(inner, [(1, 0), (2, 3)])
        near_beside = flip(near, "seq", 1)
        far_half = (1 - shard // 2) * hidden
        near_half = (shard // 2) * hidden
        up_own, up_sent = [
            jnp.concatenate(
                [
                    lax.dynamic_slice_in_dim(after(w, own_columns), start, hidden, axis=1)
                    for w in (gate_weight, up_weight)
                ],
                axis=1,
            )
            for start in (near_half, far_half)
        ]
        up_x1 = flip(after(up_sent[:half], near), "fsdp", 2)
        token_order = after(token_order, near)
        is_inner = (place == 1) | (place == 2)
        block_slots = [seq ^ d for d in range(slots)]
    else:
        w_rows = jnp.zeros((1,), jnp.int32)
        column_arrays = [lax.all_gather(own_columns, "fsdp", axis=0, tiled=True)[None]]
        column_layout = ((0, 0),)
        gathered = lax.all_gather(x, "seq", axis=0)
        x_blocks = [gathered[i] for i in range(slots)]
        block_slots = [jnp.asarray(i, jnp.int32) for i in range(slots)]

    codes = token_codes(lengths[0], token_order[0], real_token[0])
    gain_pieces = jnp.stack(
        [column_arrays[a][i, :, 3 * LANES : 3 * LANES + 2] for a, i in column_layout]
    )
    gain_rows = jnp.take(gain_pieces, w_rows, axis=0).reshape(width, 2)
    gain_1, gain_2 = gain_rows[:, 0].reshape(1, width), gain_rows[:, 1].reshape(1, width)
    state = None

    def project_block(number, block, state):
        slot = block_slots[number].reshape(1).astype(jnp.int32)
        return project(
            slot,
            w_rows,
            slots,
            heads,
            lengths.shape[1],
            block,
            column_layout,
            column_arrays,
            codes,
            state,
        )

    if direct:
        state = project_block(0, x, state)
        state = project_block(1, beside, state)
        far_inner, far_outer, _, _, _, _ = lax.optimization_barrier(
            (far_inner, far_outer, near_beside, up_x1, output_x, state[0])
        )
        third = move_chain(far_inner, [(1, 0), (2, 3)])
        far = jnp.where(is_inner, far_inner, far_outer)
        far_beside = flip(far, "seq", 1)
        up_x2 = flip(after(up_sent[half:], far_inner), "fsdp", 2)
        up_c = flip(after(up_own, far_inner), "fsdp", 1)
        state = project_block(2, near, state)
        state = project_block(3, near_beside, state)
        state = project_block(4, far, state)
        third, _, _, _, _ = lax.optimization_barrier(
            (third, far_beside, up_x2, up_c, state[0])
        )
        cross = jnp.where(is_inner, inner, third)
        cross_beside = flip(cross, "seq", 1)
        c_x = flip(after(c, cross), "fsdp", 2)
        up_xc1 = flip(after(up_x1, cross), "fsdp", 1)
        down_c = flip(after(down_weight, cross), "fsdp", 1)
        state = project_block(5, far_beside, state)
        state = project_block(6, cross, state)
        cross_beside, _, _, _ = lax.optimization_barrier((cross_beside, c_x, up_xc1, down_c))
        state = project_block(7, cross_beside, state)
    else:
        for number, block in enumerate(x_blocks):
            state = project_block(number, block, state)
    qa, ka, va, h1, own_scores = state

    att, sums, qb, own_weights = attend(qa, ka, va, own_scores, parts_of(slots * rows), slots)
    if direct:
        qkv_x = flip(after(qkv_weight, qa), "fsdp", 2)
        up_xc2 = flip(after(up_x2, qa), "fsdp", 1)
        output_c = flip(after(output_weight, qa), "fsdp", 1)
        output_xc = flip(after(output_x, qa), "fsdp", 1)
        att = lax.optimization_barrier((att, up_xc2, output_c, output_xc))[0]
    if direct:
        output_pieces = [output_weight, output_c, output_x, output_xc]
        output_entries = [(0, p, 0, p, shard_rows, 0, 0) for p in range(4)]
        d_rows = (shard % 2) ^ jnp.arange(2, dtype=jnp.int32)
        ff_sources = [up_own, up_c, up_x1, up_x2, up_xc1, up_xc2, down_weight, down_c]
        ff_entries = [
            (kind, source, 0, place, shard_rows, offset, kind * hidden)
            for kind in range(2)
            for source, place, offset in (
                (0, 0, 0), (1, 1, 0), (2, 2, 0), (3, 2, half), (4, 3, 0), (5, 3, half),
            )
        ] + [(2, 6, 1, 0, down_weight.shape[0], 0, 0), (2, 7, 1, 1, down_weight.shape[0], 0, 0)]
    else:
        output_pieces = [lax.all_gather(output_weight, "fsdp", axis=0, tiled=True)]
        output_entries = [(0, 0, 0, 0, width, 0, 0)]
        d_rows = w_rows
        ff_sources = [
            lax.all_gather(w, "fsdp", axis=0, tiled=True)
            for w in (gate_weight, up_weight, down_weight)
        ]
        hidden = gate_weight.shape[1]
        ff_entries = [(i, i, 0, 0, width, 0, 0) for i in range(3)]
    att_parts = [turn(att.reshape(slots, rows, LANES))]
    if direct:
        x, _ = lax.optimization_barrier((x, qkv_x))
    total = rows * slots
    sums = sums.reshape(total, LANES)
    qb = qb.reshape(heads, total, LANES)

    middle, h2, att = pre_stage(w_rows, att_parts, x, gain_2, output_entries, output_pieces)
    if direct:
        h2s, cs = [h2, flip(h2, "fsdp", 2)], [c, c_x]
    else:
        h2s, cs = [h2], [c]
    outs, backs, gu, dg = main_stage(
        w_rows, d_rows, h2s, cs, hidden, ff_entries, ff_sources, halves
    )
    if direct:
        line = Line()
        backs[1] = flip(backs[1], "fsdp", 2)
        up_r = Reduction(*gu, line)
        down_r = Reduction(dg[0][0], dg[1][0], line)
        up_r.core()
        down_r.core()
        up_r.halve(1)
        down_r.halve(2)
        backs[1] = lax.optimization_barrier((backs[1], up_r.own, down_r.own))[0]
    d_middle, branch, d_att = post_stage(
        w_rows, middle, backs, c, gain_2, slots, output_entries, output_pieces
    )
    og = out_terms(w_rows, att, branch, halves)
    grad_blocks = turn(d_att)
    parts = 4
    back = functools.partial(attend_back, qb, ka, va, own_weights)
    if direct:
        qkv_c = flip(after(qkv_weight, d_att), "fsdp", 1)
        output_r = Reduction(*og, line)
        down_r.hold(d_att)
        down_r.halve(1)
        output_r.core()
        up_r.hold(d_att)
        up_r.halve(2)
        grad_blocks = lax.optimization_barrier(
            (grad_blocks, down_r.own, up_r.own, qkv_c)
        )[0]
    else:
        qkv_pieces = [lax.all_gather(qkv_weight, "fsdp", axis=0, tiled=True)]
    kv_0, dq, gb = back(0, parts, slots, sums, grad_blocks, None)
    if direct:
        for r in (down_r, up_r, output_r):
            r.hold(kv_0)
        down_r.halve(4)
        up_r.halve(4)
        output_r.across()
        outs[1] = flip(after(outs[1], kv_0), "fsdp", 2)
        qkv_xc = flip(after(qkv_x, kv_0), "fsdp", 1)
        qkv_pieces = [qkv_weight, qkv_c, qkv_x, qkv_xc]
        gb = lax.optimization_barrier((gb, down_r.own, up_r.own, output_r.own))[0]
    kv_1, dq = back(1, parts, slots, None, None, (gb, dq))
    kv_early = turn(jnp.concatenate([kv_0, kv_1], axis=2))
    if direct:
        for r in (down_r, up_r, output_r):
            r.hold(kv_1)
        up_r.swap_columns()
        down_r.settle()
        down_r.widen(4)
        output_r.halve(2)
        gb = lax.optimization_barrier((gb, down_r.own, up_r.own, output_r.own, qkv_xc, outs[1]))[0]
    kv_2, dq = back(2, parts, slots, None, None, (gb, dq))
    if direct:
        for r in (down_r, up_r, output_r):
            r.hold(kv_2)
        up_r.join_columns()
        up_r.widen(4)
        down_r.widen(1)
        output_r.halve(1)
        gb = lax.optimization_barrier((gb, down_r.own, up_r.own, output_r.own))[0]
    kv_3, dq = back(3, parts, slots, None, None, (gb, dq))
    kv_late = jnp.concatenate([kv_2, kv_3], axis=2)
    late = turn(jnp.concatenate([kv_late.reshape(slots, rows, LANES), dq], axis=1))
    kv_late = late[:, :rows].reshape(kv_late.shape)
    dq_turned = late[:, rows:]
    if direct:
        for r in (down_r, up_r, output_r):
            r.hold(kv_3)
        up_r.widen(2)
        down_r.widen(2)
        dq = lax.optimization_barrier((dq, down_r.own, up_r.own, kv_early))[0]
    layer_out = (middle + sum(part.astype(f32) for part in outs)).astype(bf16)
    own = own_terms(w_rows, h1, dq, [kv_0, kv_1, kv_2, kv_3], shards, halves)
    if direct:
        own_r = Reduction(*own, line)
        own_r.core()
        for r in (up_r, output_r):
            r.hold(own[0])
        up_r.widen(1)
        output_r.halve(4)
        own_r.across()
        output_r.settle()
        output_r.widen(4)
        output_r.widen(1)
        own_r.settle()
        own_r.own = after(own_r.own[None], down_r.arrived)
        own_r.widen(4)
        output_r.widen(2)
        own_r.widen(1)
        own_r.arrived = after(own_r.arrived, late)
        own_r.widen(2)
        input_grad = last_stage(
            w_rows, dq_turned, [kv_early, kv_late], x, d_middle, gain_1, qkv_pieces
        )
        for r in (up_r, down_r, output_r):
            r.join()
        gate_grad, up_grad = up_r.own[:, : 2 * hidden], up_r.own[:, 2 * hidden :]
        down_grad, output_grad = down_r.own, output_r.own
        query_grad, key_grad, value_grad, attention_gain_grad = finish_own(
            ((seq // 2) % 2).reshape(1).astype(jnp.int32),
            own_r.own,
            own_r.arrived,
            qkv_weight,
            attention_gain.reshape(shard_rows, 1),
        )
        attention_gain_grad = attention_gain_grad.reshape(shard_rows)
    else:
        own_share = lax.psum_scatter(own[0][0], "fsdp", scatter_dimension=0, tiled=True)
        all_shares = lax.all_gather(own_share, "seq", axis=0)
        gate_grad, up_grad, down_grad, output_grad = [
            lax.psum(lax.psum_scatter(g, "fsdp", scatter_dimension=0, tiled=True), "seq")
            for g in (gu[0][0, :, :hidden], gu[0][0, :, hidden:], dg[0][0], og[0][0])
        ]
    def gain_grad(terms, gain):
        summed = sum(jnp.sum(g * w.astype(f32), axis=1) for g, w in terms)
        return summed / gain.astype(f32)

    if not direct:
        all_shares = all_shares.reshape(slots, shard_rows, 3, LANES)[..., :own_width].astype(f32)
        query_grad, key_grad, value_grad = [
            all_shares[:, :, i, :].transpose(1, 0, 2).reshape(shard_rows, width) for i in range(3)
        ]
        input_grad = last_stage(
            w_rows, dq_turned, [kv_early, kv_late], x, d_middle, gain_1, qkv_pieces
        )
        attention_gain_grad = gain_grad(
            ((query_grad, query_weight), (key_grad, key_weight), (value_grad, value_weight)),
            attention_gain,
        )
    output_grad, gate_grad, up_grad, down_grad = [
        g.astype(f32) for g in (output_grad, gate_grad, up_grad, down_grad)
    ]
    feedforward_gain_grad = gain_grad(
        ((gate_grad, gate_weight), (up_grad, up_weight)), feedforward_gain
    )
    return (
        layer_out[None],
        input_grad[None],
        query_grad,
        key_grad,
        value_grad,
        output_grad,
        gate_grad,
        up_grad,
        down_grad,
        attention_gain_grad,
        feedforward_gain_grad,
    )


def solution(mesh):
    in_specs = (
        P("fsdp", "seq", None),
        P("fsdp", "seq", None),
        P("fsdp", None),
        P("fsdp", None),
        P("fsdp", None),
        P("fsdp", None),
        P("fsdp", None),
        P("fsdp", None),
        P("fsdp", None),
        P("fsdp"),
        P("fsdp"),
        P("fsdp", None),
        P("fsdp", None),
        P("fsdp", None),
    )
    out_specs = (
        P("fsdp", "seq", None),
        P("fsdp", "seq", None),
        P("fsdp", None),
        P("fsdp", None),
        P("fsdp", None),
        P("fsdp", None),
        P("fsdp", None),
        P("fsdp", None),
        P("fsdp", None),
        P("fsdp"),
        P("fsdp"),
    )
    return jax.shard_map(
        on_device, mesh=mesh, in_specs=in_specs, out_specs=out_specs, check_vma=False
    )
```

```python
import functools

import jax
import jax.numpy as jnp
from jax import lax
from jax.experimental import pallas as pl
from jax.experimental.pallas import tpu as pltpu
from jax.sharding import PartitionSpec as P

HD = 64
LANES = 128
EPSILON = 1e-06
BLOCKED = -(2.0**100)
ROOT_2_PI = 0.7978845608028654
CUBIC = 0.044715
VMEM_LIMIT = 60 * 1024 * 1024

bf16 = jnp.bfloat16
f32 = jnp.float32


def mm(a, b):
    return jnp.dot(a, b, preferred_element_type=f32)


def mm_nt(a, b):
    return lax.dot_general(a, b, (((1,), (1,)), ((), ())), preferred_element_type=f32)


def mm_tn(a, b):
    return lax.dot_general(a, b, (((0,), (0,)), ((), ())), preferred_element_type=f32)


def params(**extra):
    return pltpu.CompilerParams(vmem_limit_bytes=VMEM_LIMIT, **extra)


def cost(flops, moved, transcendentals=0):
    return pl.CostEstimate(
        flops=int(flops), bytes_accessed=int(moved), transcendentals=int(transcendentals)
    )


def vmem():
    return pl.BlockSpec(memory_space=pltpu.VMEM)


def anywhere():
    return pl.BlockSpec(memory_space=pl.ANY)


def smem():
    return pl.BlockSpec(memory_space=pltpu.SMEM)


def lane_ids(rows):
    return lax.broadcasted_iota(jnp.int32, (rows, LANES), 1)


def split3(column):
    high = column.astype(bf16)
    rest = column - high.astype(f32)
    middle = rest.astype(bf16)
    low = (rest - middle.astype(f32)).astype(bf16)
    return (high.astype(f32), middle.astype(f32), low.astype(f32))


def project_kernel(heads, segments, layout, aliased, *refs):
    w_rows, x_ref = refs[1:3]
    arrays = 1 + max(array for array, _ in layout)
    w_refs = refs[3 : 3 + arrays]
    code_ref = refs[3 + arrays]
    qa_ref, ka_ref, va_ref, h1_ref, own_ref, gain_row = refs[4 + arrays + aliased :]
    piece_rows = w_refs[0].shape[1]
    spans = []
    for piece, (array, index) in enumerate(layout):
        at = pl.ds(pl.multiple_of(w_rows[piece] * piece_rows, piece_rows), piece_rows)
        spans.append(at)
        columns = w_refs[array][index, :, 3 * LANES :].astype(f32)
        gain_row[:, at] = columns.T[0:8, :]
    x = x_ref[...].astype(f32)
    scaling = lax.rsqrt(jnp.mean(x * x, axis=-1, keepdims=True) + EPSILON)
    h1_ref[...] = (x * scaling * gain_row[0:1, :]).astype(bf16)
    qkv = None
    for at, (array, index) in zip(spans, layout):
        part = mm(h1_ref[:, at], w_refs[array][index, :, : 3 * LANES])
        qkv = part if qkv is None else qkv + part
    rows = x.shape[0]
    lane = lane_ids(rows)
    q = qkv[:, :LANES].astype(bf16) * jnp.asarray(HD**-0.5, bf16)
    k = qkv[:, LANES : 2 * LANES].astype(bf16)
    v = qkv[:, 2 * LANES :].astype(bf16)
    place = lane % HD
    code = code_ref[...]
    same = place == code // 2
    padded = code % 2 == 0
    q_table = jnp.where(same | ((place == HD - 1) & padded), 1.0, 0.0).astype(bf16)
    k_table = jnp.where(
        place < segments,
        jnp.where(same & ~padded, 0.0, BLOCKED),
        jnp.where((place >= HD - 4) & (place < HD - 1), 1.0, 0.0),
    ).astype(bf16)
    ones = jnp.ones((rows, LANES), bf16)
    product = q.astype(f32) * k.astype(f32)
    for head in range(heads):
        own = lane // HD == head
        qa_ref[head] = jnp.where(own, q, q_table)
        ka_ref[head] = jnp.where(own, k, k_table)
        va_ref[head] = jnp.where(own, v, ones)
        score = jnp.sum(jnp.where(own, product, 0.0), axis=-1, keepdims=True)
        score = jnp.where(padded, score, 4.0 * BLOCKED)
        own_ref[head] = jnp.broadcast_to(score, (rows, LANES))


def project(slot, w_rows, slots, heads, segments, x, layout, arrays, codes, previous):
    rows, width = x.shape
    total = rows * slots
    head_spec = pl.BlockSpec((heads, rows, LANES), lambda i, s, w: (0, s[0], 0))
    shapes = [jax.ShapeDtypeStruct((heads, total, LANES), bf16)] * 3 + [
        jax.ShapeDtypeStruct((total, width), bf16),
        jax.ShapeDtypeStruct((heads, total, LANES), f32),
    ]
    extra = () if previous is None else tuple(previous)
    first = 4 + len(arrays)
    return pl.pallas_call(
        functools.partial(project_kernel, heads, segments, layout, len(extra)),
        grid_spec=pltpu.PrefetchScalarGridSpec(
            num_scalar_prefetch=2,
            grid=(1,),
            in_specs=[pl.BlockSpec((rows, width), lambda i, s, w: (0, 0))]
            + [pl.BlockSpec(a.shape, lambda i, s, w: (0, 0, 0)) for a in arrays]
            + [pl.BlockSpec((rows, 1), lambda i, s, w: (s[0], 0))]
            + [anywhere()] * len(extra),
            out_specs=[head_spec] * 3
            + [pl.BlockSpec((rows, width), lambda i, s, w: (s[0], 0)), head_spec],
            scratch_shapes=[pltpu.VMEM((8, width), f32)],
        ),
        out_shape=shapes,
        input_output_aliases={first + i: i for i in range(len(extra))},
        compiler_params=params(),
        cost_estimate=cost(2 * rows * width * 3 * LANES, 4 * rows * width + 8 * LANES * width),
        name="project",
    )(slot, w_rows, x, *arrays, codes, *extra)


def tile_of(total):
    return total if total <= 2560 else 512


def forward_kernel(
    heads, step, q_ref, own_ref, v_near, k_ref, v_ref,
    att_ref, sum_ref, qb_ref, weight_ref, scores, tops, acc,
):
    pack, rows = q_ref.shape[1], q_ref.shape[3]
    span = pack * rows
    total = k_ref.shape[1]
    lane = lane_ids(span)
    folds = step // LANES

    def queries(head):
        return q_ref[head].reshape(span, LANES)

    def find(head, at):
        found = mm_nt(queries(head), k_ref[head, at, :])
        scores[head, :, at] = found
        top = tops[head]
        for fold in range(folds):
            top = jnp.maximum(top, found[:, fold * LANES : (fold + 1) * LANES])
        tops[head] = top

    def mix(head, at):
        top = tops[head]
        shifted = scores[head, :, at] - jnp.concatenate([top] * folds, axis=1)
        acc[head] += mm(jnp.exp(shifted).astype(bf16), v_ref[head, at, :])

    def settle(head):
        top = jnp.max(tops[head], axis=-1, keepdims=True)
        tops[head] = jnp.maximum(
            jnp.broadcast_to(top, (span, LANES)), own_ref[head].reshape(span, LANES)
        )

    def sweep(first, second):
        def run(number, carry):
            at = pl.ds(pl.multiple_of(number * step, step), step)
            if second is not None:
                mix(second, at)
            if first is not None:
                find(first, at)
            return carry

        lax.fori_loop(0, total // step, run, 0)
        if first is not None:
            settle(first)

    tops[...] = jnp.full_like(tops, 4.0 * BLOCKED)
    acc[...] = jnp.zeros_like(acc)
    for head in range(heads + 1):
        sweep(head if head < heads else None, head - 1 if head > 0 else None)
    merged = None
    for head in range(heads):
        own = lane // HD == head
        other = HD if head == 0 else 0
        top = tops[head]
        value = v_near[head].reshape(span, LANES).astype(f32)
        own_weight = jnp.exp(own_ref[head].reshape(span, LANES) - top).astype(bf16).astype(f32)
        mixed = acc[head] + own_weight * value
        swapped = pltpu.roll(mixed, HD, axis=1)
        weight_sum = jnp.where(own, swapped, mixed)
        inverse = 1.0 / weight_sum
        weight_ref[head] = (own_weight * inverse).astype(bf16).reshape(pack, 1, rows, LANES)
        log_total = top + jnp.log(weight_sum)
        mixed = mixed * inverse
        merged = mixed if merged is None else jnp.where(own, mixed, merged)
        filled = queries(head).astype(f32)
        for place, part in enumerate(split3(-log_total)):
            filled = jnp.where(lane == other + HD - 4 + place, part, filled)
        qb_ref[head] = filled.astype(bf16).reshape(pack, 1, rows, LANES)
    att_ref[...] = merged.astype(bf16).reshape(pack, 1, rows, LANES)
    sum_ref[...] = merged.reshape(pack, 1, rows, LANES)


def attend(qa, ka, va, own, parts, slots):
    heads, total, _ = qa.shape
    rows = total // slots // parts
    shape = (heads, slots, parts, rows, LANES)
    view = [a.reshape(shape) for a in (qa, own, va)]
    block = pl.BlockSpec((heads, slots, 1, rows, LANES), lambda i: (0, 0, i, 0, 0))
    whole = pl.BlockSpec(ka.shape, lambda i: (0, 0, 0))
    flat = pl.BlockSpec((slots, 1, rows, LANES), lambda i: (0, i, 0, 0))
    span = slots * rows
    return pl.pallas_call(
        functools.partial(forward_kernel, heads, tile_of(total)),
        grid=(parts,),
        in_specs=[block, block, block, whole, whole],
        out_specs=[flat, flat, block, block],
        out_shape=[
            jax.ShapeDtypeStruct(shape[1:], bf16),
            jax.ShapeDtypeStruct(shape[1:], f32),
            jax.ShapeDtypeStruct(shape, bf16),
            jax.ShapeDtypeStruct(shape, bf16),
        ],
        scratch_shapes=[
            pltpu.VMEM((heads, span, total), f32),
            pltpu.VMEM((heads, span, LANES), f32),
            pltpu.VMEM((heads, span, LANES), f32),
        ],
        compiler_params=params(),
        cost_estimate=cost(
            8 * heads * total * total * LANES, 4 * heads * total * LANES, heads * total * total
        ),
        name="attend",
    )(*view, ka, va)


def backward_kernel(heads, part, parts, tile, *refs):
    first, last = part == 0, part == parts - 1
    qb_ref, k_ref, v_ref, weight_ref = refs[:4]
    if first:
        sum_ref, grad_ref, kv_ref, dq_ref, gb_ref, dk_acc, dv_acc = refs[4:]
        dq_acc = dq_ref
    elif last:
        gb_ref, dq_in, kv_ref, dq_ref, dq_acc, dk_acc, dv_acc = refs[4:]
    else:
        gb_ref, dq_in, kv_ref, dq_ref, dk_acc, dv_acc = refs[4:]
        dq_acc = dq_ref
    slots, rows = k_ref.shape[1], k_ref.shape[3]
    total = qb_ref.shape[1]
    span = slots * rows
    pack = slots
    if first:
        block_rows = grad_ref.shape[1]
        lane = lane_ids(block_rows)

        def prepare(slot, carry):
            at = pl.ds(pl.multiple_of(slot * block_rows, block_rows), block_rows)
            grad = grad_ref[slot].astype(f32)
            product = grad * sum_ref[at, :]
            for head in range(heads):
                other = HD if head == 0 else 0
                own = lane // HD == head
                delta = jnp.sum(jnp.where(own, product, 0.0), axis=-1, keepdims=True)
                filled = jnp.where(own, grad, 0.0)
                for place, piece in enumerate(split3(-delta)):
                    filled = jnp.where(lane == other + place, piece, filled)
                gb_ref[head, at, :] = filled.astype(bf16)
                dq_acc[head, at, :] = jnp.zeros((block_rows, LANES), f32)
            return carry

        lax.fori_loop(0, slots, prepare, 0)
    else:
        dq_acc[...] = dq_in[...]
    width = pack * rows
    lane = lane_ids(width)
    for index in range(slots // pack):
        keys = slice(index * pack, (index + 1) * pack)
        dk_acc[...] = jnp.zeros_like(dk_acc)
        dv_acc[...] = jnp.zeros_like(dv_acc)

        def step(number, carry):
            at = pl.ds(pl.multiple_of(number * tile, tile), tile)
            for head in range(heads):
                key = k_ref[head, keys].reshape(width, LANES)
                value = v_ref[head, keys].reshape(width, LANES)
                q = qb_ref[head, at, :]
                g = gb_ref[head, at, :]
                weights = jnp.exp(mm_nt(key, q))
                inner = mm_nt(value, g)
                score_grad = (weights * inner).astype(bf16)
                dv_acc[head] += mm(weights.astype(bf16), g)
                dk_acc[head] += mm(score_grad, q)
                dq_acc[head, at, :] += mm_tn(score_grad, key)
            return carry

        lax.fori_loop(0, total // tile, step, 0)
        dk_all, dv_all = None, None
        for head in range(heads):
            own = lane // HD == head
            starts = [
                slot * (total // slots) + part * rows
                for slot in range(index * pack, (index + 1) * pack)
            ]
            q = jnp.concatenate([qb_ref[head, b : b + rows, :] for b in starts], axis=0).astype(f32)
            g = jnp.concatenate([gb_ref[head, b : b + rows, :] for b in starts], axis=0).astype(f32)
            k = k_ref[head, keys].reshape(width, LANES).astype(f32)
            v = v_ref[head, keys].reshape(width, LANES).astype(f32)
            weight = weight_ref[head, keys].reshape(width, LANES).astype(f32)
            inner = jnp.sum(v * g, axis=-1, keepdims=True)
            score_grad = (weight * inner).astype(bf16).astype(f32)
            dk = dk_acc[head] + score_grad * q
            dv = dv_acc[head] + weight * g
            dq = score_grad * k
            for place, b in enumerate(starts):
                dq_acc[head, b : b + rows, :] += dq[place * rows : (place + 1) * rows, :]
            dk_all = dk if head == 0 else jnp.where(own, dk, dk_all)
            dv_all = dv if head == 0 else jnp.where(own, dv, dv_all)
        kv_ref[keys, 0] = dk_all.astype(bf16).reshape(pack, rows, LANES)
        kv_ref[keys, 1] = dv_all.astype(bf16).reshape(pack, rows, LANES)
    if last:
        block_rows = total // slots
        lane = lane_ids(block_rows)
        for slot in range(slots):
            at = slice(slot * block_rows, (slot + 1) * block_rows)
            dq = dq_acc[0, at, :]
            if heads == 2:
                dq = jnp.where(lane < HD, dq, dq_acc[1, at, :])
            dq_ref[slot] = (dq * HD**-0.5).astype(bf16)


def attend_back(qb, ka, va, weights, part, parts, slots, sums, grads, state):
    heads, total, _ = ka.shape
    rows = total // slots // parts
    first, last = part == 0, part == parts - 1
    shape = (heads, slots, parts, rows, LANES)
    near = pl.BlockSpec((heads, slots, 1, rows, LANES), lambda i: (0, 0, part, 0, 0))
    wide = pl.BlockSpec((heads, total, LANES), lambda i: (0, 0, 0))
    pack = slots
    accumulator = pltpu.VMEM((heads, pack * rows, LANES), f32)
    if first:
        inputs = [sums, grads]
        in_specs = [
            pl.BlockSpec((total, LANES), lambda i: (0, 0)),
            pl.BlockSpec(grads.shape, lambda i: (0, 0, 0)),
        ]
    else:
        inputs, in_specs = list(state), [wide, wide]
    out_shape = [jax.ShapeDtypeStruct((slots, 2, rows, LANES), bf16)]
    out_specs = [pl.BlockSpec((slots, 2, rows, LANES), lambda i: (0, 0, 0, 0))]
    scratch = [accumulator, accumulator]
    if last:
        out_shape.append(jax.ShapeDtypeStruct((slots, total // slots, LANES), bf16))
        out_specs.append(pl.BlockSpec((slots, total // slots, LANES), lambda i: (0, 0, 0)))
        scratch = [pltpu.VMEM((heads, total, LANES), f32)] + scratch
    else:
        out_shape.append(jax.ShapeDtypeStruct((heads, total, LANES), f32))
        out_specs.append(wide)
    if first:
        out_shape.append(jax.ShapeDtypeStruct((heads, total, LANES), bf16))
        out_specs.append(wide)
    return pl.pallas_call(
        functools.partial(backward_kernel, heads, part, parts, tile_of(total)),
        grid=(1,),
        in_specs=[wide, near, near, near] + in_specs,
        out_specs=out_specs,
        out_shape=out_shape,
        scratch_shapes=scratch,
        compiler_params=params(),
        cost_estimate=cost(
            20 * heads * total * total * LANES // parts,
            12 * heads * total * LANES,
            heads * total * total // parts,
        ),
        name="attend_back",
    )(qb, ka.reshape(shape), va.reshape(shape), weights.reshape(shape), *inputs)


def own_kernel(halves, *refs):
    w_rows, h_ref, dq_ref = refs[:3]
    parts = len(refs) - 4 - halves
    kv_refs, outs, term = refs[3 : 3 + parts], refs[3 + parts : -1], refs[-1]
    slots, _, rows, width = h_ref.shape
    summed = None
    for part in range(parts):
        span = slots * rows
        grads = [dq_ref[:, part * rows : (part + 1) * rows]] + [
            kv_refs[part][:, kind] for kind in range(2)
        ]
        grads = jnp.concatenate([g.reshape(span, LANES) for g in grads], axis=1)
        piece = mm_tn(h_ref[:, part].reshape(span, width), grads)
        summed = piece if summed is None else summed + piece
    term[...] = summed.astype(bf16)
    place_rows(halves, w_rows, term, outs)


def place_rows(halves, w_rows, source, outs):
    inner, step_rows = outs[0].shape[0], outs[0].shape[1]
    for half in range(halves):
        for index in range(inner):
            piece = index * halves + half
            at = pl.ds(pl.multiple_of(w_rows[piece] * step_rows, step_rows), step_rows)
            outs[half][index] = source[at, :]


def own_terms(w_rows, h1, dq, kvs, shards, halves):
    slots, rows = kvs[0].shape[0], kvs[0].shape[2]
    width = h1.shape[1]
    pieces = shards if halves == 2 else 1
    shape = jax.ShapeDtypeStruct((pieces // halves, width // pieces, 3 * LANES), bf16)
    return pl.pallas_call(
        functools.partial(own_kernel, halves),
        in_specs=[smem()] + [vmem()] * (2 + len(kvs)),
        out_specs=[vmem()] * halves,
        out_shape=[shape] * halves,
        scratch_shapes=[pltpu.VMEM((width, 3 * LANES), bf16)],
        compiler_params=params(),
        cost_estimate=cost(2 * h1.size * 3 * LANES, 2 * h1.size),
        name="own_terms",
    )(w_rows, h1.reshape(slots, len(kvs), rows, width), dq, *kvs)


def load_rows(entries, sources, targets, sems, rows_of):
    started = [[] for _ in targets]
    for number, (target, source, index, place, step_rows, offset, column) in enumerate(entries):
        begin = pl.multiple_of(rows_of[index][place] * step_rows + offset, 16)
        at = pl.ds(begin, sources[source].shape[0])
        width = targets[target].shape[1]
        copy = pltpu.make_async_copy(
            sources[source].at[:, column : column + width],
            targets[target].at[at, :],
            sems.at[number],
        )
        copy.start()
        started[target].append(copy)
    return started


def store_rows(source, targets, sems, index, columns, shift=0):
    moved = columns if shift == 0 else pl.ds(shift + columns.start, columns.size)
    copies = []
    halves = len(targets)
    for piece in range(halves * targets[0].shape[0]):
        step_rows = targets[0].shape[1]
        at = pl.ds(pl.multiple_of(index[piece] * step_rows, step_rows), step_rows)
        target = targets[piece % halves].at[piece // halves, :, moved]
        copies.append(pltpu.make_async_copy(source.at[at, columns], target, sems.at[piece]))
    return copies


def pre_kernel(parts, entries, *refs):
    w_rows = refs[0]
    att_refs = refs[1 : 1 + parts]
    x_ref, gain_ref = refs[1 + parts : 3 + parts]
    sources = refs[3 + parts : -5]
    mid_ref, h2_ref, att_ref, wo, sems = refs[-5:]
    loads = load_rows(entries, sources, (wo,), sems, (w_rows,))
    rows, width = x_ref.shape
    blocks = att_refs[0].shape[0]
    block_width = width // blocks
    part_rows = rows // parts
    for part in range(parts):
        for block in range(blocks):
            att_ref[
                part * part_rows : (part + 1) * part_rows,
                block * block_width : (block + 1) * block_width,
            ] = att_refs[part][block][:, :block_width]
    for copy in loads[0]:
        copy.wait()
    middle = x_ref[...].astype(f32) + mm(att_ref[...], wo[...])
    scaling = lax.rsqrt(jnp.mean(middle * middle, axis=-1, keepdims=True) + EPSILON)
    h2_ref[...] = (middle * scaling * gain_ref[...].astype(f32)).astype(bf16)
    mid_ref[...] = middle


def pre_stage(w_rows, att_parts, x, gain, entries, sources):
    rows, width = x.shape
    hbm = pl.BlockSpec(memory_space=pltpu.HBM)
    return pl.pallas_call(
        functools.partial(pre_kernel, len(att_parts), entries),
        in_specs=[smem()] + [vmem()] * (len(att_parts) + 2) + [hbm] * len(sources),
        out_specs=[vmem()] * 3,
        out_shape=[
            jax.ShapeDtypeStruct((rows, width), f32),
            jax.ShapeDtypeStruct((rows, width), bf16),
            jax.ShapeDtypeStruct((rows, width), bf16),
        ],
        scratch_shapes=[
            pltpu.VMEM((width, width), bf16),
            pltpu.SemaphoreType.DMA((len(entries),)),
        ],
        compiler_params=params(),
        cost_estimate=cost(2 * rows * width * width, 2 * width * width),
        name="pre_stage",
    )(w_rows, *att_parts, x, gain, *sources)


def main_kernel(groups, halves, entries, count, *refs):
    w_rows, d_rows = refs[:2]
    h2_refs, c_refs = refs[2 : 2 + groups], refs[2 + groups : 2 + 2 * groups]
    refs = refs[2 + 2 * groups :]
    sources, refs = refs[:count], refs[count:]
    out_refs, back_refs = refs[:groups], refs[groups : 2 * groups]
    refs = refs[2 * groups :]
    gu_refs, dg_refs = refs[:halves], refs[halves : 2 * halves]
    refs = refs[2 * halves :]
    wg, wu, wd, gg, ug, dg, h2_all, h2t, c_all, acc_out, acc_back, in_sems, out_sems = refs
    loads = load_rows(entries, sources, (wg, wu, wd), in_sems, (w_rows, d_rows))
    rows = h2_refs[0].shape[0]
    for group in range(groups):
        span = slice(group * rows, (group + 1) * rows)
        h2_all[span, :] = h2_refs[group][...]
        c_all[span, :] = c_refs[group][...]
    h2t[...] = h2_all[...].T
    acc_out[...] = jnp.zeros_like(acc_out)
    acc_back[...] = jnp.zeros_like(acc_back)
    for started in loads:
        for copy in started:
            copy.wait()

    def columns_at(at):
        h2 = h2_all[...]
        c = c_all[...]
        gate = mm(h2, wg[:, at])
        up = mm(h2, wu[:, at])
        act_grad = mm_nt(c, wd[at, :])
        square = gate * gate
        bend = jnp.tanh(gate * (ROOT_2_PI + (ROOT_2_PI * CUBIC) * square))
        half = 0.5 * (1.0 + bend)
        curve = gate * half
        slope = half + (0.5 * gate) * (1.0 - bend * bend) * (
            ROOT_2_PI + (3.0 * ROOT_2_PI * CUBIC) * square
        )
        act = (curve * up).astype(bf16)
        d_up = (act_grad * curve).astype(bf16)
        d_gate = (act_grad * up * slope).astype(bf16)
        acc_back[...] += mm_nt(d_gate, wg[:, at]) + mm_nt(d_up, wu[:, at])
        gg[:, at] = mm(h2t[...], d_gate).astype(bf16)
        ug[:, at] = mm(h2t[...], d_up).astype(bf16)
        dg[at, :] = mm_tn(act, c).astype(bf16)
        acc_out[...] += mm(act, wd[at, :])
        for kind, source in ((0, gg), (1, ug)):
            for copy in store_rows(source, gu_refs, out_sems.at[kind], w_rows, at, kind * width):
                copy.start()

    width = wg.shape[1]
    step_width = 512
    whole = width // step_width

    def column_step(number, carry):
        columns_at(pl.ds(pl.multiple_of(number * step_width, step_width), step_width))
        return carry

    lax.fori_loop(0, whole, column_step, 0)
    if width % step_width:
        columns_at(pl.ds(whole * step_width, width % step_width))
    everything = slice(None)
    stores = store_rows(dg, dg_refs, out_sems.at[2], d_rows, everything)
    for copy in stores:
        copy.start()
    for group in range(groups):
        span = slice(group * rows, (group + 1) * rows)
        kind = out_refs[group].dtype
        out_refs[group][...] = acc_out[span, :].astype(kind)
        back_refs[group][...] = acc_back[span, :].astype(kind)
    whole = pl.ds(0, width)
    stores += store_rows(gg, gu_refs, out_sems.at[0], w_rows, whole)
    stores += store_rows(ug, gu_refs, out_sems.at[1], w_rows, whole, width)
    for copy in stores:
        copy.wait()


def main_stage(w_rows, d_rows, h2s, cs, hidden, entries, sources, halves):
    groups = len(h2s)
    rows, width = h2s[0].shape
    pieces, d_pieces = w_rows.shape[0], d_rows.shape[0]
    hbm = pl.BlockSpec(memory_space=pltpu.HBM)
    partial = [jax.ShapeDtypeStruct((rows, width), f32 if g == 0 else bf16) for g in range(groups)]
    up_shape = jax.ShapeDtypeStruct((pieces // halves, width // pieces, 2 * hidden), bf16)
    down_shape = jax.ShapeDtypeStruct((d_pieces // halves, hidden // d_pieces, width), bf16)
    total = groups * rows
    out = pl.pallas_call(
        functools.partial(main_kernel, groups, halves, entries, len(sources)),
        in_specs=[smem(), smem()] + [vmem()] * (2 * groups) + [hbm] * len(sources),
        out_specs=[vmem()] * (2 * groups) + [hbm] * (2 * halves),
        out_shape=partial * 2 + [up_shape] * halves + [down_shape] * halves,
        scratch_shapes=[
            pltpu.VMEM((width, hidden), bf16),
            pltpu.VMEM((width, hidden), bf16),
            pltpu.VMEM((hidden, width), bf16),
            pltpu.VMEM((width, hidden), bf16),
            pltpu.VMEM((width, hidden), bf16),
            pltpu.VMEM((hidden, width), bf16),
            pltpu.VMEM((total, width), bf16),
            pltpu.VMEM((width, total), bf16),
            pltpu.VMEM((total, width), bf16),
            pltpu.VMEM((total, width), f32),
            pltpu.VMEM((total, width), f32),
            pltpu.SemaphoreType.DMA((len(entries),)),
            pltpu.SemaphoreType.DMA((3, max(pieces, d_pieces))),
        ],
        compiler_params=params(),
        cost_estimate=cost(18 * total * width * hidden, 12 * width * hidden),
        name="main_stage",
    )(w_rows, d_rows, *h2s, *cs, *sources)
    outs, backs, grads = list(out[:groups]), list(out[groups : 2 * groups]), out[2 * groups :]
    return (outs, backs, grads[:halves], grads[halves:])


def post_kernel(groups, entries, count, *refs):
    w_rows, mid_ref = refs[:2]
    backs, refs = refs[2 : 2 + groups], refs[2 + groups :]
    c_ref, gain_ref = refs[:2]
    sources, refs = refs[2 : 2 + count], refs[2 + count :]
    dmid_ref, branch_ref, da_ref, wo, in_sems = refs
    loads = load_rows(entries, sources, (wo,), in_sems, (w_rows,))
    middle = mid_ref[...]
    scaling = lax.rsqrt(jnp.mean(middle * middle, axis=-1, keepdims=True) + EPSILON)
    incoming = sum(ref[...].astype(f32) for ref in backs) * gain_ref[...].astype(f32)
    centre = jnp.mean(incoming * middle, axis=-1, keepdims=True)
    d_middle = (
        c_ref[...].astype(f32)
        + scaling * incoming
        - middle * (scaling * scaling * scaling * centre)
    )
    dmid_ref[...] = d_middle
    branch = d_middle.astype(bf16)
    branch_ref[...] = branch
    for copy in loads[0]:
        copy.wait()
    d_att = mm_nt(branch, wo[...]).astype(bf16)
    blocks = da_ref.shape[0]
    block_width = d_att.shape[1] // blocks
    for block in range(blocks):
        piece = d_att[:, block * block_width : (block + 1) * block_width]
        if block_width < LANES:
            piece = jnp.concatenate([piece] * (LANES // block_width), axis=1)
        da_ref[block] = piece


def post_stage(w_rows, middle, backs, c, gain, slots, entries, sources):
    groups = len(backs)
    rows, width = middle.shape
    hbm = pl.BlockSpec(memory_space=pltpu.HBM)
    return pl.pallas_call(
        functools.partial(post_kernel, groups, entries, len(sources)),
        in_specs=[smem()] + [vmem()] * (3 + groups) + [hbm] * len(sources),
        out_specs=[vmem()] * 3,
        out_shape=[
            jax.ShapeDtypeStruct((rows, width), f32),
            jax.ShapeDtypeStruct((rows, width), bf16),
            jax.ShapeDtypeStruct((slots, rows, LANES), bf16),
        ],
        scratch_shapes=[
            pltpu.VMEM((width, width), bf16),
            pltpu.SemaphoreType.DMA((len(entries),)),
        ],
        compiler_params=params(),
        cost_estimate=cost(2 * rows * width * width, 4 * width * width),
        name="post_stage",
    )(w_rows, middle, *backs, c, gain, *sources)


def out_kernel(halves, w_rows, att_ref, branch_ref, *refs):
    og, sems = refs[halves:]
    og[...] = mm_tn(att_ref[...], branch_ref[...]).astype(bf16)
    stores = store_rows(og, refs[:halves], sems, w_rows, slice(None))
    for copy in stores:
        copy.start()
    for copy in stores:
        copy.wait()


def out_terms(w_rows, att, branch, halves):
    rows, width = att.shape
    pieces = w_rows.shape[0]
    hbm = pl.BlockSpec(memory_space=pltpu.HBM)
    shape = jax.ShapeDtypeStruct((pieces // halves, width // pieces, width), bf16)
    return pl.pallas_call(
        functools.partial(out_kernel, halves),
        in_specs=[smem(), vmem(), vmem()],
        out_specs=[hbm] * halves,
        out_shape=[shape] * halves,
        scratch_shapes=[pltpu.VMEM((width, width), bf16), pltpu.SemaphoreType.DMA((pieces,))],
        compiler_params=params(),
        cost_estimate=cost(2 * rows * width * width, 4 * width * width),
        name="out_terms",
    )(w_rows, att, branch)


def last_kernel(parts, pieces, *refs):
    w_rows, dq_ref = refs[:2]
    kv_refs = refs[2 : 2 + parts]
    x_ref, dmid_ref, gain_ref = refs[2 + parts : 5 + parts]
    weight_refs = refs[5 + parts : 5 + parts + pieces]
    out_ref, grad, total = refs[5 + parts + pieces :]
    rows, width = x_ref.shape
    blocks = dq_ref.shape[0]
    block_width = width // blocks
    piece_width = width // pieces
    done = 0
    for part in range(parts):
        part_rows = kv_refs[part].shape[2]
        for block in range(blocks):
            lanes = slice(block * block_width, (block + 1) * block_width)
            for kind in range(2):
                grad[kind + 1, done : done + part_rows, lanes] = kv_refs[part][block, kind][
                    :, :block_width
                ]
        done += part_rows
    for block in range(blocks):
        lanes = slice(block * block_width, (block + 1) * block_width)
        grad[0, :, lanes] = dq_ref[block][:, :block_width]
    for piece in range(pieces):
        at = pl.ds(pl.multiple_of(w_rows[piece] * piece_width, piece_width), piece_width)
        w = weight_refs[piece]
        total[:, at] = (
            mm_nt(grad[0], w[:, :width])
            + mm_nt(grad[1], w[:, width : 2 * width])
            + mm_nt(grad[2], w[:, 2 * width :])
        )
    x = x_ref[...].astype(f32)
    scaling = lax.rsqrt(jnp.mean(x * x, axis=-1, keepdims=True) + EPSILON)
    incoming = total[...] * gain_ref[...].astype(f32)
    centre = jnp.mean(incoming * x, axis=-1, keepdims=True)
    out_ref[...] = dmid_ref[...] + scaling * incoming - x * (scaling * scaling * scaling * centre)


def last_stage(w_rows, dq, kvs, x, d_middle, gain, weights):
    rows, width = x.shape
    return pl.pallas_call(
        functools.partial(last_kernel, len(kvs), len(weights)),
        in_specs=[smem()] + [vmem()] * (4 + len(kvs) + len(weights)),
        out_specs=vmem(),
        out_shape=jax.ShapeDtypeStruct((rows, width), f32),
        scratch_shapes=[pltpu.VMEM((3, rows, width), bf16), pltpu.VMEM((rows, width), f32)],
        compiler_params=params(),
        cost_estimate=cost(6 * rows * width * width, 6 * width * width),
        name="last_stage",
    )(w_rows, dq, *kvs, x, d_middle, gain, *weights)


def finish_kernel(mine_ref, own_ref, other_ref, w_ref, gain_ref, *outs):
    width = outs[0].shape[1]
    mine = mine_ref[0]
    for source, bit in ((own_ref, mine), (other_ref, 1 - mine)):
        for index in range(4):
            slot = (index % 2) * 4 + bit * 2 + index // 2
            at = pl.ds(pl.multiple_of(slot * LANES, LANES), LANES)
            for kind in range(3):
                outs[kind][:, at] = source[index, :, kind * LANES : (kind + 1) * LANES].astype(f32)
    total = None
    for kind in range(3):
        weight = w_ref[:, kind * width : (kind + 1) * width].astype(f32)
        part = jnp.sum(outs[kind][...] * weight, axis=-1, keepdims=True)
        total = part if total is None else total + part
    outs[3][...] = total / gain_ref[...].astype(f32)


def finish_own(mine, own, other, weights, gain):
    rows, width = own.shape[1], weights.shape[1] // 3
    return pl.pallas_call(
        finish_kernel,
        in_specs=[smem()] + [vmem()] * 4,
        out_specs=[vmem()] * 4,
        out_shape=[jax.ShapeDtypeStruct((rows, width), f32)] * 3
        + [jax.ShapeDtypeStruct((rows, 1), f32)],
        compiler_params=params(),
        cost_estimate=cost(6 * rows * width, 20 * rows * width),
        name="finish_own",
    )(mine, own, other, weights, gain)


def flip(values, axis, delta):
    count = lax.axis_size(axis)
    return lax.ppermute(values, axis, [(i, i ^ delta) for i in range(count)])


def after(values, *others):
    return lax.optimization_barrier((values, *others))[0]


def bits_of(count):
    return [1 << i for i in range(count.bit_length() - 1)]


def add_low(a, b):
    return (a.astype(f32) + b.astype(f32)).astype(bf16)


def cut(values, start, size):
    return lax.dynamic_slice_in_dim(values, start, size, axis=-2)


class Line:
    def __init__(self):
        self.last = None

    def hold(self, values):
        if self.last is not None:
            values = after(values, self.last)
        self.last = values
        return values


class Reduction:
    def __init__(self, kept, given, line):
        self.own, self.given, self.line, self.joined = kept, given, line, None

    def core(self):
        self.arrived = flip(self.line.hold(self.given), "fsdp", 1)

    def hold(self, *others):
        self.arrived = lax.optimization_barrier((self.arrived, *others))[0]

    def across(self):
        given = self.line.hold(add_low(self.own[1], self.arrived[1]))
        self.own = add_low(self.own[0], self.arrived[0])
        self.arrived = flip(given, "fsdp", 2)

    def halve(self, bit):
        place = lax.axis_index("seq")
        half = self.own.shape[-2] // 2
        mine = (place // bit) % 2
        keep, give = mine * half, (1 - mine) * half
        given = add_low(cut(self.own, give, half), cut(self.arrived, give, half))
        kept = add_low(cut(self.own, keep, half), cut(self.arrived, keep, half))
        self.own, self.arrived = kept, flip(self.line.hold(given), "seq", bit)

    def settle(self):
        self.own = add_low(self.own, self.arrived)

    def swap_columns(self):
        self.settle()
        self.arrived = flip(self.line.hold(self.own[1]), "fsdp", 2)

    def join_columns(self):
        upper = (lax.axis_index("fsdp") // 2) == 1
        width = self.arrived.shape[-1] // 2
        parts = []
        for kind in range(2):
            here = self.own[0, :, kind * width : (kind + 1) * width]
            there = self.arrived[:, kind * width : (kind + 1) * width]
            parts += [jnp.where(upper, there, here), jnp.where(upper, here, there)]
        self.own = jnp.concatenate(parts, axis=-1)

    def widen(self, bit):
        self.join()
        self.own = self.line.hold(self.own)
        self.arrived, self.joined = flip(self.own, "seq", bit), bit

    def join(self):
        if self.joined is None:
            return
        upper = ((lax.axis_index("seq") // self.joined) % 2) == 1
        first = jnp.where(upper, self.arrived, self.own)
        second = jnp.where(upper, self.own, self.arrived)
        self.own, self.joined = jnp.concatenate([first, second], axis=0), None


def token_codes(lengths_row, order_row, real_row):
    total = order_row.shape[0]
    ends_at = jnp.cumsum(lengths_row)
    positions = jnp.arange(total, dtype=jnp.int32)
    packed_segment = jnp.sum((positions[:, None] >= ends_at[None, :]).astype(jnp.int32), axis=1)
    packed_code = packed_segment * 2 + (real_row > 0).astype(jnp.int32)
    return jnp.sum(
        jnp.where(positions[:, None] == order_row[None, :], packed_code[None, :], 0), axis=1
    ).reshape(total, 1)


def parts_of(total):
    return max(2, total // 1280)


def move_chain(array, pairs):
    return lax.ppermute(
        array, "seq", [(a * 2 + low, b * 2 + low) for a, b in pairs for low in range(2)]
    )


def turn(blocks):
    return lax.all_to_all(blocks, "seq", split_axis=0, concat_axis=0, tiled=True)


def on_device(
    tokens,
    cotangent,
    query_weight,
    key_weight,
    value_weight,
    output_weight,
    gate_weight,
    up_weight,
    down_weight,
    attention_gain,
    feedforward_gain,
    lengths,
    token_order,
    real_token,
):
    x, c = tokens[0], cotangent[0]
    rows, width = x.shape
    slots = lax.axis_size("seq")
    shards = lax.axis_size("fsdp")
    seq, shard = lax.axis_index("seq"), lax.axis_index("fsdp")
    direct = slots == 8 and shards == 4
    heads = width // slots // HD
    own_width = heads * HD
    shard_rows = width // shards
    halves = 2 if direct else 1

    own_columns = [
        lax.dynamic_slice_in_dim(w, seq * own_width, own_width, axis=1)
        for w in (query_weight, key_weight, value_weight)
    ]
    gains = jnp.stack([attention_gain, feedforward_gain], axis=1)
    own_columns = jnp.concatenate(
        [jnp.pad(w, ((0, 0), (0, LANES - own_width))) for w in own_columns]
        + [jnp.pad(gains, ((0, 0), (0, LANES - 2)))],
        axis=1,
    )
    qkv_weight = jnp.concatenate([query_weight, key_weight, value_weight], axis=1)

    if direct:
        w_rows = shard ^ jnp.arange(shards, dtype=jnp.int32)
        place = seq // 2
        half = shard_rows // 2
        hidden = gate_weight.shape[1] // 2
        columns_x = flip(own_columns, "fsdp", 2)
        beside = flip(x, "seq", 1)
        near = move_chain(x, [(0, 1), (1, 0), (2, 3), (3, 2)])
        inner = move_chain(x, [(1, 2), (2, 1)])
        output_x = flip(output_weight, "fsdp", 2)
        both = jnp.stack([own_columns, columns_x])
        both_c = flip(both, "fsdp", 1)
        column_arrays = [both, both_c]
        column_layout = ((0, 0), (1, 0), (0, 1), (1, 1))
        near, inner, _ = lax.optimization_barrier((near, inner, beside))
        far_inner = move_chain(near, [(1, 2), (2, 1)])
        far_outer = move_chain(inner, [(1, 0), (2, 3)])
        near_beside = flip(near, "seq", 1)
        far_half = (1 - shard // 2) * hidden
        near_half = (shard // 2) * hidden
        up_own, up_sent = [
            jnp.concatenate(
                [
                    lax.dynamic_slice_in_dim(after(w, own_columns), start, hidden, axis=1)
                    for w in (gate_weight, up_weight)
                ],
                axis=1,
            )
            for start in (near_half, far_half)
        ]
        up_x1 = flip(after(up_sent[:half], near), "fsdp", 2)
        token_order = after(token_order, near)
        is_inner = (place == 1) | (place == 2)
        block_slots = [seq ^ d for d in range(slots)]
    else:
        w_rows = jnp.zeros((1,), jnp.int32)
        column_arrays = [lax.all_gather(own_columns, "fsdp", axis=0, tiled=True)[None]]
        column_layout = ((0, 0),)
        gathered = lax.all_gather(x, "seq", axis=0)
        x_blocks = [gathered[i] for i in range(slots)]
        block_slots = [jnp.asarray(i, jnp.int32) for i in range(slots)]

    codes = token_codes(lengths[0], token_order[0], real_token[0])
    gain_pieces = jnp.stack(
        [column_arrays[a][i, :, 3 * LANES : 3 * LANES + 2] for a, i in column_layout]
    )
    gain_rows = jnp.take(gain_pieces, w_rows, axis=0).reshape(width, 2)
    gain_1, gain_2 = gain_rows[:, 0].reshape(1, width), gain_rows[:, 1].reshape(1, width)
    state = None

    def project_block(number, block, state):
        slot = block_slots[number].reshape(1).astype(jnp.int32)
        return project(
            slot,
            w_rows,
            slots,
            heads,
            lengths.shape[1],
            block,
            column_layout,
            column_arrays,
            codes,
            state,
        )

    if direct:
        state = project_block(0, x, state)
        state = project_block(1, beside, state)
        far_inner, far_outer, _, _, _, _ = lax.optimization_barrier(
            (far_inner, far_outer, near_beside, up_x1, output_x, state[0])
        )
        third = move_chain(far_inner, [(1, 0), (2, 3)])
        far = jnp.where(is_inner, far_inner, far_outer)
        far_beside = flip(far, "seq", 1)
        up_x2 = flip(after(up_sent[half:], far_inner), "fsdp", 2)
        up_c = flip(after(up_own, far_inner), "fsdp", 1)
        state = project_block(2, near, state)
        state = project_block(3, near_beside, state)
        state = project_block(4, far, state)
        third, _, _, _, _ = lax.optimization_barrier(
            (third, far_beside, up_x2, up_c, state[0])
        )
        cross = jnp.where(is_inner, inner, third)
        cross_beside = flip(cross, "seq", 1)
        c_x = flip(after(c, cross), "fsdp", 2)
        up_xc1 = flip(after(up_x1, cross), "fsdp", 1)
        down_c = flip(after(down_weight, cross), "fsdp", 1)
        state = project_block(5, far_beside, state)
        state = project_block(6, cross, state)
        cross_beside, _, _, _ = lax.optimization_barrier((cross_beside, c_x, up_xc1, down_c))
        state = project_block(7, cross_beside, state)
    else:
        for number, block in enumerate(x_blocks):
            state = project_block(number, block, state)
    qa, ka, va, h1, own_scores = state

    att, sums, qb, own_weights = attend(qa, ka, va, own_scores, parts_of(slots * rows), slots)
    if direct:
        qkv_x = flip(after(qkv_weight, qa), "fsdp", 2)
        up_xc2 = flip(after(up_x2, qa), "fsdp", 1)
        output_c = flip(after(output_weight, qa), "fsdp", 1)
        output_xc = flip(after(output_x, qa), "fsdp", 1)
        att = lax.optimization_barrier((att, up_xc2, output_c, output_xc))[0]
    if direct:
        output_pieces = [output_weight, output_c, output_x, output_xc]
        output_entries = [(0, p, 0, p, shard_rows, 0, 0) for p in range(4)]
        d_rows = (shard % 2) ^ jnp.arange(2, dtype=jnp.int32)
        ff_sources = [up_own, up_c, up_x1, up_x2, up_xc1, up_xc2, down_weight, down_c]
        ff_entries = [
            (kind, source, 0, place, shard_rows, offset, kind * hidden)
            for kind in range(2)
            for source, place, offset in (
                (0, 0, 0), (1, 1, 0), (2, 2, 0), (3, 2, half), (4, 3, 0), (5, 3, half),
            )
        ] + [(2, 6, 1, 0, down_weight.shape[0], 0, 0), (2, 7, 1, 1, down_weight.shape[0], 0, 0)]
    else:
        output_pieces = [lax.all_gather(output_weight, "fsdp", axis=0, tiled=True)]
        output_entries = [(0, 0, 0, 0, width, 0, 0)]
        d_rows = w_rows
        ff_sources = [
            lax.all_gather(w, "fsdp", axis=0, tiled=True)
            for w in (gate_weight, up_weight, down_weight)
        ]
        hidden = gate_weight.shape[1]
        ff_entries = [(i, i, 0, 0, width, 0, 0) for i in range(3)]
    att_parts = [turn(att.reshape(slots, rows, LANES))]
    if direct:
        x, _ = lax.optimization_barrier((x, qkv_x))
    total = rows * slots
    sums = sums.reshape(total, LANES)
    qb = qb.reshape(heads, total, LANES)

    middle, h2, att = pre_stage(w_rows, att_parts, x, gain_2, output_entries, output_pieces)
    if direct:
        h2s, cs = [h2, flip(h2, "fsdp", 2)], [c, c_x]
    else:
        h2s, cs = [h2], [c]
    outs, backs, gu, dg = main_stage(
        w_rows, d_rows, h2s, cs, hidden, ff_entries, ff_sources, halves
    )
    if direct:
        line = Line()
        backs[1] = flip(backs[1], "fsdp", 2)
        up_r = Reduction(*gu, line)
        down_r = Reduction(dg[0][0], dg[1][0], line)
        up_r.core()
        down_r.core()
        up_r.halve(1)
        down_r.halve(2)
        backs[1] = lax.optimization_barrier((backs[1], up_r.own, down_r.own))[0]
    d_middle, branch, d_att = post_stage(
        w_rows, middle, backs, c, gain_2, slots, output_entries, output_pieces
    )
    og = out_terms(w_rows, att, branch, halves)
    grad_blocks = turn(d_att)
    parts = 4
    back = functools.partial(attend_back, qb, ka, va, own_weights)
    if direct:
        qkv_c = flip(after(qkv_weight, d_att), "fsdp", 1)
        output_r = Reduction(*og, line)
        down_r.hold(d_att)
        down_r.halve(1)
        output_r.core()
        up_r.hold(d_att)
        up_r.halve(2)
        grad_blocks = lax.optimization_barrier(
            (grad_blocks, down_r.own, up_r.own, qkv_c)
        )[0]
    else:
        qkv_pieces = [lax.all_gather(qkv_weight, "fsdp", axis=0, tiled=True)]
    kv_0, dq, gb = back(0, parts, slots, sums, grad_blocks, None)
    if direct:
        for r in (down_r, up_r, output_r):
            r.hold(kv_0)
        down_r.halve(4)
        up_r.halve(4)
        output_r.across()
        outs[1] = flip(after(outs[1], kv_0), "fsdp", 2)
        qkv_xc = flip(after(qkv_x, kv_0), "fsdp", 1)
        qkv_pieces = [qkv_weight, qkv_c, qkv_x, qkv_xc]
        gb = lax.optimization_barrier((gb, down_r.own, up_r.own, output_r.own))[0]
    kv_1, dq = back(1, parts, slots, None, None, (gb, dq))
    kv_early = turn(jnp.concatenate([kv_0, kv_1], axis=2))
    if direct:
        for r in (down_r, up_r, output_r):
            r.hold(kv_1)
        up_r.swap_columns()
        down_r.settle()
        down_r.widen(4)
        output_r.halve(2)
        gb = lax.optimization_barrier((gb, down_r.own, up_r.own, output_r.own, qkv_xc, outs[1]))[0]
    kv_2, dq = back(2, parts, slots, None, None, (gb, dq))
    if direct:
        for r in (down_r, up_r, output_r):
            r.hold(kv_2)
        up_r.join_columns()
        up_r.widen(4)
        down_r.widen(1)
        output_r.halve(1)
        gb = lax.optimization_barrier((gb, down_r.own, up_r.own, output_r.own))[0]
    kv_3, dq = back(3, parts, slots, None, None, (gb, dq))
    kv_late = jnp.concatenate([kv_2, kv_3], axis=2)
    late = turn(jnp.concatenate([kv_late.reshape(slots, rows, LANES), dq], axis=1))
    kv_late = late[:, :rows].reshape(kv_late.shape)
    dq_turned = late[:, rows:]
    if direct:
        for r in (down_r, up_r, output_r):
            r.hold(kv_3)
        up_r.widen(2)
        down_r.widen(2)
        dq = lax.optimization_barrier((dq, down_r.own, up_r.own, kv_early))[0]
    layer_out = (middle + sum(part.astype(f32) for part in outs)).astype(bf16)
    own = own_terms(w_rows, h1, dq, [kv_0, kv_1, kv_2, kv_3], shards, halves)
    if direct:
        own_r = Reduction(*own, line)
        own_r.core()
        for r in (up_r, output_r):
            r.hold(own[0])
        up_r.widen(1)
        output_r.halve(4)
        own_r.across()
        output_r.settle()
        output_r.widen(4)
        output_r.widen(1)
        own_r.settle()
        own_r.own = after(own_r.own[None], down_r.arrived)
        own_r.widen(4)
        output_r.widen(2)
        own_r.widen(1)
        own_r.arrived = after(own_r.arrived, late)
        own_r.widen(2)
        input_grad = last_stage(
            w_rows, dq_turned, [kv_early, kv_late], x, d_middle, gain_1, qkv_pieces
        )
        for r in (up_r, down_r, output_r):
            r.join()
        gate_grad, up_grad = up_r.own[:, : 2 * hidden], up_r.own[:, 2 * hidden :]
        down_grad, output_grad = down_r.own, output_r.own
        query_grad, key_grad, value_grad, attention_gain_grad = finish_own(
            ((seq // 2) % 2).reshape(1).astype(jnp.int32),
            own_r.own,
            own_r.arrived,
            qkv_weight,
            attention_gain.reshape(shard_rows, 1),
        )
        attention_gain_grad = attention_gain_grad.reshape(shard_rows)
    else:
        own_share = lax.psum_scatter(own[0][0], "fsdp", scatter_dimension=0, tiled=True)
        all_shares = lax.all_gather(own_share, "seq", axis=0)
        gate_grad, up_grad, down_grad, output_grad = [
            lax.psum(lax.psum_scatter(g, "fsdp", scatter_dimension=0, tiled=True), "seq")
            for g in (gu[0][0, :, :hidden], gu[0][0, :, hidden:], dg[0][0], og[0][0])
        ]
    def gain_grad(terms, gain):
        summed = sum(jnp.sum(g * w.astype(f32), axis=1) for g, w in terms)
        return summed / gain.astype(f32)

    if not direct:
        all_shares = all_shares.reshape(slots, shard_rows, 3, LANES)[..., :own_width].astype(f32)
        query_grad, key_grad, value_grad = [
            all_shares[:, :, i, :].transpose(1, 0, 2).reshape(shard_rows, width) for i in range(3)
        ]
        input_grad = last_stage(
            w_rows, dq_turned, [kv_early, kv_late], x, d_middle, gain_1, qkv_pieces
        )
        attention_gain_grad = gain_grad(
            ((query_grad, query_weight), (key_grad, key_weight), (value_grad, value_weight)),
            attention_gain,
        )
    output_grad, gate_grad, up_grad, down_grad = [
        g.astype(f32) for g in (output_grad, gate_grad, up_grad, down_grad)
    ]
    feedforward_gain_grad = gain_grad(
        ((gate_grad, gate_weight), (up_grad, up_weight)), feedforward_gain
    )
    return (
        layer_out[None],
        input_grad[None],
        query_grad,
        key_grad,
        value_grad,
        output_grad,
        gate_grad,
        up_grad,
        down_grad,
        attention_gain_grad,
        feedforward_gain_grad,
    )


def solution(mesh):
    in_specs = (
        P("fsdp", "seq", None),
        P("fsdp", "seq", None),
        P("fsdp", None),
        P("fsdp", None),
        P("fsdp", None),
        P("fsdp", None),
        P("fsdp", None),
        P("fsdp", None),
        P("fsdp", None),
        P("fsdp"),
        P("fsdp"),
        P("fsdp", None),
        P("fsdp", None),
        P("fsdp", None),
    )
    out_specs = (
        P("fsdp", "seq", None),
        P("fsdp", "seq", None),
        P("fsdp", None),
        P("fsdp", None),
        P("fsdp", None),
        P("fsdp", None),
        P("fsdp", None),
        P("fsdp", None),
        P("fsdp", None),
        P("fsdp"),
        P("fsdp"),
    )
    return jax.shard_map(
        on_device, mesh=mesh, in_specs=in_specs, out_specs=out_specs, check_vma=False
    )
```
